32 devices in a mesh: dp: 8 (over y, x, core), tensor: 4 (over z).
Axes of the slice: x: 2, y: 2, z: 4, core: 2. Of those that a mesh axis runs over, the one named last changes fastest.
Arguments:
- tokens: bfloat16 [16384, 768], P('dp'), may hold values from -6 to 6
- cotangent: bfloat16 [16384, 768], P('dp'), may hold values from -6 to 6
- segment: int32 [32, 512], P('dp'), may hold values from 0 to 15, never falling along the last dimension, each value on 1 to 256 neighbouring positions
- box_x: int32 [32, 512], P('dp'), may hold values from 0 to 127
- box_y: int32 [32, 512], P('dp'), may hold values from 0 to 127
- page_tokens: int32 [32], P('dp'), may hold values from 128 to 512, as said below
- gain_attn: float32 [768], replicated, may hold values from 0.5 to 1.5
- shift_attn: float32 [768], replicated, may hold values from -3 to 3
- w_query: bfloat16 [768, 768], P(None, 'tensor'), may hold values from -0.21875 to 0.21875
- b_query: float32 [12, 64], P('tensor'), may hold values from -4 to 4
- w_key: bfloat16 [768, 768], P(None, 'tensor'), may hold values from -0.21875 to 0.21875
- w_value: bfloat16 [768, 768], P(None, 'tensor'), may hold values from -0.21875 to 0.21875
- b_value: float32 [12, 64], P('tensor'), may hold values from -4 to 4
- table_x: float32 [12, 64], P('tensor'), may hold values from -4 to 4
- table_y: float32 [12, 64], P('tensor'), may hold values from -4 to 4
- w_attn_out: bfloat16 [768, 768], P('tensor'), may hold values from -0.875 to 0.875
- b_attn_out: float32 [768], replicated, may hold values from -4 to 4
- gain_mlp: float32 [768], replicated, may hold values from 0.5 to 1.5
- shift_mlp: float32 [768], replicated, may hold values from -3 to 3
- w_in: bfloat16 [768, 3072], P(None, 'tensor'), may hold values from -0.21875 to 0.21875
- b_in: float32 [24, 128], P('tensor'), may hold values from -4 to 4
- w_out: bfloat16 [3072, 768], P('tensor'), may hold values from -0.109375 to 0.109375
- b_out: float32 [768], replicated, may hold values from -4 to 4
Outputs:
- layer_out: bfloat16 [16384, 768], P('dp')
- input_grad: bfloat16 [16384, 768], P('dp')
- grad_gain_attn: float32 [768], P('dp')
- grad_shift_attn: float32 [768], P('dp')
- grad_w_query: float32 [768, 768], P('dp', 'tensor')
- grad_b_query: float32 [12, 64], P('tensor', 'dp')
- grad_w_key: float32 [768, 768], P('dp', 'tensor')
- grad_w_value: float32 [768, 768], P('dp', 'tensor')
- grad_b_value: float32 [12, 64], P('tensor', 'dp')
- grad_table_x: float32 [12, 64], P('tensor', 'dp')
- grad_table_y: float32 [12, 64], P('tensor', 'dp')
- grad_w_attn_out: float32 [768, 768], P('tensor', 'dp')
- grad_b_attn_out: float32 [768], P('dp')
- grad_gain_mlp: float32 [768], P('dp')
- grad_shift_mlp: float32 [768], P('dp')
- grad_w_in: float32 [768, 3072], P('dp', 'tensor')
- grad_b_in: float32 [24, 128], P('tensor', 'dp')
- grad_w_out: float32 [3072, 768], P('tensor', 'dp')
- grad_b_out: float32 [768], P('dp')
The draws below stay inside these ranges and needn't reach their ends.
Inputs may be any that keep to these rules, and one draw needn't show every extreme that they name: `page_tokens`: some page of every draw holds 512 tokens. Within a page the segment numbers never fall.
All inputs are finite; a program needn't handle non-finite values.
Results may differ from the reference program's by a relative error of at most 0.023.
Values may be sent and summed in bfloat16 or wider, within the bound.
No kernel may reach another device: no remote copies, remote signals or barrier semaphores. Data moves between devices by JAX's collectives and lax.ppermute only.
A program may use at most 192 MiB of HBM per device.

```python
import math
import jax
import jax.numpy as jnp
import numpy as np
from jax import lax

D = 768
H = 12
HD = 64
FF = 3072
BINS = 64
BOXES = 128
PAGE = 512
SEGS = 16
PAGES = 32
TOKENS = 16384
N_TENSOR = 4


def draw_page_tokens(key, part):
    first, second = jax.random.split(jax.random.fold_in(key, 11))
    counts = jax.random.randint(first, (PAGES,), PAGE // 4, PAGE + 1)
    full_page = jax.random.randint(second, (), 0, PAGES)
    return jnp.where(jnp.arange(PAGES) == full_page, PAGE, counts).astype(jnp.int32)


def with_ends(entries, stream_key, low, largest):
    shape = entries.shape
    spot = [jax.random.randint(jax.random.fold_in(stream_key, axis), (), 0, shape[axis]) for axis in range(len(shape))]
    entries = entries.at[tuple(spot)].set(low)
    longest = shape.index(max(shape))
    spot[longest] = (spot[longest] + 1) % shape[longest]
    return entries.at[tuple(spot)].set(largest)


def with_spikes(array, rng, source, target, parts, factor):
    owner, partner = [(jnp.arange(array.shape[dim]) // (array.shape[dim] // parts)).reshape([-1 if axis == dim else 1 for axis in range(array.ndim)]) for dim in (source, target)]
    chosen = jax.random.permutation(rng, parts)[partner]
    strong = (owner == chosen) | (owner == (partner + parts // 2) % parts)
    return jnp.where(strong, factor * array, array)


def shard_levels(rng, extent, cuts, least, high):
    loudness, own = 1.0, jax.random.fold_in(rng, 6)
    for position, parts in cuts:
        heights = jnp.exp(jax.random.uniform(jax.random.fold_in(own, position), (parts,), jnp.float32, least / len(cuts), high / len(cuts)))
        loudness = loudness * jnp.repeat(heights, extent[position] // parts).reshape([-1 if axis == position else 1 for axis in range(len(extent))])
    return loudness


def split_up(number_of, total, most, slope):
    weights = [(1 << 20) // math.isqrt(standing ** slope) + 1 for standing in range(2, number_of + 1)]
    rest, given = total - most - (number_of - 1), [1] * (number_of - 1)
    while rest > 0:
        candidates = [i for i in range(number_of - 1) if given[i] < most]
        pool, remaining = sum([weights[i] for i in candidates]), rest
        for i in candidates:
            extra = min(most - given[i], max(1, remaining * weights[i] // pool), rest)
            given[i] = given[i] + extra
            rest = rest - extra
    return np.array([most] + given)


def uneven(own_key, number_of, total, bound, slope):
    if number_of == 2:
        one = jax.random.randint(own_key, (), max(1, total - bound), min(bound, total - 1) + 1)
        return jnp.stack([one, total - one])
    tallies = jnp.asarray(split_up(number_of, total, bound, slope), jnp.int32)
    twos = (number_of - 1) // 2
    source_of, receiver = tallies[1:1 + 2 * twos:2], tallies[2:2 + 2 * twos:2]
    margin = jnp.minimum(source_of - 1, bound - receiver)
    shifted = jax.random.randint(jax.random.fold_in(own_key, 1), (twos,), 0, 1 << 20) % (margin + 1)
    tallies = tallies.at[1:1 + 2 * twos:2].set(source_of - shifted).at[2:2 + 2 * twos:2].set(receiver + shifted)
    return tallies[jax.random.permutation(jax.random.fold_in(own_key, 2), number_of)]


def scatter_about(key, dims, width, limit, cuts=(), kind=jnp.bfloat16):
    drawn = jax.random.normal(key, dims, jnp.float32) * width
    if len(cuts) > 0:
        drawn = shard_levels(key, dims, cuts, -0.22, 0.18) * drawn
    return jnp.clip(drawn, min=-limit, max=limit).astype(kind)


def heavy_noise(rng, dims, width, most, cuts, heavy, kind=jnp.bfloat16):
    values = width * jax.random.normal(rng, dims, jnp.float32)
    if cuts:
        values = values * shard_levels(rng, dims, cuts, -0.22, 0.18)
    return jnp.clip(with_spikes(values, jax.random.fold_in(rng, 3), *heavy), -most, most).astype(kind)


def setup_inputs(seed: int = 0) -> dict:
    splits = jax.random.split(jax.random.key(seed), 24)
    return {
        "tokens": heavy_noise(splits[0], (TOKENS, D), 1.0, 6.0, ((0, 8),), (0, 1, 8, 2.0)),
        "cotangent": heavy_noise(splits[1], (TOKENS, D), 1.0, 6.0, ((0, 8),), (0, 1, 8, 2.0)),
        "segment": jax.vmap(lambda own: jnp.searchsorted(jnp.cumsum(uneven(own, SEGS, PAGE, PAGE // 2, 1)), jnp.arange(PAGE), side="right"))(jax.random.split(splits[2], PAGES)).reshape((PAGES, PAGE)).astype(jnp.int32),
        "box_x": with_ends(jax.random.randint(splits[3], (PAGES, PAGE), 0, BOXES), jax.random.fold_in(splits[3], 1), 0, BOXES - 1).astype(jnp.int32),
        "box_y": with_ends(jax.random.randint(splits[4], (PAGES, PAGE), 0, BOXES), jax.random.fold_in(splits[4], 1), 0, BOXES - 1).astype(jnp.int32),
        "page_tokens": draw_page_tokens(jax.random.fold_in(splits[23], 71), 0),
        "gain_attn": jnp.clip(1.0 + 0.1 * jax.random.normal(splits[6], (D,), jnp.float32), 0.5, 1.5),
        "shift_attn": scatter_about(splits[7], (D,), 0.3, 3.0, (), jnp.float32),
        "w_query": scatter_about(splits[8], (D, D), D ** -0.5, 0.21875, ((1, 4),)),
        "b_query": scatter_about(splits[9], (H, HD), 0.5, 4.0, ((0, 4),), jnp.float32),
        "w_key": scatter_about(splits[10], (D, D), D ** -0.5, 0.21875, ((1, 4),)),
        "w_value": scatter_about(splits[11], (D, D), D ** -0.5, 0.21875, ((1, 4),)),
        "b_value": scatter_about(splits[12], (H, HD), 0.5, 4.0, ((0, 4),), jnp.float32),
        "table_x": scatter_about(splits[13], (H, BINS), 0.7, 4.0, ((0, 4),), jnp.float32),
        "table_y": scatter_about(splits[14], (H, BINS), 0.7, 4.0, ((0, 4),), jnp.float32),
        "w_attn_out": scatter_about(splits[15], (D, D), (D // 16) ** -0.5, 0.875, ((0, 4),)),
        "b_attn_out": scatter_about(splits[16], (D,), 0.5, 4.0, (), jnp.float32),
        "gain_mlp": jnp.clip(1.0 + 0.1 * jax.random.normal(splits[17], (D,), jnp.float32), 0.5, 1.5),
        "shift_mlp": scatter_about(splits[18], (D,), 0.3, 3.0, (), jnp.float32),
        "w_in": scatter_about(splits[19], (D, FF), D ** -0.5, 0.21875, ((1, 4),)),
        "b_in": scatter_about(splits[20], (FF // 128, 128), 0.5, 4.0, ((0, 4),), jnp.float32),
        "w_out": scatter_about(splits[21], (FF, D), FF ** -0.5, 0.109375, ((0, 4),)),
        "b_out": scatter_about(splits[22], (D,), 0.5, 4.0, (), jnp.float32),
    }


EPS = 1e-05
MASKED = -1e+30
HIGH = lax.Precision.HIGHEST

@jax.custom_vjp
def low(v):
    return lax.optimization_barrier(v.astype(jnp.bfloat16)).astype(jnp.float32)

@jax.custom_vjp
def low_back(v):
    return v

def low_keep(v):
    return (low(v), None)

def low_pass(kept, grad):
    return (grad,)

def back_keep(v):
    return (v, None)

def back_low(kept, grad):
    return (low(grad),)
low.defvjp(low_keep, low_pass)
low_back.defvjp(back_keep, back_low)

def both_ways(value):
    return low(low_back(value))

def layer_norm(rows, gain, shift):
    mean = lax.optimization_barrier(jnp.mean(rows, axis=-1, keepdims=True))
    centred = rows - mean
    inverse = lax.rsqrt(lax.optimization_barrier(jnp.mean(centred * centred, axis=-1, keepdims=True)) + EPS)
    return centred * inverse * gain + shift

def attend(query, key_rows, value, page_seg, page_bx, page_by, length, table_x, table_y):
    count = page_seg.shape[0]
    place = jnp.arange(count, dtype=jnp.int32)
    valid = place < length
    allowed = valid[None, :] & ((page_seg[:, None] == page_seg[None, :]) | ~valid[:, None])
    half = BINS // 2
    rel_x = jnp.clip(page_bx[None, :] - page_bx[:, None], -half, half - 1) + half
    rel_y = jnp.clip(page_by[None, :] - page_by[:, None], -half, half - 1) + half
    bias = table_x[:, rel_x] + table_y[:, rel_y]
    scores = jnp.einsum('ihd,jhd->hij', query, key_rows, precision=HIGH) * HD ** (-0.5) + bias
    scores = low_back(scores)
    scores = jnp.where(allowed[None], scores, MASKED)
    probs = jax.nn.softmax(scores, axis=-1)
    return jnp.einsum('hij,jhd->ihd', low(probs), value, precision=HIGH)

def forward(params, rows, page_seg, page_bx, page_by, lengths):
    gain_attn, shift_attn, w_query, b_query, w_key, w_value, b_value, table_x, table_y, w_attn_out, b_attn_out, gain_mlp, shift_mlp, w_in, b_in, w_out, b_out = params
    count = rows.shape[0]
    normed = low(layer_norm(rows, gain_attn, shift_attn))
    query = both_ways(jnp.dot(normed, w_query, precision=HIGH) + b_query.reshape(-1))
    key_rows = both_ways(jnp.dot(normed, w_key, precision=HIGH))
    value = both_ways(jnp.dot(normed, w_value, precision=HIGH) + b_value.reshape(-1))
    shaped = (page_seg.shape[0], page_seg.shape[1], H, HD)
    context = jax.vmap(attend, in_axes=(0, 0, 0, 0, 0, 0, 0, None, None))(query.reshape(shaped), key_rows.reshape(shaped), value.reshape(shaped), page_seg, page_bx, page_by, lengths, table_x, table_y)
    context = both_ways(context.reshape(count, D))
    cols = D // N_TENSOR
    attn = low(jnp.dot(context[:, :cols], w_attn_out[:cols], precision=HIGH))
    for group in range(1, N_TENSOR):
        attn = attn + low(jnp.dot(context[:, group * cols:(group + 1) * cols], w_attn_out[group * cols:(group + 1) * cols], precision=HIGH))
    attn = low_back(attn + b_attn_out)
    resid = rows + attn
    normed_mlp = low(layer_norm(resid, gain_mlp, shift_mlp))
    before = low_back(jnp.dot(normed_mlp, w_in, precision=HIGH) + b_in.reshape(-1))
    active = low(jax.nn.gelu(before, approximate=False))
    hidden = FF // N_TENSOR
    mlp = low(jnp.dot(active[:, :hidden], w_out[:hidden], precision=HIGH))
    for group in range(1, N_TENSOR):
        mlp = mlp + low(jnp.dot(active[:, group * hidden:(group + 1) * hidden], w_out[group * hidden:(group + 1) * hidden], precision=HIGH))
    mlp = low_back(mlp + b_out)
    return resid + mlp

def reference(tokens, cotangent, segment, box_x, box_y, page_tokens, gain_attn, shift_attn, w_query, b_query, w_key, w_value, b_value, table_x, table_y, w_attn_out, b_attn_out, gain_mlp, shift_mlp, w_in, b_in, w_out, b_out):
    params = tuple((item.astype(jnp.float32) for item in (gain_attn, shift_attn, w_query, b_query, w_key, w_value, b_value, table_x, table_y, w_attn_out, b_attn_out, gain_mlp, shift_mlp, w_in, b_in, w_out, b_out)))
    group = math.gcd(PAGES, max(1, 4096 // PAGE))
    turns = PAGES // group
    rows = tokens.astype(jnp.float32).reshape(turns, group * PAGE, D)
    grads_top = cotangent.astype(jnp.float32).reshape(turns, group * PAGE, D)
    segs = segment.reshape(turns, group, PAGE)
    boxes_x = box_x.reshape(turns, group, PAGE)
    boxes_y = box_y.reshape(turns, group, PAGE)
    lengths = page_tokens.reshape(turns, group)

    def step(total, pieces):
        rows_g, grad_g, seg_g, bx_g, by_g, len_g = pieces

        def run(weights, inputs):
            return forward(weights, inputs, seg_g, bx_g, by_g, len_g)
        result, back = jax.vjp(run, params, rows_g)
        grad_weights, grad_inputs = back(grad_g)
        total = jax.tree.map(jnp.add, total, grad_weights)
        return (total, (result.astype(jnp.bfloat16), grad_inputs.astype(jnp.bfloat16)))
    start = jax.tree.map(jnp.zeros_like, params)
    total, (outputs, grad_inputs) = lax.scan(step, start, (rows, grads_top, segs, boxes_x, boxes_y, lengths))
    g_gain_attn, g_shift_attn, g_w_query, g_b_query, g_w_key, g_w_value, g_b_value, g_table_x, g_table_y, g_w_attn_out, g_b_attn_out, g_gain_mlp, g_shift_mlp, g_w_in, g_b_in, g_w_out, g_b_out = total
    return (outputs.reshape(TOKENS, D), grad_inputs.reshape(TOKENS, D), g_gain_attn, g_shift_attn, g_w_query, g_b_query, g_w_key, g_w_value, g_b_value, g_table_x, g_table_y, g_w_attn_out, g_b_attn_out, g_gain_mlp, g_shift_mlp, g_w_in, g_b_in, g_w_out, g_b_out)
```

```python
import jax
import jax.numpy as jnp
from jax import lax
from jax.experimental import pallas as pl
from jax.experimental.pallas import tpu as pltpu
from jax.sharding import PartitionSpec as P

LEVELS = 128
BINS = 64
SEGS = 16
GROUP = 8
EPS = 1e-05
BARRED = -1e30
F32 = jnp.float32
BF16 = jnp.bfloat16
VMEM_BYTES = 56 * 1024 * 1024

NN = (((1,), (0,)), ((), ()))
NT = (((1,), (1,)), ((), ()))
TN = (((0,), (0,)), ((), ()))


def mm(left, right, dims=NN):
    return lax.dot_general(left, right, dims, preferred_element_type=F32)


def norm_stats(rows):
    mean = jnp.mean(rows, axis=-1, keepdims=True)
    centred = rows - mean
    inverse = lax.rsqrt(jnp.mean(centred * centred, axis=-1, keepdims=True) + EPS)
    return centred * inverse, inverse


def norm_back(grad_out, unit, inverse, gain):
    scaled = grad_out * gain
    return inverse * (
        scaled
        - jnp.mean(scaled, axis=-1, keepdims=True)
        - unit * jnp.mean(scaled * unit, axis=-1, keepdims=True)
    )


def page_columns(seg_row, bx_row, by_row):
    count = seg_row.shape[1]
    rows = jnp.concatenate(
        [seg_row.astype(F32), bx_row.astype(F32), by_row.astype(F32), jnp.zeros((5, count), F32)],
        axis=0,
    )
    columns = jnp.transpose(rows).astype(jnp.int32)
    return columns[:, 0:1], columns[:, 1:2], columns[:, 2:3]


def segment_terms(seg_col, length):
    count = seg_col.shape[0]
    lane = lax.broadcasted_iota(jnp.int32, (count, 64), 1)
    place = lax.broadcasted_iota(jnp.int32, (count, 64), 0)
    valid = place < length
    same = seg_col == lane
    query_side = jnp.where(valid, jnp.where(same, 1.0, 0.0), jnp.where(lane == SEGS, 1.0, 0.0))
    key_side = jnp.where(
        valid,
        jnp.where(same | (lane >= SEGS), 0.0, BARRED),
        jnp.where(lane <= SEGS, BARRED, 0.0),
    )
    return query_side.astype(BF16), key_side.astype(BF16)


def level_onehot(column):
    count = column.shape[0]
    lane = lax.broadcasted_iota(jnp.int32, (count, LEVELS), 1)
    return jnp.where(column == lane, 1.0, 0.0).astype(BF16)


def level_onehot_t(row):
    count = row.shape[1]
    level = lax.broadcasted_iota(jnp.int32, (LEVELS, count), 0)
    return jnp.where(row == level, 1.0, 0.0).astype(BF16)


def lookup_pair(offsets_row):
    wide = jnp.broadcast_to(offsets_row, (LEVELS, 2 * LEVELS))
    table = pltpu.roll(wide, 0, 1, stride=1, stride_axis=0)[:, LEVELS:]
    high = table.astype(BF16)
    rest = (table - high.astype(F32)).astype(BF16)
    return jnp.concatenate([high, rest], axis=1)


def attn_forward_kernel(
    lengths, tokens, seg, bx, by, gain, shift, weights, bias, offsets, context, looks, q_side, k_side
):
    step = pl.program_id(0)
    heads = looks.shape[0]
    size = weights.shape[1] // 3 // heads
    inner = heads * size

    @pl.when(step == 0)
    def _():
        for h in range(heads):
            looks[h, 0] = lookup_pair(offsets[h, 0:1, :])
            looks[h, 1] = lookup_pair(offsets[h, 1:2, :])

    unit, _ = norm_stats(tokens[0].astype(F32))
    normed = (unit * gain[...] + shift[...]).astype(BF16)
    qkv = (mm(normed, weights[...]) + bias[...]).astype(BF16)
    seg_col, bx_col, by_col = page_columns(seg[0], bx[0], by[0])
    seg_q, seg_k = segment_terms(seg_col, lengths[step])
    hot_x = level_onehot(bx_col)
    hot_y = level_onehot(by_col)
    k_side[:, 128:256] = hot_x
    k_side[:, 256:384] = hot_x
    k_side[:, 384:512] = hot_y
    k_side[:, 512:640] = hot_y
    factor = jnp.asarray(size ** (-0.5), BF16)
    ones = jnp.ones((qkv.shape[0], size), BF16)
    results = []
    for h in range(heads):
        query = qkv[:, h * size : (h + 1) * size] * factor
        key = qkv[:, inner + h * size : inner + (h + 1) * size]
        value = qkv[:, 2 * inner + h * size : 2 * inner + (h + 1) * size]
        q_side[:, 0:128] = jnp.concatenate([query, seg_q], axis=1)
        k_side[:, 0:128] = jnp.concatenate([key, seg_k], axis=1)
        q_side[:, 128:384] = mm(hot_x, looks[h, 0]).astype(BF16)
        q_side[:, 384:640] = mm(hot_y, looks[h, 1]).astype(BF16)
        scores = mm(q_side[...], k_side[...], NT)
        peak = jnp.max(scores, axis=1, keepdims=True)
        raised = jnp.exp(scores - peak).astype(BF16)
        both = mm(raised, jnp.concatenate([value, ones], axis=1))
        results.append(both[:, :size] / both[:, size : size + 1])
    context[0] = jnp.concatenate(results, axis=1).astype(BF16)


def attn_forward(lengths, tokens, seg, bx, by, gain, shift, weights, bias, offsets):
    pages, count, width = tokens.shape
    heads = offsets.shape[0]
    inner = weights.shape[1] // 3
    row = pl.BlockSpec((1, 1, count), lambda p, n: (p, 0, 0))
    whole = lambda shape: pl.BlockSpec(shape, lambda p, n: (0,) * len(shape))
    return pl.pallas_call(
        attn_forward_kernel,
        out_shape=jax.ShapeDtypeStruct((pages, count, inner), BF16),
        grid_spec=pltpu.PrefetchScalarGridSpec(
            num_scalar_prefetch=1,
            grid=(pages,),
            in_specs=[
                pl.BlockSpec((1, count, width), lambda p, n: (p, 0, 0)),
                row,
                row,
                row,
                whole((1, width)),
                whole((1, width)),
                whole((width, 3 * inner)),
                whole((1, 3 * inner)),
                whole((heads, 8, 2 * LEVELS)),
            ],
            out_specs=pl.BlockSpec((1, count, inner), lambda p, n: (p, 0, 0)),
            scratch_shapes=[
                pltpu.VMEM((heads, 2, LEVELS, 2 * LEVELS), BF16),
                pltpu.VMEM((count, 640), BF16),
                pltpu.VMEM((count, 640), BF16),
            ],
        ),
        compiler_params=pltpu.CompilerParams(vmem_limit_bytes=VMEM_BYTES),
        name="attn_forward",
    )(lengths, tokens, seg, bx, by, gain, shift, weights, bias, offsets)


def mlp_kernel(
    tokens,
    cotangent,
    context,
    w_attn,
    b_attn,
    gain,
    shift,
    w_in,
    b_in,
    w_out,
    b_out,
    layer_out,
    grad_resid,
    grads,
    rows_out,
    grad_b_in,
    resid,
    low,
    low_t,
    cot_t,
    out_sum,
    back_sum,
):
    step = pl.program_id(0)
    count, width = resid.shape
    hidden = w_in.shape[3]

    @pl.when(step == 0)
    def _():
        total = b_attn[...]
        for t in range(context.shape[0]):
            piece = w_attn[:, t].reshape(width, context.shape[2])
            total = total + mm(context[t], piece, NT)
        resid[...] = tokens[...].astype(F32) + total
        unit, _ = norm_stats(resid[...])
        normed = (unit * gain[...] + shift[...]).astype(BF16)
        low[...] = normed
        low_t[...] = jnp.transpose(normed)
        cot_t[...] = jnp.transpose(cotangent[...])
        out_sum[...] = jnp.zeros_like(out_sum)
        back_sum[...] = jnp.zeros_like(back_sum)

    w_up = w_in[:, 0].reshape(width, hidden)
    w_down = w_out[:, 0].reshape(hidden, width)
    before = mm(low[...], w_up) + b_in[0]
    half = 0.5 * (1.0 + lax.erf(before * (0.5**0.5)))
    active = (before * half).astype(BF16)
    slope = half + before * (jnp.exp(-0.5 * before * before) * 0.3989422804014327)
    out_sum[...] += mm(active, w_down)
    grad_before = (mm(cotangent[...], w_down, NT) * slope).astype(BF16)
    back_sum[...] += mm(grad_before, w_up, NT)
    grads[:, 0, 0] = mm(low_t[...], grad_before).astype(BF16).reshape(grads.shape[0], -1, hidden)
    grads[:, 0, 1] = mm(cot_t[...], active).astype(BF16).reshape(grads.shape[0], -1, hidden)
    grad_b_in[0] = jnp.sum(grad_before.astype(F32), axis=0, keepdims=True)

    @pl.when(step == pl.num_programs(0) - 1)
    def _():
        top = cotangent[...].astype(F32)
        layer_out[...] = (resid[...] + (out_sum[...] + b_out[...])).astype(BF16)
        unit, inverse = norm_stats(resid[...])
        back = back_sum[...]
        grad = top + norm_back(back, unit, inverse, gain[...])
        grad_resid[...] = grad
        rows_out[...] = jnp.concatenate(
            [
                jnp.sum(back * unit, axis=0, keepdims=True),
                jnp.sum(back, axis=0, keepdims=True),
                jnp.sum(grad.astype(BF16).astype(F32), axis=0, keepdims=True),
                jnp.sum(top, axis=0, keepdims=True),
                jnp.zeros((4, width), F32),
            ],
            axis=0,
        )


def mlp(tokens, cotangent, context, w_attn, b_attn, gain, shift, w_in, b_in, w_out, b_out):
    count, width = tokens.shape
    parts, groups, piece, hidden = w_in.shape
    whole = lambda shape: pl.BlockSpec(shape, lambda g: (0,) * len(shape))
    chunk = pl.BlockSpec((parts, 1, piece, hidden), lambda g: (0, g, 0, 0))
    return pl.pallas_call(
        mlp_kernel,
        out_shape=(
            jax.ShapeDtypeStruct((count, width), BF16),
            jax.ShapeDtypeStruct((count, width), F32),
            jax.ShapeDtypeStruct((GROUP, groups, 2, width // GROUP, hidden), BF16),
            jax.ShapeDtypeStruct((8, width), F32),
            jax.ShapeDtypeStruct((groups, 1, hidden), F32),
        ),
        grid_spec=pltpu.PrefetchScalarGridSpec(
            num_scalar_prefetch=0,
            grid=(groups,),
            in_specs=[
                whole(tokens.shape),
                whole(cotangent.shape),
                whole(context.shape),
                whole(w_attn.shape),
                whole((1, width)),
                whole((1, width)),
                whole((1, width)),
                chunk,
                pl.BlockSpec((1, 1, hidden), lambda g: (g, 0, 0)),
                chunk,
                whole((1, width)),
            ],
            out_specs=(
                whole((count, width)),
                whole((count, width)),
                pl.BlockSpec(
                    (GROUP, 1, 2, width // GROUP, hidden), lambda g: (0, g, 0, 0, 0)
                ),
                whole((8, width)),
                pl.BlockSpec((1, 1, hidden), lambda g: (g, 0, 0)),
            ),
            scratch_shapes=[
                pltpu.VMEM((count, width), F32),
                pltpu.VMEM((count, width), BF16),
                pltpu.VMEM((width, count), BF16),
                pltpu.VMEM((width, count), BF16),
                pltpu.VMEM((count, width), F32),
                pltpu.VMEM((count, width), F32),
            ],
        ),
        compiler_params=pltpu.CompilerParams(vmem_limit_bytes=VMEM_BYTES),
        name="mlp",
    )(tokens, cotangent, context, w_attn, b_attn, gain, shift, w_in, b_in, w_out, b_out)


def attn_backward_kernel(
    lengths,
    tokens,
    grad_resid,
    context,
    seg,
    bx,
    by,
    gain,
    shift,
    weights,
    bias,
    offsets,
    input_grad,
    grads,
    rows_out,
    bias_out,
    table_out,
    low,
    low_t,
    branch,
    branch_t,
    back_sum,
    hot,
    hot_t,
    q_side,
    k_side,
):
    step = pl.program_id(0)
    count, width = low.shape
    heads = offsets.shape[1]
    inner = context.shape[2]
    size = inner // heads

    @pl.when(step == 0)
    def _():
        unit, _ = norm_stats(tokens[...].astype(F32))
        normed = (unit * gain[...] + shift[...]).astype(BF16)
        low[...] = normed
        low_t[...] = jnp.transpose(normed)
        rounded = grad_resid[...].astype(BF16)
        branch[...] = rounded
        branch_t[...] = jnp.transpose(rounded)
        back_sum[...] = jnp.zeros_like(back_sum)
        seg_col, bx_col, by_col = page_columns(seg[...], bx[...], by[...])
        seg_q, seg_k = segment_terms(seg_col, lengths[0])
        hot_x = level_onehot(bx_col)
        hot_y = level_onehot(by_col)
        hot[:, 0:128] = level_onehot(LEVELS - 1 - bx_col)
        hot[:, 128:256] = level_onehot(LEVELS - 1 - by_col)
        hot_t[0:128, :] = level_onehot_t(bx[...])
        hot_t[128:256, :] = level_onehot_t(by[...])
        q_side[:, 0:128] = jnp.concatenate([seg_q, seg_q], axis=1)
        k_side[:, 0:128] = jnp.concatenate([seg_k, seg_k], axis=1)
        k_side[:, 128:256] = hot_x
        k_side[:, 256:384] = hot_x
        k_side[:, 384:512] = hot_y
        k_side[:, 512:640] = hot_y

    w_all = weights[:, 0].reshape(width, 4 * inner)
    w_qkv = w_all[:, : 3 * inner]
    qkv = (mm(low[...], w_qkv) + bias[0]).astype(BF16)
    grad_ctx = mm(branch[...], w_all[:, 3 * inner :]).astype(BF16)
    factor = jnp.asarray(size ** (-0.5), BF16)
    grad_q, grad_k, grad_v = [], [], []
    for h in range(heads):
        query = qkv[:, h * size : (h + 1) * size] * factor
        key = qkv[:, inner + h * size : inner + (h + 1) * size]
        value = qkv[:, 2 * inner + h * size : 2 * inner + (h + 1) * size]
        grad_here = grad_ctx[:, h * size : (h + 1) * size]
        q_side[:, 0:size] = query
        k_side[:, 0:size] = key
        q_side[:, 128:384] = mm(k_side[:, 128:256], lookup_pair(offsets[0, h, 0:1, :])).astype(BF16)
        q_side[:, 384:640] = mm(k_side[:, 384:512], lookup_pair(offsets[0, h, 1:2, :])).astype(BF16)
        scores = mm(k_side[...], q_side[...], NT)
        raised = jnp.exp(scores - jnp.max(scores, axis=0, keepdims=True))
        probs = raised * (1.0 / jnp.sum(raised, axis=0, keepdims=True))
        grad_v.append(mm(probs.astype(BF16), grad_here))
        weighted = probs * mm(value, grad_here, NT)
        grad_scores = weighted - probs * jnp.sum(weighted, axis=0, keepdims=True)
        low_scores = grad_scores.astype(BF16)
        grad_k.append(mm(low_scores, query))
        grad_q.append(jnp.transpose(mm(key, low_scores, TN)) * (size ** (-0.5)))
        spread = mm(low_scores, hot[...]).astype(BF16)
        for axis in range(2):
            lanes = slice(axis * LEVELS, (axis + 1) * LEVELS)
            square = mm(hot_t[lanes, :], spread[:, lanes])
            wide = jnp.concatenate([square, jnp.zeros_like(square)], axis=1)
            turned = pltpu.roll(wide, 0, 1, stride=1, stride_axis=0)
            table_out[0, h, axis : axis + 1, :] = jnp.sum(turned, axis=0, keepdims=True)
    grad_q = jnp.concatenate(grad_q, axis=1).astype(BF16)
    grad_k = jnp.concatenate(grad_k, axis=1).astype(BF16)
    grad_v = jnp.concatenate(grad_v, axis=1).astype(BF16)
    bias_out[0] = jnp.concatenate(
        [
            jnp.sum(grad_q.astype(F32), axis=0, keepdims=True),
            jnp.sum(grad_v.astype(F32), axis=0, keepdims=True),
            jnp.zeros((6, inner), F32),
        ],
        axis=0,
    )
    grad_qkv = jnp.concatenate([grad_q, grad_k, grad_v], axis=1)
    back_sum[...] += mm(grad_qkv, w_qkv, NT)
    grads[:, 0] = (
        jnp.concatenate(
            [mm(low_t[...], grad_qkv), mm(branch_t[...], context[0])], axis=1
        )
        .astype(BF16)
        .reshape(grads.shape[0], -1, 4 * inner)
    )

    @pl.when(step == pl.num_programs(0) - 1)
    def _():
        back = back_sum[...]
        unit, inverse = norm_stats(tokens[...].astype(F32))
        input_grad[...] = (grad_resid[...] + norm_back(back, unit, inverse, gain[...])).astype(BF16)
        rows_out[...] = jnp.concatenate(
            [
                jnp.sum(back * unit, axis=0, keepdims=True),
                jnp.sum(back, axis=0, keepdims=True),
                jnp.zeros((6, width), F32),
            ],
            axis=0,
        )


def attn_backward(
    length, tokens, grad_resid, context, seg, bx, by, gain, shift, weights, bias, offsets
):
    count, width = tokens.shape
    groups, _, inner = context.shape
    heads = offsets.shape[1]
    parts, _, piece, _ = weights.shape
    whole = lambda shape: pl.BlockSpec(shape, lambda g, n: (0,) * len(shape))
    return pl.pallas_call(
        attn_backward_kernel,
        out_shape=(
            jax.ShapeDtypeStruct((count, width), BF16),
            jax.ShapeDtypeStruct((GROUP, groups, width // GROUP, 4 * inner), BF16),
            jax.ShapeDtypeStruct((8, width), F32),
            jax.ShapeDtypeStruct((groups, 8, inner), F32),
            jax.ShapeDtypeStruct((groups, heads, 8, 2 * LEVELS), F32),
        ),
        grid_spec=pltpu.PrefetchScalarGridSpec(
            num_scalar_prefetch=1,
            grid=(groups,),
            in_specs=[
                whole((count, width)),
                whole((count, width)),
                pl.BlockSpec((1, count, inner), lambda g, n: (g, 0, 0)),
                whole((1, count)),
                whole((1, count)),
                whole((1, count)),
                whole((1, width)),
                whole((1, width)),
                pl.BlockSpec((parts, 1, piece, 4 * inner), lambda g, n: (0, g, 0, 0)),
                pl.BlockSpec((1, 1, 3 * inner), lambda g, n: (g, 0, 0)),
                pl.BlockSpec((1, heads, 8, 2 * LEVELS), lambda g, n: (g, 0, 0, 0)),
            ],
            out_specs=(
                whole((count, width)),
                pl.BlockSpec((GROUP, 1, width // GROUP, 4 * inner), lambda g, n: (0, g, 0, 0)),
                whole((8, width)),
                pl.BlockSpec((1, 8, inner), lambda g, n: (g, 0, 0)),
                pl.BlockSpec((1, heads, 8, 2 * LEVELS), lambda g, n: (g, 0, 0, 0)),
            ),
            scratch_shapes=[
                pltpu.VMEM((count, width), BF16),
                pltpu.VMEM((width, count), BF16),
                pltpu.VMEM((count, width), BF16),
                pltpu.VMEM((width, count), BF16),
                pltpu.VMEM((count, width), F32),
                pltpu.VMEM((count, 256), BF16),
                pltpu.VMEM((256, count), BF16),
                pltpu.VMEM((count, 640), BF16),
                pltpu.VMEM((count, 640), BF16),
            ],
        ),
        compiler_params=pltpu.CompilerParams(vmem_limit_bytes=VMEM_BYTES),
        name="attn_backward",
    )(length, tokens, grad_resid, context, seg, bx, by, gain, shift, weights, bias, offsets)


def offset_rows(table_x, table_y):
    half = BINS // 2
    first = LEVELS - half

    def spread(table):
        heads = table.shape[0]
        return jnp.concatenate(
            [
                jnp.broadcast_to(table[:, :1], (heads, first)),
                table,
                jnp.broadcast_to(table[:, -1:], (heads, 2 * LEVELS - first - BINS)),
            ],
            axis=1,
        )

    both = jnp.stack([spread(table_x), spread(table_y)], axis=1)
    return jnp.pad(both, ((0, 0), (0, 6), (0, 0)))


def fold_offsets(sums):
    half = BINS // 2
    start = LEVELS - 1 - half
    middle = sums[..., start + 1 : start + BINS - 1]
    low = jnp.sum(sums[..., : start + 1], axis=-1, keepdims=True)
    high = jnp.sum(sums[..., start + BINS - 1 :], axis=-1, keepdims=True)
    return jnp.concatenate([low, middle, high], axis=-1)


def local(
    tokens,
    cotangent,
    segment,
    box_x,
    box_y,
    page_tokens,
    gain_attn,
    shift_attn,
    w_query,
    b_query,
    w_key,
    w_value,
    b_value,
    table_x,
    table_y,
    w_attn_out,
    b_attn_out,
    gain_mlp,
    shift_mlp,
    w_in,
    b_in,
    w_out,
    b_out,
):
    pages, count = segment.shape
    width = tokens.shape[1]
    heads, size = b_query.shape
    inner = heads * size
    hidden = w_in.shape[1]
    n_dp = lax.axis_size("dp")
    n_tensor = lax.axis_size("tensor")
    dp_at = lax.axis_index("dp")
    page_at = lax.axis_index("tensor")

    w_attn = jnp.concatenate([w_query, w_key, w_value, w_attn_out.T], axis=1)
    qkv_bias = jnp.concatenate(
        [b_query.reshape(1, -1), jnp.zeros((1, inner), F32), b_value.reshape(1, -1)], axis=1
    )
    offsets = offset_rows(table_x, table_y)

    def gather(weight):
        piece = weight.shape[0] // n_dp
        own = lax.dynamic_slice_in_dim(weight, dp_at * piece, piece, 0)
        column = lax.all_gather(own, "tensor", axis=0)
        parts = lax.all_gather(column, "dp", axis=0)
        if n_dp != GROUP:
            parts = parts.reshape(GROUP, n_dp // GROUP, n_tensor, piece, -1)
            parts = jnp.swapaxes(parts, 1, 2).reshape(
                GROUP, n_tensor, weight.shape[0] // GROUP, -1
            )
        return parts

    full_attn = gather(w_attn)
    full_in = gather(w_in)
    full_out = gather(w_out)
    small = jnp.concatenate(
        [qkv_bias.reshape(-1), b_in.reshape(-1), offsets.reshape(-1)]
    )
    small = lax.all_gather(small, "tensor", axis=0)
    full_bias = small[:, : 3 * inner].reshape(n_tensor, 1, 3 * inner)
    full_b_in = small[:, 3 * inner : 3 * inner + hidden].reshape(n_tensor, 1, hidden)
    full_offsets = small[:, 3 * inner + hidden :].reshape((n_tensor,) + offsets.shape)

    row = lambda v: v.reshape(1, -1)
    context = attn_forward(
        page_tokens,
        tokens.reshape(pages, count, width),
        segment.reshape(pages, 1, count),
        box_x.reshape(pages, 1, count),
        box_y.reshape(pages, 1, count),
        row(gain_attn),
        row(shift_attn),
        w_attn[:, : 3 * inner],
        qkv_bias,
        offsets,
    )
    context = lax.all_to_all(context, "tensor", 0, 0, tiled=True)
    mine = lambda array, rows: lax.dynamic_slice_in_dim(array, page_at * rows, rows, 0)
    own_tokens = mine(tokens, count)
    layer_part, grad_resid, grads_mlp, rows_mlp, grad_b_in = mlp(
        own_tokens,
        mine(cotangent, count),
        context,
        full_attn[:, :, :, 3 * inner :],
        row(b_attn_out),
        row(gain_mlp),
        row(shift_mlp),
        full_in,
        full_b_in,
        full_out,
        row(b_out),
    )
    input_part, grads_attn, rows_attn, grad_bias, grad_tables = attn_backward(
        mine(page_tokens, 1),
        own_tokens,
        grad_resid,
        context,
        mine(segment, 1),
        mine(box_x, 1),
        mine(box_y, 1),
        row(gain_attn),
        row(shift_attn),
        full_attn,
        full_bias,
        full_offsets,
    )
    layer_out = lax.all_gather(layer_part, "tensor", axis=0, tiled=True)
    input_grad = lax.all_gather(input_part, "tensor", axis=0, tiled=True)

    def scatter(array):
        if n_dp != GROUP:
            rest = array.shape[1:-2]
            more = n_dp // GROUP
            array = array.reshape((GROUP,) + rest + (more, -1, array.shape[-1]))
            array = jnp.moveaxis(array, -3, 1).reshape((n_dp,) + rest + (-1, array.shape[-1]))
        array = lax.psum_scatter(array, "dp", scatter_dimension=0, tiled=False)
        return lax.psum_scatter(array, "tensor", scatter_dimension=0, tiled=False)

    sum_mlp = scatter(grads_mlp).astype(F32)
    sum_attn = scatter(grads_attn).astype(F32)
    vectors = jnp.concatenate([rows_attn[:2], rows_mlp[:4]], axis=0)
    vectors = jnp.swapaxes(vectors.reshape(6, n_dp, -1), 0, 1)
    vectors = jnp.broadcast_to(vectors[:, None], (n_dp, n_tensor) + vectors.shape[1:])
    tables = fold_offsets(grad_tables[:, :, :2, :])

    def by_dp(array):
        array = array.reshape(n_tensor, -1, n_dp, array.shape[-1] // n_dp)
        return jnp.moveaxis(array, 2, 0)

    pieces = [
        vectors.reshape(n_dp, n_tensor, -1),
        by_dp(grad_bias[:, 0].reshape(n_tensor, heads, size)).reshape(n_dp, n_tensor, -1),
        by_dp(grad_bias[:, 1].reshape(n_tensor, heads, size)).reshape(n_dp, n_tensor, -1),
        by_dp(tables[:, :, 0]).reshape(n_dp, n_tensor, -1),
        by_dp(tables[:, :, 1]).reshape(n_dp, n_tensor, -1),
        by_dp(grad_b_in.reshape((n_tensor,) + b_in.shape)).reshape(n_dp, n_tensor, -1),
    ]
    packed = jnp.concatenate(pieces, axis=2)
    packed = lax.psum_scatter(packed, "dp", scatter_dimension=0, tiled=False)
    packed = lax.psum_scatter(packed, "tensor", scatter_dimension=0, tiled=False)
    sizes = [p.shape[2] for p in pieces]
    starts = [sum(sizes[:i]) for i in range(len(sizes))]
    cut = [packed[s : s + n] for s, n in zip(starts, sizes)]
    sum_vectors = cut[0].reshape(6, -1)
    head_shape = (heads, -1)
    return (
        layer_out,
        input_grad,
        sum_vectors[0],
        sum_vectors[1],
        sum_attn[:, :inner],
        cut[1].reshape(head_shape),
        sum_attn[:, inner : 2 * inner],
        sum_attn[:, 2 * inner : 3 * inner],
        cut[2].reshape(head_shape),
        cut[3].reshape(head_shape),
        cut[4].reshape(head_shape),
        sum_attn[:, 3 * inner :].T,
        sum_vectors[4],
        sum_vectors[2],
        sum_vectors[3],
        sum_mlp[0],
        cut[5].reshape(b_in.shape[0], -1),
        sum_mlp[1].T,
        sum_vectors[5],
    )


def solution(mesh):
    split = P("tensor", None)
    return jax.shard_map(
        local,
        mesh=mesh,
        in_specs=(
            P("dp", None),
            P("dp", None),
            P("dp", None),
            P("dp", None),
            P("dp", None),
            P("dp"),
            P(),
            P(),
            P(None, "tensor"),
            split,
            P(None, "tensor"),
            P(None, "tensor"),
            split,
            split,
            split,
            split,
            P(),
            P(),
            P(),
            P(None, "tensor"),
            split,
            split,
            P(),
        ),
        out_specs=(
            P("dp", None),
            P("dp", None),
            P("dp"),
            P("dp"),
            P("dp", "tensor"),
            P("tensor", "dp"),
            P("dp", "tensor"),
            P("dp", "tensor"),
            P("tensor", "dp"),
            P("tensor", "dp"),
            P("tensor", "dp"),
            P("tensor", "dp"),
            P("dp"),
            P("dp"),
            P("dp"),
            P("dp", "tensor"),
            P("tensor", "dp"),
            P("tensor", "dp"),
            P("dp"),
        ),
        check_vma=False,
    )
```

```python
import jax
import jax.numpy as jnp
from jax import lax
from jax.experimental import pallas as pl
from jax.experimental.pallas import tpu as pltpu
from jax.sharding import PartitionSpec as P

LEVELS = 128
BINS = 64
SEGS = 16
GROUP = 8
EPS = 1e-05
BARRED = -1e30
F32 = jnp.float32
BF16 = jnp.bfloat16
VMEM_BYTES = 56 * 1024 * 1024

NN = (((1,), (0,)), ((), ()))
NT = (((1,), (1,)), ((), ()))
TN = (((0,), (0,)), ((), ()))


def mm(left, right, dims=NN):
    return lax.dot_general(left, right, dims, preferred_element_type=F32)


def norm_stats(rows):
    mean = jnp.mean(rows, axis=-1, keepdims=True)
    centred = rows - mean
    inverse = lax.rsqrt(jnp.mean(centred * centred, axis=-1, keepdims=True) + EPS)
    return centred * inverse, inverse


def norm_back(grad_out, unit, inverse, gain):
    scaled = grad_out * gain
    return inverse * (
        scaled
        - jnp.mean(scaled, axis=-1, keepdims=True)
        - unit * jnp.mean(scaled * unit, axis=-1, keepdims=True)
    )


def page_columns(marks):
    return jnp.transpose(marks.astype(F32)).astype(jnp.int32)


def segment_terms(seg_col, length):
    count = seg_col.shape[0]
    lane = lax.broadcasted_iota(jnp.int32, (count, 64), 1)
    place = lax.broadcasted_iota(jnp.int32, (count, 64), 0)
    valid = place < length
    same = seg_col == lane
    query_side = jnp.where(valid, jnp.where(same, 1.0, 0.0), jnp.where(lane == SEGS, 1.0, 0.0))
    key_side = jnp.where(
        valid,
        jnp.where(same | (lane >= SEGS), 0.0, BARRED),
        jnp.where(lane <= SEGS, BARRED, 0.0),
    )
    return query_side.astype(BF16), key_side.astype(BF16)


def level_onehot(column):
    count = column.shape[0]
    lane = lax.broadcasted_iota(jnp.int32, (count, LEVELS), 1)
    return jnp.where(column == lane, 1.0, 0.0).astype(BF16)


def level_onehot_t(row):
    count = row.shape[1]
    level = lax.broadcasted_iota(jnp.int32, (LEVELS, count), 0)
    return jnp.where(row == level, 1.0, 0.0).astype(BF16)


def lookup_pair(table_row):
    lane = lax.broadcasted_iota(jnp.int32, (8, 2 * LEVELS), 1)
    first = LEVELS - BINS // 2
    wide = jnp.concatenate([table_row, jnp.zeros((1, 2 * LEVELS - BINS), F32)], axis=1)
    wide = pltpu.roll(jnp.broadcast_to(wide, (8, 2 * LEVELS)), first, 1)
    wide = jnp.where(lane < first, table_row[:, 0:1], wide)
    wide = jnp.where(lane >= first + BINS, table_row[:, BINS - 1 : BINS], wide)
    wide = jnp.broadcast_to(wide[0:1, :], (LEVELS, 2 * LEVELS))
    table = pltpu.roll(wide, 0, 1, stride=1, stride_axis=0)[:, LEVELS:]
    high = table.astype(BF16)
    rest = (table - high.astype(F32)).astype(BF16)
    return jnp.concatenate([high, rest], axis=1)


def fold_row(sums):
    lane = lax.broadcasted_iota(jnp.int32, (1, 2 * LEVELS), 1)
    start = LEVELS - 1 - BINS // 2
    low = jnp.sum(jnp.where(lane <= start, sums, 0.0), axis=1, keepdims=True)
    high = jnp.sum(jnp.where(lane >= start + BINS - 1, sums, 0.0), axis=1, keepdims=True)
    turned = pltpu.roll(jnp.broadcast_to(sums, (8, 2 * LEVELS)), 2 * LEVELS - start, 1)
    middle = turned[0:1, :BINS]
    lane = lane[:, :BINS]
    return jnp.where(lane == 0, low, jnp.where(lane == BINS - 1, high, middle))


def whole(array):
    return pl.BlockSpec(array.shape, lambda *at: (0,) * len(array.shape))


def cost(flops, arrays, exps=0):
    return pl.CostEstimate(
        flops=int(flops) // 16,
        bytes_accessed=int(sum(a.size * a.dtype.itemsize for a in arrays)) // 16,
        transcendentals=int(exps) // 16,
    )


def small_parts(heads, size, hidden):
    inner = heads * size
    b_q = slice(0, inner)
    b_v = slice(inner, 2 * inner)
    b_in = slice(2 * inner, 2 * inner + hidden)
    at = 2 * inner + hidden
    tables = [
        [slice(at + (axis * heads + h) * BINS, at + (axis * heads + h + 1) * BINS) for axis in (0, 1)]
        for h in range(heads)
    ]
    return b_q, b_v, b_in, tables


def attn_forward_kernel(
    pick, lengths, tokens, marks, vectors, w_query, w_key, w_value, small, context, *scratch
):
    looks, q_side, k_side = scratch
    step = pl.program_id(0)
    heads = looks.shape[0]
    inner = w_query.shape[0]
    size = inner // heads
    b_q, b_v, _, tables = small_parts(heads, size, small.shape[1] - 2 * inner - 2 * heads * BINS)

    @pl.when(step == 0)
    def _():
        for h in range(heads):
            for axis in range(2):
                looks[h, axis] = lookup_pair(small[0:1, tables[h][axis]])

    unit, _ = norm_stats(tokens[0].astype(F32))
    normed = (unit * vectors[0:1, :] + vectors[1:2, :]).astype(BF16)
    queries = (mm(normed, w_query[...], NT) + small[0:1, b_q]).astype(BF16)
    keys = mm(normed, w_key[...], NT).astype(BF16)
    values = (mm(normed, w_value[...], NT) + small[0:1, b_v]).astype(BF16)
    columns = page_columns(marks[0])
    seg_q, seg_k = segment_terms(columns[:, 0:1], lengths[pick[step]])
    hot_x = level_onehot(columns[:, 1:2])
    hot_y = level_onehot(columns[:, 2:3])
    k_side[:, 128:256] = hot_x
    k_side[:, 256:384] = hot_x
    k_side[:, 384:512] = hot_y
    k_side[:, 512:640] = hot_y
    factor = jnp.asarray(size ** (-0.5), BF16)
    ones = jnp.ones((queries.shape[0], size), BF16)
    results = []
    for h in range(heads):
        lanes = slice(h * size, (h + 1) * size)
        q_side[:, 0:128] = jnp.concatenate([queries[:, lanes] * factor, seg_q], axis=1)
        k_side[:, 0:128] = jnp.concatenate([keys[:, lanes], seg_k], axis=1)
        q_side[:, 128:384] = mm(hot_x, looks[h, 0]).astype(BF16)
        q_side[:, 384:640] = mm(hot_y, looks[h, 1]).astype(BF16)
        scores = mm(q_side[...], k_side[...], NT)
        peak = jnp.max(scores, axis=1, keepdims=True)
        raised = jnp.exp(scores - peak).astype(BF16)
        both = mm(raised, jnp.concatenate([values[:, lanes], ones], axis=1))
        results.append(both[:, :size] / both[:, size : size + 1])
    context[0] = jnp.concatenate(results, axis=1).astype(BF16)


def attn_forward(heads, pages, lengths, tokens, marks, vectors, weights, small):
    _, count, width = tokens.shape
    n_pages = pages.shape[0]
    inner = weights[0].shape[0]
    flops = n_pages * (2 * count * width * 3 * inner + heads * 2 * count * count * 1400)
    return pl.pallas_call(
        attn_forward_kernel,
        out_shape=jax.ShapeDtypeStruct((n_pages, count, inner), BF16),
        grid_spec=pltpu.PrefetchScalarGridSpec(
            num_scalar_prefetch=2,
            grid=(n_pages,),
            in_specs=[
                pl.BlockSpec((1, count, width), lambda i, p, n: (p[i], 0, 0)),
                pl.BlockSpec((1,) + marks.shape[1:], lambda i, p, n: (p[i], 0, 0)),
                whole(vectors),
            ]
            + [whole(w) for w in weights]
            + [whole(small)],
            out_specs=pl.BlockSpec((1, count, inner), lambda i, p, n: (i, 0, 0)),
            scratch_shapes=[
                pltpu.VMEM((heads, 2, LEVELS, 2 * LEVELS), BF16),
                pltpu.VMEM((count, 640), BF16),
                pltpu.VMEM((count, 640), BF16),
            ],
        ),
        compiler_params=pltpu.CompilerParams(vmem_limit_bytes=VMEM_BYTES),
        cost_estimate=cost(flops, [tokens], n_pages * heads * count * count),
        name="attn_forward",
    )(pages, lengths, tokens, marks, vectors, *weights, small)


EARLY = (0, 4, 2, 6)
LATE = (0, 2, 4, 6)
TURNS = (0, 1, 3, 2)
GAIN_ATTN, SHIFT_ATTN, GAIN_MLP, SHIFT_MLP, B_ATTN, B_OUT, GROUP_ROWS = range(7)


def hand_out(panel, place, order, near, far, send):
    rows = panel.shape[0] // GROUP
    for slot in range(4):
        spot = place[1] ^ order[slot]
        held = (near, far)[slot // 2][slot % 2]
        held[...] = panel[pl.ds(pl.multiple_of(spot * rows, rows), rows), :]
        other = spot ^ 1
        send[slot][...] = panel[pl.ds(pl.multiple_of(other * rows, rows), rows), :]


def mlp_chunk(state, w_up, w_down, b_up, order, near, far, send):
    place, low, low_t, cotangent, cot_t, out_sum, back_sum, held = state
    before = mm(low[...], w_up) + b_up
    half = 0.5 * (1.0 + lax.erf(before * (0.5**0.5)))
    active = (before * half).astype(BF16)
    slope = half + before * (jnp.exp(-0.5 * before * before) * 0.3989422804014327)
    out_sum[...] += mm(active, w_down)
    grad_before = (mm(cotangent, w_down, NT) * slope).astype(BF16)
    back_sum[...] += mm(grad_before, w_up, NT)
    held[0] = mm(low_t[...], grad_before).astype(BF16)
    held[1] = mm(cot_t[...], active).astype(BF16)
    for side in range(2):
        hand_out(
            held.at[side],
            place,
            order,
            [near.at[s, side] for s in range(2)],
            [far.at[s, side] for s in range(2)],
            [send.at[s, side] for s in range(4)],
        )
    return jnp.sum(grad_before.astype(F32), axis=0, keepdims=True)


def mlp_kernel(place, tokens, cotangent, *rest):
    contexts = rest[:4]
    w_attn, w_in, w_out, vectors, small, panels, panels_all = rest[4:11]
    pieces = rest[11 : 11 + GROUP]
    near, far, send, packed, layer_out, grad_resid = rest[11 + GROUP : 17 + GROUP]
    resid, low, low_t, cot_t, out_sum, back_sum, held, others, extra, sems, late_sems = rest[
        17 + GROUP :
    ]
    step = pl.program_id(0)
    width, hidden = w_in.shape
    inner = w_attn.shape[0]
    rows = width // GROUP
    share = 2 * inner // GROUP
    top = cotangent[0]
    state = (place, low, low_t, top, cot_t, out_sum, back_sum, held)

    def chunk(w_up, w_down, order):
        row = mlp_chunk(
            state,
            w_up,
            w_down,
            small[0, 0:1, 2 * inner : 2 * inner + hidden],
            order,
            near.at[:, 0],
            far.at[:, 0],
            send.at[:, 0],
        )
        turn = jnp.where(step < 2, step, 5 - step)
        packed[pl.ds(GROUP_ROWS + 1 + 2 * (place[0] ^ turn), 1), :] = row

    late_copies = []
    for j in range(GROUP):
        spot = (place[2] ^ j) * rows
        for side in range(2):
            target = pl.multiple_of(side * width + spot, rows)
            late_copies.append(
                pltpu.make_async_copy(
                    pieces[j].at[pl.ds(side * rows, rows), :],
                    extra.at[pl.ds(target, rows), :],
                    late_sems.at[len(late_copies)],
                )
            )

    @pl.when(step == 0)
    def _():
        copies = []
        for g in range(3):
            for j in range(0, GROUP, 2):
                source = panels_all.at[j, g] if g < 2 else pieces[j]
                spot = j // 2 if g < 2 else (place[2] ^ j) // 2
                target = pl.multiple_of(g * inner + spot * share, share)
                copies.append(
                    pltpu.make_async_copy(
                        source.at[pl.ds(2 * rows, share), :],
                        others.at[pl.ds(target, share), :],
                        sems.at[len(copies)],
                    )
                )
        for copy in copies + late_copies:
            copy.start()
        packed[...] = jnp.zeros_like(packed)
        cot_t[...] = jnp.transpose(top)
        total = tokens[0].astype(F32) + vectors[2:3, :]
        total = total + mm(contexts[0][0], w_attn[...])
        for copy in copies:
            copy.wait()
        total = total + mm(jnp.concatenate([c[0] for c in contexts[1:]], axis=1), others[...])
        resid[...] = total
        unit, _ = norm_stats(total)
        normed = (unit * vectors[3:4, :] + vectors[4:5, :]).astype(BF16)
        low[...] = normed
        low_t[...] = jnp.transpose(normed)
        out_sum[...] = jnp.zeros_like(out_sum)
        back_sum[...] = jnp.zeros_like(back_sum)
        chunk(w_in[...], w_out[...], EARLY)

    @pl.when((step == 1) | (step == 2))
    def _():
        late = step >= 2
        chunk(
            panels[:, 0, :rows, :].reshape(width, hidden),
            panels[:, 0, rows : 2 * rows, :].reshape(hidden, width),
            (0, jnp.where(late, 2, 4), jnp.where(late, 4, 2), 6),
        )

    @pl.when(step == 3)
    def _():
        for copy in late_copies:
            copy.wait()
        chunk(extra[:width, :], extra[width:, :], LATE)

    @pl.when(step == pl.num_programs(0) - 1)
    def _():
        wide = top.astype(F32)
        layer_out[...] = (resid[...] + (out_sum[...] + vectors[5:6, :])).astype(BF16)
        unit, inverse = norm_stats(resid[...])
        back = back_sum[...]
        grad = wide + norm_back(back, unit, inverse, vectors[3:4, :])
        grad_resid[...] = grad
        column_sum = lambda v: jnp.sum(v, axis=0, keepdims=True)
        packed[GAIN_MLP : GAIN_MLP + 1, :] = column_sum(back * unit)
        packed[SHIFT_MLP : SHIFT_MLP + 1, :] = column_sum(back)
        packed[B_ATTN : B_ATTN + 1, :] = column_sum(grad.astype(BF16).astype(F32))
        packed[B_OUT : B_OUT + 1, :] = column_sum(wide)


def mlp(place, tokens, cotangent, contexts, w_attn, w_in, w_out, vectors, small, panels, pieces):
    _, count, width = tokens.shape
    hidden = w_in.shape[1]
    inner = w_attn.shape[0]
    groups = len(contexts)
    rows = width // GROUP
    page = pl.BlockSpec((1, count, width), lambda g, p: (p[0], 0, 0))
    outs = (
        jax.ShapeDtypeStruct((2, groups, 2, rows, hidden), BF16),
        jax.ShapeDtypeStruct((2, groups, 2, rows, hidden), BF16),
        jax.ShapeDtypeStruct((4, groups, 2, rows, hidden), BF16),
        jax.ShapeDtypeStruct((16, width), F32),
        jax.ShapeDtypeStruct((count, width), BF16),
        jax.ShapeDtypeStruct((count, width), F32),
    )
    held = lambda n: pl.BlockSpec((n, 1, 2, rows, hidden), lambda g, p: (0, g, 0, 0, 0))
    return pl.pallas_call(
        mlp_kernel,
        out_shape=outs,
        grid_spec=pltpu.PrefetchScalarGridSpec(
            num_scalar_prefetch=1,
            grid=(groups,),
            in_specs=[page, page]
            + [whole(c) for c in contexts]
            + [whole(w_attn), whole(w_in), whole(w_out), whole(vectors)]
            + [
                pl.BlockSpec((1,) + small.shape[1:], lambda g, p: (g, 0, 0)),
                pl.BlockSpec(
                    (GROUP, 1, 2 * rows, width),
                    lambda g, p: (0, jnp.minimum(jnp.maximum(g - 1, 0), 1), 0, 0),
                ),
                pl.BlockSpec(memory_space=pl.ANY),
            ]
            + [pl.BlockSpec(memory_space=pl.ANY)] * GROUP,
            out_specs=(held(2), held(2), held(4), whole(outs[3]), whole(outs[4]), whole(outs[5])),
            scratch_shapes=[
                pltpu.VMEM((count, width), F32),
                pltpu.VMEM((count, width), BF16),
                pltpu.VMEM((width, count), BF16),
                pltpu.VMEM((width, count), BF16),
                pltpu.VMEM((count, width), F32),
                pltpu.VMEM((count, width), F32),
                pltpu.VMEM((2, width, hidden), BF16),
                pltpu.VMEM((3 * inner, width), BF16),
                pltpu.VMEM((2 * width, hidden), BF16),
                pltpu.SemaphoreType.DMA((12,)),
                pltpu.SemaphoreType.DMA((2 * GROUP,)),
            ],
        ),
        compiler_params=pltpu.CompilerParams(vmem_limit_bytes=VMEM_BYTES),
        cost_estimate=cost(2 * count * width * (width + 24 * hidden), outs, 4 * count * hidden),
        name="mlp",
    )(
        place,
        tokens,
        cotangent,
        *contexts,
        w_attn,
        w_in,
        w_out,
        vectors,
        small,
        panels,
        panels,
        *pieces,
    )


def attn_backward_kernel(last, place, lengths, tokens, grad_resid, *rest):
    groups = 2
    context_refs = rest[:groups]
    marks, vectors, packed_start = rest[groups : groups + 3]
    at = groups + 3
    if last:
        back_start = rest[at]
        at += 1
    n_sources = GROUP + 1 if last else 5
    sources = rest[at : at + n_sources]
    at += n_sources
    small, result, near, far, send, packed = rest[at : at + 6]
    at += 6
    low, low_t, branch, branch_t, back_sum = rest[at : at + 5]
    hot, hot_t, q_side, k_side, both_weights, context, panel, sems = rest[at + 5 :]
    step = pl.program_id(0)
    count, width = low.shape
    inner = context.shape[1]
    heads = (small.shape[2] - width - 2 * inner) // (2 * BINS)
    size = inner // heads
    b_q, b_v, _, tables = small_parts(heads, size, width)
    rows = width // GROUP
    first_row = 2 * rows + 2 * inner // GROUP
    copies = [[], []]

    def fetch(slot, source, target, size):
        copies[slot].append(
            pltpu.make_async_copy(
                source, both_weights.at[slot, pl.ds(target, size), :], sems.at[slot, len(copies[slot])]
            )
        )

    for j in range(GROUP):
        spot = pl.multiple_of((place[2] ^ j) * rows, rows)
        cut = pl.ds(first_row, rows)
        if last:
            fetch(0, sources[0].at[j, 1, pl.ds(0, rows), :], j * rows, rows)
            fetch(1, sources[1 + j].at[cut, :], spot, rows)
        else:
            fetch(1, sources[4].at[j, 0, pl.ds(0, rows), :], j * rows, rows)
    if not last:
        for i in range(4):
            fetch(0, sources[i], i * inner, inner)

    @pl.when(step == 0)
    def _():
        for copy in copies[0] + copies[1]:
            copy.start()
        packed[...] = packed_start[...]
        unit, _ = norm_stats(tokens[0].astype(F32))
        normed = (unit * vectors[0:1, :] + vectors[1:2, :]).astype(BF16)
        low[...] = normed
        low_t[...] = jnp.transpose(normed)
        rounded = grad_resid[...].astype(BF16)
        branch[...] = rounded
        branch_t[...] = jnp.transpose(rounded)
        back_sum[...] = back_start[...] if last else jnp.zeros_like(back_sum)
        columns = page_columns(marks[0])
        seg_q, seg_k = segment_terms(columns[:, 0:1], lengths[place[0]])
        hot_x = level_onehot(columns[:, 1:2])
        hot_y = level_onehot(columns[:, 2:3])
        hot[:, 0:128] = level_onehot(LEVELS - 1 - columns[:, 1:2])
        hot[:, 128:256] = level_onehot(LEVELS - 1 - columns[:, 2:3])
        hot_t[0:128, :] = level_onehot_t(marks[0, 1:2, :])
        hot_t[128:256, :] = level_onehot_t(marks[0, 2:3, :])
        q_side[:, 0:128] = jnp.concatenate([seg_q, seg_q], axis=1)
        k_side[:, 0:128] = jnp.concatenate([seg_k, seg_k], axis=1)
        k_side[:, 128:256] = hot_x
        k_side[:, 256:384] = hot_x
        k_side[:, 384:512] = hot_y
        k_side[:, 512:640] = hot_y

    for g in range(groups):

        @pl.when(step == g)
        def _(g=g):
            context[...] = context_refs[g][0]
            for copy in copies[g]:
                copy.wait()

    weights = both_weights.at[step]
    w_qkv = weights[: 3 * inner, :]
    qkv = mm(low[...], w_qkv, NT)
    queries = (qkv[:, :inner] + small[0, 0:1, b_q]).astype(BF16)
    keys = qkv[:, inner : 2 * inner].astype(BF16)
    values = (qkv[:, 2 * inner :] + small[0, 0:1, b_v]).astype(BF16)
    grad_ctx = mm(branch[...], weights[3 * inner :, :], NT).astype(BF16)
    factor = jnp.asarray(size ** (-0.5), BF16)
    grad_q, grad_k, grad_v = [], [], []
    tables_out = [[], []]
    for h in range(heads):
        lanes = slice(h * size, (h + 1) * size)
        query = queries[:, lanes] * factor
        key = keys[:, lanes]
        grad_here = grad_ctx[:, lanes]
        q_side[:, 0:size] = query
        k_side[:, 0:size] = key
        q_side[:, 128:384] = mm(
            k_side[:, 128:256], lookup_pair(small[0, 0:1, tables[h][0]])
        ).astype(BF16)
        q_side[:, 384:640] = mm(
            k_side[:, 384:512], lookup_pair(small[0, 0:1, tables[h][1]])
        ).astype(BF16)
        scores = mm(k_side[...], q_side[...], NT)
        raised = jnp.exp(scores - jnp.max(scores, axis=0, keepdims=True))
        probs = raised * (1.0 / jnp.sum(raised, axis=0, keepdims=True))
        grad_v.append(mm(probs.astype(BF16), grad_here))
        weighted = probs * mm(values[:, lanes], grad_here, NT)
        grad_scores = weighted - probs * jnp.sum(weighted, axis=0, keepdims=True)
        low_scores = grad_scores.astype(BF16)
        grad_k.append(mm(low_scores, query))
        grad_q.append(jnp.transpose(mm(key, low_scores, TN)) * (size ** (-0.5)))
        spread = mm(low_scores, hot[...]).astype(BF16)
        for axis in range(2):
            cut = slice(axis * LEVELS, (axis + 1) * LEVELS)
            square = mm(hot_t[cut, :], spread[:, cut])
            wide = jnp.concatenate([square, jnp.zeros_like(square)], axis=1)
            turned = pltpu.roll(wide, 0, 1, stride=1, stride_axis=0)
            tables_out[axis].append(fold_row(jnp.sum(turned, axis=0, keepdims=True)))
    grad_q = jnp.concatenate(grad_q, axis=1).astype(BF16)
    grad_k = jnp.concatenate(grad_k, axis=1).astype(BF16)
    grad_v = jnp.concatenate(grad_v, axis=1).astype(BF16)
    bases = [TURNS[2 + g] if last else TURNS[g] for g in range(groups)]
    turn = jnp.where(step == 0, bases[0], bases[1])
    packed[pl.ds(GROUP_ROWS + 2 * (place[0] ^ turn), 1), :] = jnp.concatenate(
        [
            jnp.sum(grad_q.astype(F32), axis=0, keepdims=True),
            jnp.sum(grad_v.astype(F32), axis=0, keepdims=True),
        ]
        + tables_out[0]
        + tables_out[1],
        axis=1,
    )
    grad_qkv = jnp.concatenate([grad_q, grad_k, grad_v], axis=1)
    back_sum[...] += mm(grad_qkv, w_qkv)
    panel[...] = jnp.concatenate(
        [mm(low_t[...], grad_qkv), mm(branch_t[...], context[...])], axis=1
    ).astype(BF16)
    hand_out(
        panel,
        place,
        LATE if last else EARLY,
        [near.at[s, 0] for s in range(2)],
        [far.at[s, 0] for s in range(2)],
        [send.at[s, 0] for s in range(4)],
    )

    @pl.when(step == groups - 1)
    def _():
        back = back_sum[...]
        if last:
            unit, inverse = norm_stats(tokens[0].astype(F32))
            result[...] = (
                grad_resid[...] + norm_back(back, unit, inverse, vectors[0:1, :])
            ).astype(BF16)
            packed[GAIN_ATTN : GAIN_ATTN + 1, :] = jnp.sum(back * unit, axis=0, keepdims=True)
            packed[SHIFT_ATTN : SHIFT_ATTN + 1, :] = jnp.sum(back, axis=0, keepdims=True)
        else:
            result[...] = back


def attn_backward(
    last,
    heads,
    place,
    lengths,
    tokens,
    grad_resid,
    contexts,
    marks,
    vectors,
    packed,
    extra,
    sources,
    small,
):
    _, count, width = tokens.shape
    groups = len(contexts)
    inner = contexts[0].shape[2]
    rows = width // GROUP
    first = 2 if last else 0
    outs = (
        jax.ShapeDtypeStruct((count, width), BF16 if last else F32),
        jax.ShapeDtypeStruct((2, groups, rows, 4 * inner), BF16),
        jax.ShapeDtypeStruct((2, groups, rows, 4 * inner), BF16),
        jax.ShapeDtypeStruct((4, groups, rows, 4 * inner), BF16),
        jax.ShapeDtypeStruct(packed.shape, F32),
    )
    held = lambda n: pl.BlockSpec((n, 1, rows, 4 * inner), lambda g, p, q: (0, g, 0, 0))
    flops = groups * (6 * count * width * 4 * inner + heads * 2 * count * count * 2900)
    body = lambda *refs: attn_backward_kernel(last, *refs)
    return pl.pallas_call(
        body,
        out_shape=outs,
        grid_spec=pltpu.PrefetchScalarGridSpec(
            num_scalar_prefetch=2,
            grid=(groups,),
            in_specs=[
                pl.BlockSpec((1, count, width), lambda g, p, n: (p[0], 0, 0)),
                whole(grad_resid),
            ]
            + [whole(c) for c in contexts]
            + [
                pl.BlockSpec((1,) + marks.shape[1:], lambda g, p, n: (p[0], 0, 0)),
                whole(vectors),
                whole(packed),
            ]
            + [whole(e) for e in extra]
            + [pl.BlockSpec(memory_space=pl.ANY)] * len(sources)
            + [pl.BlockSpec((1,) + small.shape[1:], lambda g, p, n: (g + first, 0, 0))],
            out_specs=(whole(outs[0]), held(2), held(2), held(4), whole(outs[4])),
            scratch_shapes=[
                pltpu.VMEM((count, width), BF16),
                pltpu.VMEM((width, count), BF16),
                pltpu.VMEM((count, width), BF16),
                pltpu.VMEM((width, count), BF16),
                pltpu.VMEM((count, width), F32),
                pltpu.VMEM((count, 256), BF16),
                pltpu.VMEM((256, count), BF16),
                pltpu.VMEM((count, 640), BF16),
                pltpu.VMEM((count, 640), BF16),
                pltpu.VMEM((2, 4 * inner, width), BF16),
                pltpu.VMEM((count, inner), BF16),
                pltpu.VMEM((width, 4 * inner), BF16),
                pltpu.SemaphoreType.DMA((2, GROUP)),
            ],
        ),
        compiler_params=pltpu.CompilerParams(vmem_limit_bytes=VMEM_BYTES),
        cost_estimate=cost(flops, outs, groups * heads * count * count),
        name="attn_backward",
    )(
        place,
        lengths,
        tokens,
        grad_resid,
        *contexts,
        marks,
        vectors,
        packed,
        *extra,
        *sources,
        small,
    )


def move_kernel(source, target):
    target[...] = source[...]


def move(array):
    rows, width = array.shape
    spec = pl.BlockSpec((rows // 4, width), lambda i: (i, 0))
    return pl.pallas_call(
        move_kernel,
        out_shape=jax.ShapeDtypeStruct(array.shape, array.dtype),
        grid=(4,),
        in_specs=[spec],
        out_specs=spec,
        cost_estimate=cost(0, [array, array]),
        name="move",
    )(array)


def swap(array, axis, offset):
    size = lax.axis_size(axis)
    return lax.ppermute(array, axis, [(i, i ^ offset) for i in range(size)])


def add_low(left, right):
    return (left.astype(F32) + right.astype(F32)).astype(BF16)


def after(values, *first):
    flat, tree = jax.tree.flatten(values, is_leaf=lambda v: v is None)
    held = [i for i, v in enumerate(flat) if v is not None]
    tied = lax.optimization_barrier(tuple(flat[i] for i in held) + first)
    for i, v in zip(held, tied):
        flat[i] = v
    return jax.tree.unflatten(tree, flat)


def start_slices(own, turn):
    piece = [None] * GROUP
    piece[0] = own
    for step in turn:
        piece[step] = swap(own, "dp", step)
    return piece


def local(
    tokens,
    cotangent,
    segment,
    box_x,
    box_y,
    page_tokens,
    gain_attn,
    shift_attn,
    w_query,
    b_query,
    w_key,
    w_value,
    b_value,
    table_x,
    table_y,
    w_attn_out,
    b_attn_out,
    gain_mlp,
    shift_mlp,
    w_in,
    b_in,
    w_out,
    b_out,
):
    pages, count = segment.shape
    width = tokens.shape[1]
    heads, size = b_query.shape
    inner = heads * size
    hidden = w_in.shape[1]
    n_dp = lax.axis_size("dp")
    n_tensor = lax.axis_size("tensor")
    dp_at = lax.axis_index("dp")
    page_at = lax.axis_index("tensor")
    slice_at = dp_at % GROUP
    rows = width // GROUP
    natural = n_dp != GROUP
    place_out = 0 * slice_at if natural else slice_at
    place = jnp.stack([page_at, place_out, slice_at]).astype(jnp.int32)

    tokens3 = tokens.reshape(pages, count, width)
    cotangent3 = cotangent.reshape(pages, count, width)
    cut = lambda w, at, size: lax.dynamic_slice_in_dim(w, at * size, size, 0)
    share = 2 * inner // GROUP
    slice_mlp = [cut(w_in, slice_at, rows), cut(w_out, slice_at, rows)]
    slice_out = cut(w_attn_out, slice_at // 2, share)
    own = [w_query.T, w_key.T, w_value.T, w_attn_out]
    slice_mlp = jnp.concatenate(slice_mlp + [slice_out], axis=0)
    got = [swap(slice_mlp, "tensor", k) for k in TURNS[1:3]]

    small = jnp.concatenate([v.reshape(-1) for v in (b_query, b_value, b_in, table_x, table_y)])
    marks = jnp.stack([segment, box_x, box_y] + [jnp.zeros_like(segment)] * 5, axis=1)
    zero_row = jnp.zeros_like(gain_attn)
    vectors = jnp.stack(
        [gain_attn, shift_attn, b_attn_out, gain_mlp, shift_mlp, b_out, zero_row, zero_row]
    )
    order = jnp.stack([page_at ^ k for k in (1, 3, 2, 0)]).astype(jnp.int32)
    forward = lambda which: attn_forward(
        heads, which, page_tokens, tokens3, marks, vectors, own[:3], small.reshape(1, -1)
    )
    sent = forward(order[:2])
    terms, rest = [], small
    for _ in range(3):
        term = lax.reduce_precision(rest, 8, 7)
        terms.append(term.astype(BF16))
        rest = rest - term
    terms = jnp.stack(terms).reshape(-1, width)
    terms_rows = terms.shape[0]
    slice_attn = lax.select_n(slice_at // 2, *[cut(w, slice_at % 2, inner // 2) for w in own])
    slice_attn = jnp.concatenate([slice_attn, terms], axis=0)
    slice_all = jnp.concatenate([slice_mlp, slice_attn], axis=0)
    sent, turn, got, slice_attn, slice_all = after((sent, order[2:], got, slice_attn, slice_all))
    blocks = [list(range(b, b + GROUP)) for b in range(0, n_dp, GROUP)]
    groups = None if n_dp == GROUP else blocks
    gather = lambda a: lax.all_gather(a, "dp", axis=0, axis_index_groups=groups)
    panels = gather(jnp.stack(got))
    got_last = swap(slice_all, "tensor", TURNS[3])
    contexts = [swap(sent[g : g + 1], "tensor", TURNS[g + 1]) for g in (0, 1)]
    got = [swap(slice_attn, "tensor", k) for k in TURNS[1:3]]
    kept = forward(turn)
    contexts, kept, got_last = after((contexts, kept, got_last))

    contexts = [kept[1:2]] + contexts + [swap(kept[0:1], "tensor", TURNS[3])]
    piece = start_slices(got_last, (4, 2))
    piece, got = after((piece, got))
    piece[6] = swap(piece[4], "dp", 2)
    for j in (0, 4, 2):
        piece[j + 1] = swap(piece[j], "dp", 1)
    smalls = [small]
    for g in got + [got_last]:
        three = g[-terms_rows:].reshape(3, -1).astype(F32)
        smalls.append(three[0] + three[1] + three[2])
    smalls = jnp.stack(smalls).reshape(n_tensor, 1, -1)
    contexts, piece, smalls = after((contexts, piece, smalls))
    piece[7] = swap(piece[6], "dp", 1)
    got = jnp.stack(got)
    contexts, piece, smalls, panels, got = after((contexts, piece, smalls, panels, got))

    attn_panels = gather(got)
    near_a, far_a, send_a, packed, layer_part, grad_resid = mlp(
        place, tokens3, cotangent3, contexts, w_attn_out, w_in, w_out, vectors, smalls, panels, piece
    )
    near_a, far_a, send_a, packed, layer_part, grad_resid, attn_panels = after(
        (near_a, far_a, send_a, packed, layer_part, grad_resid, attn_panels)
    )
    layer_out = lax.all_gather(layer_part, "tensor", axis=0, tiled=True)

    def backward(last, packed_in, grad_in, extra):
        side = slice(2, 4) if last else slice(0, 2)
        return attn_backward(
            last,
            heads,
            place,
            page_tokens,
            tokens3,
            grad_in,
            contexts[side],
            marks,
            vectors,
            packed_in,
            extra,
            [attn_panels] + piece if last else own + [attn_panels],
            smalls,
        )

    if natural:
        back_part, near_c, far_c, send_c, packed = backward(False, packed, grad_resid, [])
        input_part, near_d, far_d, send_d, packed = backward(True, packed, grad_resid, [back_part])
        input_grad = lax.all_gather(input_part, "tensor", axis=0, tiled=True)
        more = n_dp // GROUP

        def scatter(near, far, given, early):
            both = jnp.stack([jnp.concatenate([near, far]), given], axis=1)
            both = both.reshape((2, 2) + both.shape[1:])
            if early:
                both = jnp.swapaxes(both, 0, 1)
            inside = both.shape[3:-2]
            both = both.reshape((GROUP,) + inside + (more, -1, both.shape[-1]))
            both = jnp.moveaxis(both, -3, 1).reshape((n_dp,) + inside + (-1, both.shape[-1]))
            total = lax.psum_scatter(both, "dp", scatter_dimension=0, tiled=False)
            return total.astype(F32)

        sum_a = scatter(near_a[:, :2], far_a[:, :2], send_a[:, :2], True)
        sum_b = scatter(near_a[:, 2:], far_a[:, 2:], send_a[:, 2:], False)
        sum_c = scatter(near_c, far_c, send_c, True)
        sum_d = scatter(near_d, far_d, send_d, False)
        packed = lax.psum(packed, ("dp", "tensor"))
    else:
        got_a = swap(send_a, "dp", 1)
        back_part, near_c, far_c, send_c, packed = backward(False, packed, grad_resid, [])
        got_a, back_part, near_c, far_c, send_c, packed, grad_resid, near_a, far_a = after(
            (got_a, back_part, near_c, far_c, send_c, packed, grad_resid, near_a, far_a)
        )
        near_a = [add_low(near_a[:, s], got_a[:2, s]) for s in (slice(0, 2), slice(2, 4))]
        far_a = [add_low(far_a[:, s], got_a[2:, s]) for s in (slice(0, 2), slice(2, 4))]
        near_a, far_a, back_part, packed = after((near_a, far_a, back_part, packed))
        got_a = swap(far_a[0], "dp", 2)
        got_b = swap(far_a[1], "dp", 4)
        got_c = swap(send_c, "dp", 1)
        input_part, near_d, far_d, send_d, packed = backward(True, packed, grad_resid, [back_part])
        values = (got_a, got_b, got_c, near_a, near_c, far_c)
        values += (input_part, near_d, far_d, send_d, packed)
        values = after(values)
        got_a, got_b, got_c, near_a, near_c, far_c = values[:6]
        input_part, near_d, far_d, send_d, packed = values[6:]
        input_grad = lax.all_gather(input_part, "tensor", axis=0, tiled=True)
        got_d, got_p = swap(send_d, "dp", 1), swap(packed, "dp", 1)
        got_d, got_p, layer_out = after((got_d, got_p, layer_out))
        near_a, near_b = add_low(near_a[0], got_a), add_low(near_a[1], got_b)
        near_c, far_c = add_low(near_c, got_c[:2]), add_low(far_c, got_c[2:])
        near_d, far_d = add_low(near_d, got_d[:2]), add_low(far_d, got_d[2:])
        packed = packed + got_p
        got_a, got_b = swap(near_a[1], "dp", 4), swap(near_b[1], "dp", 2)
        got_c, got_d = swap(far_c, "dp", 2), swap(far_d, "dp", 4)
        got_p = swap(packed, "dp", 2)
        values = (got_a, got_b, got_c, got_d, got_p, near_a, near_b, near_c, near_d, packed)
        got_a, got_b, got_c, got_d, got_p, near_a, near_b, near_c, near_d, packed = after(values)
        near_c, near_d = add_low(near_c, got_c), add_low(near_d, got_d)
        packed = packed + got_p
        got_c, got_d = swap(near_c[1], "dp", 4), swap(near_d[1], "dp", 2)
        got_p = swap(packed, "dp", 4)
        layer_out = move(after(layer_out, near_d))
        got_c, got_d, got_p, near_c, near_d, packed = after(
            (got_c, got_d, got_p, near_c, near_d, packed)
        )
        sum_a = near_a[0].astype(F32) + got_a.astype(F32)
        sum_b = near_b[0].astype(F32) + got_b.astype(F32)
        sum_c = near_c[0].astype(F32) + got_c.astype(F32)
        sum_d = near_d[0].astype(F32) + got_d.astype(F32)
        packed = packed + got_p

    group = lambda mlp_sum, attn_sum: jnp.concatenate([mlp_sum, attn_sum[None]])
    if not natural:
        sum_a, sum_b, sum_c, sum_d, input_grad = after((sum_a, sum_b, sum_c, sum_d, input_grad))
    parts = [group(sum_a[g], sum_c[g]) for g in (0, 1)] + [group(sum_b[g], sum_d[g]) for g in (0, 1)]
    crossed = swap(jnp.stack([parts[1], parts[2]]).astype(BF16), "tensor", TURNS[1])
    if not natural:
        got_p = swap(packed, "tensor", TURNS[1])
        crossed, got_p = after((crossed, got_p))
        packed = packed + got_p
        got_p = swap(packed, "tensor", TURNS[3])
    total = parts[0] + crossed[0].astype(F32)
    given = (parts[3] + crossed[1].astype(F32)).astype(BF16)
    given = swap(given, "tensor", TURNS[3])
    if not natural:
        given, got_p = after((given, got_p), total)
        packed = packed + got_p
    total = total + given.astype(F32)
    sum_mlp, sum_attn = total[:2], total[2]
    if not natural:
        input_grad = move(input_grad)

    part = width // n_dp
    sums = lax.dynamic_slice_in_dim(packed[:GROUP_ROWS], dp_at * part, part, 1)
    mine = lax.dynamic_slice_in_dim(packed, GROUP_ROWS + 2 * page_at, 2, 0)

    def split_last(row, like):
        part = like.shape[-1] // n_dp
        return lax.dynamic_slice_in_dim(row.reshape(like.shape), dp_at * part, part, 1)

    at = 2 * inner + heads * BINS
    return (
        layer_out,
        input_grad,
        sums[GAIN_ATTN],
        sums[SHIFT_ATTN],
        sum_attn[:, :inner],
        split_last(mine[0, :inner], b_query),
        sum_attn[:, inner : 2 * inner],
        sum_attn[:, 2 * inner : 3 * inner],
        split_last(mine[0, inner : 2 * inner], b_value),
        split_last(mine[0, 2 * inner : at], table_x),
        split_last(mine[0, at:], table_y),
        sum_attn[:, 3 * inner :].T,
        sums[B_ATTN],
        sums[GAIN_MLP],
        sums[SHIFT_MLP],
        sum_mlp[0],
        split_last(mine[1], b_in),
        sum_mlp[1].T,
        sums[B_OUT],
    )


def solution(mesh):
    split = P("tensor", None)
    return jax.shard_map(
        local,
        mesh=mesh,
        in_specs=(
            P("dp", None),
            P("dp", None),
            P("dp", None),
            P("dp", None),
            P("dp", None),
            P("dp"),
            P(),
            P(),
            P(None, "tensor"),
            split,
            P(None, "tensor"),
            P(None, "tensor"),
            split,
            split,
            split,
            split,
            P(),
            P(),
            P(),
            P(None, "tensor"),
            split,
            split,
            P(),
        ),
        out_specs=(
            P("dp", None),
            P("dp", None),
            P("dp"),
            P("dp"),
            P("dp", "tensor"),
            P("tensor", "dp"),
            P("dp", "tensor"),
            P("dp", "tensor"),
            P("tensor", "dp"),
            P("tensor", "dp"),
            P("tensor", "dp"),
            P("tensor", "dp"),
            P("dp"),
            P("dp"),
            P("dp"),
            P("dp", "tensor"),
            P("tensor", "dp"),
            P("tensor", "dp"),
            P("dp"),
        ),
        check_vma=False,
    )
```

```python
import jax
import jax.numpy as jnp
from jax import lax
from jax.experimental import pallas as pl
from jax.experimental.pallas import tpu as pltpu
from jax.sharding import PartitionSpec as P

LEVELS = 128
BINS = 64
SEGS = 16
GROUP = 8
EPS = 1e-05
BARRED = -1e30
F32 = jnp.float32
BF16 = jnp.bfloat16
VMEM_BYTES = 56 * 1024 * 1024

NN = (((1,), (0,)), ((), ()))
NT = (((1,), (1,)), ((), ()))
TN = (((0,), (0,)), ((), ()))


def mm(left, right, dims=NN):
    return lax.dot_general(left, right, dims, preferred_element_type=F32)


def norm_stats(rows):
    mean = jnp.mean(rows, axis=-1, keepdims=True)
    centred = rows - mean
    inverse = lax.rsqrt(jnp.mean(centred * centred, axis=-1, keepdims=True) + EPS)
    return centred * inverse, inverse


def norm_back(grad_out, unit, inverse, gain):
    scaled = grad_out * gain
    return inverse * (
        scaled
        - jnp.mean(scaled, axis=-1, keepdims=True)
        - unit * jnp.mean(scaled * unit, axis=-1, keepdims=True)
    )


def page_columns(marks):
    return jnp.transpose(marks.astype(F32)).astype(jnp.int32)


def segment_terms(seg_col, length):
    count = seg_col.shape[0]
    lane = lax.broadcasted_iota(jnp.int32, (count, 64), 1)
    place = lax.broadcasted_iota(jnp.int32, (count, 64), 0)
    valid = place < length
    same = seg_col == lane
    query_side = jnp.where(valid, jnp.where(same, 1.0, 0.0), jnp.where(lane == SEGS, 1.0, 0.0))
    key_side = jnp.where(
        valid,
        jnp.where(same | (lane >= SEGS), 0.0, BARRED),
        jnp.where(lane <= SEGS, BARRED, 0.0),
    )
    return query_side.astype(BF16), key_side.astype(BF16)


def level_onehot(column):
    count = column.shape[0]
    lane = lax.broadcasted_iota(jnp.int32, (count, LEVELS), 1)
    return jnp.where(column == lane, 1.0, 0.0).astype(BF16)


def level_onehot_t(row):
    count = row.shape[1]
    level = lax.broadcasted_iota(jnp.int32, (LEVELS, count), 0)
    return jnp.where(row == level, 1.0, 0.0).astype(BF16)


def lookup_pair(table_row):
    lane = lax.broadcasted_iota(jnp.int32, (8, 2 * LEVELS), 1)
    first = LEVELS - BINS // 2
    wide = jnp.concatenate([table_row, jnp.zeros((1, 2 * LEVELS - BINS), F32)], axis=1)
    wide = pltpu.roll(jnp.broadcast_to(wide, (8, 2 * LEVELS)), first, 1)
    wide = jnp.where(lane < first, table_row[:, 0:1], wide)
    wide = jnp.where(lane >= first + BINS, table_row[:, BINS - 1 : BINS], wide)
    wide = jnp.broadcast_to(wide[0:1, :], (LEVELS, 2 * LEVELS))
    table = pltpu.roll(wide, 0, 1, stride=1, stride_axis=0)[:, LEVELS:]
    high = table.astype(BF16)
    rest = (table - high.astype(F32)).astype(BF16)
    return jnp.concatenate([high, rest], axis=1)


def fold_row(sums):
    lane = lax.broadcasted_iota(jnp.int32, (1, 2 * LEVELS), 1)
    start = LEVELS - 1 - BINS // 2
    low = jnp.sum(jnp.where(lane <= start, sums, 0.0), axis=1, keepdims=True)
    high = jnp.sum(jnp.where(lane >= start + BINS - 1, sums, 0.0), axis=1, keepdims=True)
    turned = pltpu.roll(jnp.broadcast_to(sums, (8, 2 * LEVELS)), 2 * LEVELS - start, 1)
    middle = turned[0:1, :BINS]
    lane = lane[:, :BINS]
    return jnp.where(lane == 0, low, jnp.where(lane == BINS - 1, high, middle))


def whole(array):
    return pl.BlockSpec(array.shape, lambda *at: (0,) * len(array.shape))


def cost(flops, arrays, exps=0):
    return pl.CostEstimate(
        flops=int(flops) // 16,
        bytes_accessed=int(sum(a.size * a.dtype.itemsize for a in arrays)) // 16,
        transcendentals=int(exps) // 16,
    )


def small_parts(heads, size, hidden):
    inner = heads * size
    b_q = slice(0, inner)
    b_v = slice(inner, 2 * inner)
    b_in = slice(2 * inner, 2 * inner + hidden)
    at = 2 * inner + hidden
    tables = [
        [slice(at + (axis * heads + h) * BINS, at + (axis * heads + h + 1) * BINS) for axis in (0, 1)]
        for h in range(heads)
    ]
    return b_q, b_v, b_in, tables


def attn_forward_kernel(
    pick, lengths, tokens, marks, vectors, w_query, w_key, w_value, small, context, *scratch
):
    looks, q_side, k_side = scratch
    step = pl.program_id(0)
    heads = looks.shape[0]
    inner = w_query.shape[0]
    size = inner // heads
    b_q, b_v, _, tables = small_parts(heads, size, small.shape[1] - 2 * inner - 2 * heads * BINS)

    @pl.when(step == 0)
    def _():
        for h in range(heads):
            for axis in range(2):
                looks[h, axis] = lookup_pair(small[0:1, tables[h][axis]])

    unit, _ = norm_stats(tokens[0].astype(F32))
    normed = (unit * vectors[0:1, :] + vectors[1:2, :]).astype(BF16)
    queries = (mm(normed, w_query[...], NT) + small[0:1, b_q]).astype(BF16)
    keys = mm(normed, w_key[...], NT).astype(BF16)
    values = (mm(normed, w_value[...], NT) + small[0:1, b_v]).astype(BF16)
    columns = page_columns(marks[0])
    seg_q, seg_k = segment_terms(columns[:, 0:1], lengths[pick[step]])
    hot_x = level_onehot(columns[:, 1:2])
    hot_y = level_onehot(columns[:, 2:3])
    k_side[:, 128:256] = hot_x
    k_side[:, 256:384] = hot_x
    k_side[:, 384:512] = hot_y
    k_side[:, 512:640] = hot_y
    factor = jnp.asarray(size ** (-0.5), BF16)
    ones = jnp.ones((queries.shape[0], size), BF16)
    results = []
    for h in range(heads):
        lanes = slice(h * size, (h + 1) * size)
        q_side[:, 0:128] = jnp.concatenate([queries[:, lanes] * factor, seg_q], axis=1)
        k_side[:, 0:128] = jnp.concatenate([keys[:, lanes], seg_k], axis=1)
        q_side[:, 128:384] = mm(hot_x, looks[h, 0]).astype(BF16)
        q_side[:, 384:640] = mm(hot_y, looks[h, 1]).astype(BF16)
        scores = mm(q_side[...], k_side[...], NT)
        peak = jnp.max(scores, axis=1, keepdims=True)
        raised = jnp.exp(scores - peak).astype(BF16)
        both = mm(raised, jnp.concatenate([values[:, lanes], ones], axis=1))
        results.append(both[:, :size] / both[:, size : size + 1])
    context[0] = jnp.concatenate(results, axis=1).astype(BF16)


def attn_forward(heads, pages, lengths, tokens, marks, vectors, weights, small):
    _, count, width = tokens.shape
    n_pages = pages.shape[0]
    inner = weights[0].shape[0]
    flops = n_pages * (2 * count * width * 3 * inner + heads * 2 * count * count * 1400)
    return pl.pallas_call(
        attn_forward_kernel,
        out_shape=jax.ShapeDtypeStruct((n_pages, count, inner), BF16),
        grid_spec=pltpu.PrefetchScalarGridSpec(
            num_scalar_prefetch=2,
            grid=(n_pages,),
            in_specs=[
                pl.BlockSpec((1, count, width), lambda i, p, n: (p[i], 0, 0)),
                pl.BlockSpec((1,) + marks.shape[1:], lambda i, p, n: (p[i], 0, 0)),
                whole(vectors),
            ]
            + [whole(w) for w in weights]
            + [whole(small)],
            out_specs=pl.BlockSpec((1, count, inner), lambda i, p, n: (i, 0, 0)),
            scratch_shapes=[
                pltpu.VMEM((heads, 2, LEVELS, 2 * LEVELS), BF16),
                pltpu.VMEM((count, 640), BF16),
                pltpu.VMEM((count, 640), BF16),
            ],
        ),
        compiler_params=pltpu.CompilerParams(vmem_limit_bytes=VMEM_BYTES),
        cost_estimate=cost(flops, [tokens], n_pages * heads * count * count),
        name="attn_forward",
    )(pages, lengths, tokens, marks, vectors, *weights, small)


EARLY = (0, 4, 2, 6)
LATE = (0, 2, 4, 6)
TURNS = (0, 1, 3, 2)
GAIN_ATTN, SHIFT_ATTN, GAIN_MLP, SHIFT_MLP, B_ATTN, B_OUT, GROUP_ROWS = range(7)


def slot_order(turned, ordered, place, orders):
    rows = turned.shape[0] // GROUP
    for v, order in enumerate(orders):
        for slot in range(4):
            spot = place[1] ^ order[slot]
            at = slot * rows
            ordered[v, at : at + rows, :] = turned[pl.ds(pl.multiple_of(spot * rows, rows), rows), :]
            other = spot ^ 1
            at = (4 + slot) * rows
            ordered[v, at : at + rows, :] = turned[pl.ds(pl.multiple_of(other * rows, rows), rows), :]


def hand_out(values, near, far, send):
    rows = values.shape[0] // GROUP
    low = values.astype(BF16)
    for slot in range(4):
        held = (near, far)[slot // 2][slot % 2]
        held[...] = low[slot * rows : (slot + 1) * rows, :]
        send[slot][...] = low[(4 + slot) * rows : (5 + slot) * rows, :]


def mlp_chunk(state, w_up, w_down, b_up, variant, near, far, send):
    low, low_t, cotangent, cot_t, out_sum, back_sum = state
    before = mm(low[...], w_up) + b_up
    half = 0.5 * (1.0 + lax.erf(before * (0.5**0.5)))
    active = (before * half).astype(BF16)
    slope = half + before * (jnp.exp(-0.5 * before * before) * 0.3989422804014327)
    out_sum[...] += mm(active, w_down)
    grad_before = (mm(cotangent, w_down, NT) * slope).astype(BF16)
    back_sum[...] += mm(grad_before, w_up, NT)
    for side, values in ((0, mm(low_t[variant], grad_before)), (1, mm(cot_t[variant], active))):
        hand_out(
            values,
            [near.at[s, side] for s in range(2)],
            [far.at[s, side] for s in range(2)],
            [send.at[s, side] for s in range(4)],
        )
    return jnp.sum(grad_before.astype(F32), axis=0, keepdims=True)


def mlp_kernel(place, tokens, cotangent, *rest):
    contexts = rest[:4]
    w_attn, w_in, w_out, vectors, small, panels, panels_all = rest[4:11]
    pieces = rest[11 : 11 + GROUP]
    near, far, send, packed, layer_out, grad_resid = rest[11 + GROUP : 17 + GROUP]
    resid, low, low_t, cot_t, out_sum, back_sum, turned, others, extra, sems, late_sems = rest[
        17 + GROUP :
    ]
    step = pl.program_id(0)
    width, hidden = w_in.shape
    inner = w_attn.shape[0]
    rows = width // GROUP
    share = 2 * inner // GROUP
    top = cotangent[0]
    state = (low, low_t, top, cot_t, out_sum, back_sum)

    def chunk(w_up, w_down, variant):
        row = mlp_chunk(
            state,
            w_up,
            w_down,
            small[0, 0:1, 2 * inner : 2 * inner + hidden],
            variant,
            near.at[:, 0],
            far.at[:, 0],
            send.at[:, 0],
        )
        turn = jnp.where(step < 2, step, 5 - step)
        packed[pl.ds(GROUP_ROWS + 1 + 2 * (place[0] ^ turn), 1), :] = row

    late_copies = []
    for j in range(GROUP):
        spot = (place[2] ^ j) * rows
        for side in range(2):
            target = pl.multiple_of(side * width + spot, rows)
            late_copies.append(
                pltpu.make_async_copy(
                    pieces[j].at[pl.ds(side * rows, rows), :],
                    extra.at[pl.ds(target, rows), :],
                    late_sems.at[len(late_copies)],
                )
            )

    @pl.when(step == 0)
    def _():
        copies = []
        for g in range(3):
            for j in range(0, GROUP, 2):
                source = panels_all.at[j, g] if g < 2 else pieces[j]
                spot = j // 2 if g < 2 else (place[2] ^ j) // 2
                target = pl.multiple_of(g * inner + spot * share, share)
                copies.append(
                    pltpu.make_async_copy(
                        source.at[pl.ds(2 * rows, share), :],
                        others.at[pl.ds(target, share), :],
                        sems.at[len(copies)],
                    )
                )
        for copy in copies + late_copies:
            copy.start()
        packed[...] = jnp.zeros_like(packed)
        turned[...] = jnp.transpose(top)
        slot_order(turned, cot_t, place, (EARLY, LATE))
        total = tokens[0].astype(F32) + vectors[2:3, :]
        total = total + mm(contexts[0][0], w_attn[...])
        for copy in copies:
            copy.wait()
        total = total + mm(jnp.concatenate([c[0] for c in contexts[1:]], axis=1), others[...])
        resid[...] = total
        unit, _ = norm_stats(total)
        normed = (unit * vectors[3:4, :] + vectors[4:5, :]).astype(BF16)
        low[...] = normed
        turned[...] = jnp.transpose(normed)
        slot_order(turned, low_t, place, (EARLY, LATE))
        out_sum[...] = jnp.zeros_like(out_sum)
        back_sum[...] = jnp.zeros_like(back_sum)
        chunk(w_in[...], w_out[...], 0)

    @pl.when((step == 1) | (step == 2))
    def _():
        late = step >= 2
        chunk(
            panels[:, 0, :rows, :].reshape(width, hidden),
            panels[:, 0, rows : 2 * rows, :].reshape(hidden, width),
            jnp.where(late, 1, 0),
        )

    @pl.when(step == 3)
    def _():
        for copy in late_copies:
            copy.wait()
        chunk(extra[:width, :], extra[width:, :], 1)

    @pl.when(step == pl.num_programs(0) - 1)
    def _():
        wide = top.astype(F32)
        layer_out[...] = (resid[...] + (out_sum[...] + vectors[5:6, :])).astype(BF16)
        unit, inverse = norm_stats(resid[...])
        back = back_sum[...]
        grad = wide + norm_back(back, unit, inverse, vectors[3:4, :])
        grad_resid[...] = grad
        column_sum = lambda v: jnp.sum(v, axis=0, keepdims=True)
        packed[GAIN_MLP : GAIN_MLP + 1, :] = column_sum(back * unit)
        packed[SHIFT_MLP : SHIFT_MLP + 1, :] = column_sum(back)
        packed[B_ATTN : B_ATTN + 1, :] = column_sum(grad.astype(BF16).astype(F32))
        packed[B_OUT : B_OUT + 1, :] = column_sum(wide)


def mlp(place, tokens, cotangent, contexts, w_attn, w_in, w_out, vectors, small, panels, pieces):
    _, count, width = tokens.shape
    hidden = w_in.shape[1]
    inner = w_attn.shape[0]
    groups = len(contexts)
    rows = width // GROUP
    page = pl.BlockSpec((1, count, width), lambda g, p: (p[0], 0, 0))
    outs = (
        jax.ShapeDtypeStruct((2, groups, 2, rows, hidden), BF16),
        jax.ShapeDtypeStruct((2, groups, 2, rows, hidden), BF16),
        jax.ShapeDtypeStruct((4, groups, 2, rows, hidden), BF16),
        jax.ShapeDtypeStruct((16, width), F32),
        jax.ShapeDtypeStruct((count, width), BF16),
        jax.ShapeDtypeStruct((count, width), F32),
    )
    held = lambda n: pl.BlockSpec((n, 1, 2, rows, hidden), lambda g, p: (0, g, 0, 0, 0))
    return pl.pallas_call(
        mlp_kernel,
        out_shape=outs,
        grid_spec=pltpu.PrefetchScalarGridSpec(
            num_scalar_prefetch=1,
            grid=(groups,),
            in_specs=[page, page]
            + [whole(c) for c in contexts]
            + [whole(w_attn), whole(w_in), whole(w_out), whole(vectors)]
            + [
                pl.BlockSpec((1,) + small.shape[1:], lambda g, p: (g, 0, 0)),
                pl.BlockSpec(
                    (GROUP, 1, 2 * rows, width),
                    lambda g, p: (0, jnp.minimum(jnp.maximum(g - 1, 0), 1), 0, 0),
                ),
                pl.BlockSpec(memory_space=pl.ANY),
            ]
            + [pl.BlockSpec(memory_space=pl.ANY)] * GROUP,
            out_specs=(held(2), held(2), held(4), whole(outs[3]), whole(outs[4]), whole(outs[5])),
            scratch_shapes=[
                pltpu.VMEM((count, width), F32),
                pltpu.VMEM((count, width), BF16),
                pltpu.VMEM((2, width, count), BF16),
                pltpu.VMEM((2, width, count), BF16),
                pltpu.VMEM((count, width), F32),
                pltpu.VMEM((count, width), F32),
                pltpu.VMEM((width, count), BF16),
                pltpu.VMEM((3 * inner, width), BF16),
                pltpu.VMEM((2 * width, hidden), BF16),
                pltpu.SemaphoreType.DMA((12,)),
                pltpu.SemaphoreType.DMA((2 * GROUP,)),
            ],
        ),
        compiler_params=pltpu.CompilerParams(vmem_limit_bytes=VMEM_BYTES),
        cost_estimate=cost(2 * count * width * (width + 24 * hidden), outs, 4 * count * hidden),
        name="mlp",
    )(
        place,
        tokens,
        cotangent,
        *contexts,
        w_attn,
        w_in,
        w_out,
        vectors,
        small,
        panels,
        panels,
        *pieces,
    )


def attn_backward_kernel(last, groups, place, lengths, tokens, grad_resid, *rest):
    context_refs = rest[:groups]
    marks, vectors, packed_start = rest[groups : groups + 3]
    at = groups + 3
    if last:
        back_start = rest[at]
        at += 1
    n_sources = GROUP if last else 4
    sources = rest[at : at + n_sources]
    at += n_sources
    small, result, near, far, send, packed = rest[at : at + 6]
    at += 6
    low, low_t, branch, branch_t, back_sum = rest[at : at + 5]
    hot, hot_t, q_side, k_side, both_weights, context, turned, sems = rest[at + 5 :]
    step = pl.program_id(0)
    count, width = low.shape
    inner = context.shape[1]
    heads = (small.shape[2] - width - 2 * inner) // (2 * BINS)
    size = inner // heads
    b_q, b_v, _, tables = small_parts(heads, size, width)
    rows = width // GROUP
    copies = [[] for _ in range(groups)]

    def fetch(slot, source, target, size):
        copies[slot].append(
            pltpu.make_async_copy(
                source, both_weights.at[slot, pl.ds(target, size), :], sems.at[slot, len(copies[slot])]
            )
        )

    if last:
        for j in range(GROUP):
            spot = pl.multiple_of((place[2] ^ j) * rows, rows)
            for slot in range(groups):
                fetch(slot, sources[j].at[pl.ds(slot * rows, rows), :], spot, rows)
    else:
        for i in range(4):
            fetch(0, sources[i], i * inner, inner)

    @pl.when(step == 0)
    def _():
        for slot in range(groups):
            for copy in copies[slot]:
                copy.start()
        packed[...] = packed_start[...]
        unit, _ = norm_stats(tokens[0].astype(F32))
        normed = (unit * vectors[0:1, :] + vectors[1:2, :]).astype(BF16)
        order = (LATE if last else EARLY,)
        low[...] = normed
        turned[...] = jnp.transpose(normed)
        slot_order(turned, low_t, place, order)
        rounded = grad_resid[...].astype(BF16)
        branch[...] = rounded
        turned[...] = jnp.transpose(rounded)
        slot_order(turned, branch_t, place, order)
        back_sum[...] = back_start[...] if last else jnp.zeros_like(back_sum)
        columns = page_columns(marks[0])
        seg_q, seg_k = segment_terms(columns[:, 0:1], lengths[place[0]])
        hot_x = level_onehot(columns[:, 1:2])
        hot_y = level_onehot(columns[:, 2:3])
        hot[:, 0:128] = level_onehot(LEVELS - 1 - columns[:, 1:2])
        hot[:, 128:256] = level_onehot(LEVELS - 1 - columns[:, 2:3])
        hot_t[0:128, :] = level_onehot_t(marks[0, 1:2, :])
        hot_t[128:256, :] = level_onehot_t(marks[0, 2:3, :])
        q_side[:, 0:128] = jnp.concatenate([seg_q, seg_q], axis=1)
        k_side[:, 0:128] = jnp.concatenate([seg_k, seg_k], axis=1)
        k_side[:, 128:256] = hot_x
        k_side[:, 256:384] = hot_x
        k_side[:, 384:512] = hot_y
        k_side[:, 512:640] = hot_y

    for g in range(groups):

        @pl.when(step == g)
        def _(g=g):
            context[...] = context_refs[g][0]
            for copy in copies[g]:
                copy.wait()

    weights = both_weights.at[step]
    w_qkv = weights[: 3 * inner, :]
    qkv = mm(low[...], w_qkv, NT)
    queries = (qkv[:, :inner] + small[0, 0:1, b_q]).astype(BF16)
    keys = qkv[:, inner : 2 * inner].astype(BF16)
    values = (qkv[:, 2 * inner :] + small[0, 0:1, b_v]).astype(BF16)
    grad_ctx = mm(branch[...], weights[3 * inner :, :], NT).astype(BF16)
    factor = jnp.asarray(size ** (-0.5), BF16)
    grad_q, grad_k, grad_v = [], [], []
    tables_out = [[], []]
    for h in range(heads):
        lanes = slice(h * size, (h + 1) * size)
        query = queries[:, lanes] * factor
        key = keys[:, lanes]
        grad_here = grad_ctx[:, lanes]
        q_side[:, 0:size] = query
        k_side[:, 0:size] = key
        q_side[:, 128:384] = mm(
            k_side[:, 128:256], lookup_pair(small[0, 0:1, tables[h][0]])
        ).astype(BF16)
        q_side[:, 384:640] = mm(
            k_side[:, 384:512], lookup_pair(small[0, 0:1, tables[h][1]])
        ).astype(BF16)
        scores = mm(k_side[...], q_side[...], NT)
        raised = jnp.exp(scores - jnp.max(scores, axis=0, keepdims=True))
        probs = raised * (1.0 / jnp.sum(raised, axis=0, keepdims=True))
        grad_v.append(mm(probs.astype(BF16), grad_here))
        weighted = probs * mm(values[:, lanes], grad_here, NT)
        grad_scores = weighted - probs * jnp.sum(weighted, axis=0, keepdims=True)
        low_scores = grad_scores.astype(BF16)
        grad_k.append(mm(low_scores, query))
        grad_q.append(jnp.transpose(mm(key, low_scores, TN)) * (size ** (-0.5)))
        spread = mm(low_scores, hot[...]).astype(BF16)
        for axis in range(2):
            cut = slice(axis * LEVELS, (axis + 1) * LEVELS)
            square = mm(hot_t[cut, :], spread[:, cut])
            wide = jnp.concatenate([square, jnp.zeros_like(square)], axis=1)
            turned = pltpu.roll(wide, 0, 1, stride=1, stride_axis=0)
            tables_out[axis].append(fold_row(jnp.sum(turned, axis=0, keepdims=True)))
    grad_q = jnp.concatenate(grad_q, axis=1).astype(BF16)
    grad_k = jnp.concatenate(grad_k, axis=1).astype(BF16)
    grad_v = jnp.concatenate(grad_v, axis=1).astype(BF16)
    group = step + 1 if last else step
    turn = jnp.where(group < 2, group, 5 - group)
    packed[pl.ds(GROUP_ROWS + 2 * (place[0] ^ turn), 1), :] = jnp.concatenate(
        [
            jnp.sum(grad_q.astype(F32), axis=0, keepdims=True),
            jnp.sum(grad_v.astype(F32), axis=0, keepdims=True),
        ]
        + tables_out[0]
        + tables_out[1],
        axis=1,
    )
    grad_qkv = jnp.concatenate([grad_q, grad_k, grad_v], axis=1)
    back_sum[...] += mm(grad_qkv, w_qkv)
    hand_out(
        jnp.concatenate([mm(low_t[0], grad_qkv), mm(branch_t[0], context[...])], axis=1),
        [near.at[s, 0] for s in range(2)],
        [far.at[s, 0] for s in range(2)],
        [send.at[s, 0] for s in range(4)],
    )

    @pl.when(step == groups - 1)
    def _():
        back = back_sum[...]
        if last:
            unit, inverse = norm_stats(tokens[0].astype(F32))
            result[...] = (
                grad_resid[...] + norm_back(back, unit, inverse, vectors[0:1, :])
            ).astype(BF16)
            packed[GAIN_ATTN : GAIN_ATTN + 1, :] = jnp.sum(back * unit, axis=0, keepdims=True)
            packed[SHIFT_ATTN : SHIFT_ATTN + 1, :] = jnp.sum(back, axis=0, keepdims=True)
        else:
            result[...] = back


def attn_backward(
    last,
    heads,
    place,
    lengths,
    tokens,
    grad_resid,
    contexts,
    marks,
    vectors,
    packed,
    extra,
    sources,
    small,
):
    _, count, width = tokens.shape
    groups = len(contexts)
    inner = contexts[0].shape[2]
    rows = width // GROUP
    first = 1 if last else 0
    outs = (
        jax.ShapeDtypeStruct((count, width), BF16 if last else F32),
        jax.ShapeDtypeStruct((2, groups, rows, 4 * inner), BF16),
        jax.ShapeDtypeStruct((2, groups, rows, 4 * inner), BF16),
        jax.ShapeDtypeStruct((4, groups, rows, 4 * inner), BF16),
        jax.ShapeDtypeStruct(packed.shape, F32),
    )
    held = lambda n: pl.BlockSpec((n, 1, rows, 4 * inner), lambda g, p, q: (0, g, 0, 0))
    flops = groups * (6 * count * width * 4 * inner + heads * 2 * count * count * 2900)
    body = lambda *refs: attn_backward_kernel(last, groups, *refs)
    return pl.pallas_call(
        body,
        out_shape=outs,
        grid_spec=pltpu.PrefetchScalarGridSpec(
            num_scalar_prefetch=2,
            grid=(groups,),
            in_specs=[
                pl.BlockSpec((1, count, width), lambda g, p, n: (p[0], 0, 0)),
                whole(grad_resid),
            ]
            + [whole(c) for c in contexts]
            + [
                pl.BlockSpec((1,) + marks.shape[1:], lambda g, p, n: (p[0], 0, 0)),
                whole(vectors),
                whole(packed),
            ]
            + [whole(e) for e in extra]
            + [pl.BlockSpec(memory_space=pl.ANY)] * len(sources)
            + [pl.BlockSpec((1,) + small.shape[1:], lambda g, p, n: (g + first, 0, 0))],
            out_specs=(whole(outs[0]), held(2), held(2), held(4), whole(outs[4])),
            scratch_shapes=[
                pltpu.VMEM((count, width), BF16),
                pltpu.VMEM((1, width, count), BF16),
                pltpu.VMEM((count, width), BF16),
                pltpu.VMEM((1, width, count), BF16),
                pltpu.VMEM((count, width), F32),
                pltpu.VMEM((count, 256), BF16),
                pltpu.VMEM((256, count), BF16),
                pltpu.VMEM((count, 640), BF16),
                pltpu.VMEM((count, 640), BF16),
                pltpu.VMEM((groups, 4 * inner, width), BF16),
                pltpu.VMEM((count, inner), BF16),
                pltpu.VMEM((width, count), BF16),
                pltpu.SemaphoreType.DMA((groups, GROUP)),
            ],
        ),
        compiler_params=pltpu.CompilerParams(vmem_limit_bytes=VMEM_BYTES),
        cost_estimate=cost(flops, outs, groups * heads * count * count),
        name="attn_backward",
    )(
        place,
        lengths,
        tokens,
        grad_resid,
        *contexts,
        marks,
        vectors,
        packed,
        *extra,
        *sources,
        small,
    )


def move_kernel(source, target):
    target[...] = source[...]


def move(array):
    rows, width = array.shape
    spec = pl.BlockSpec((rows // 4, width), lambda i: (i, 0))
    return pl.pallas_call(
        move_kernel,
        out_shape=jax.ShapeDtypeStruct(array.shape, array.dtype),
        grid=(4,),
        in_specs=[spec],
        out_specs=spec,
        cost_estimate=cost(0, [array, array]),
        name="move",
    )(array)


def finish_kernel(place, own_mlp, own_attn, own_packed, *rest):
    mlp_parts, attn_parts = rest[:3], rest[3:6]
    grad_in, grad_out, grad_qkv, grad_attn_out = rest[6], rest[7], rest[8:11], rest[11]
    small_heads, small_hidden, vectors = rest[12:16], rest[16], rest[17:23]
    summed = rest[23]
    rows = own_attn.shape[0]
    inner = grad_qkv[0].shape[1]
    for side, target in ((0, grad_in), (1, grad_out)):
        total = own_mlp[side]
        for part in mlp_parts:
            total = total + part[side].astype(F32)
        target[...] = total
    total = own_attn[...]
    packed = own_packed[...]
    for part in attn_parts:
        total = total + part[:rows, :].astype(F32)
        for i in range(3):
            start = rows + 16 * i
            packed = packed + part[start : start + 16, :].astype(F32)
    for i in range(3):
        grad_qkv[i][...] = total[:, i * inner : (i + 1) * inner]
    grad_attn_out[...] = jnp.transpose(total[:, 3 * inner :])
    summed[...] = packed
    width = packed.shape[1]

    def lanes(row, start, size):
        wide = jnp.broadcast_to(row, (8, width))
        return pltpu.roll(wide, width - start, 1)[0:1, :size]

    share = vectors[0].shape[1]
    for i, target in enumerate(vectors):
        target[...] = lanes(packed[i : i + 1, :], place[1] * share, share)
    heads, part = small_heads[0].shape
    head_size = part * (width // share)
    mine = summed[pl.ds(GROUP_ROWS + 2 * place[0], 1), :]
    for i, target in enumerate(small_heads):
        for h in range(heads):
            start = (i * heads + h) * head_size + place[1] * part
            target[h : h + 1, :] = lanes(mine, start, part)
    mine = summed[pl.ds(GROUP_ROWS + 1 + 2 * place[0], 1), :]
    lines, part = small_hidden.shape
    for r in range(lines):
        start = r * (width // lines) + place[1] * part
        small_hidden[r : r + 1, :] = lanes(mine, start, part)


def finish(place, own_mlp, own_attn, own_packed, mlp_parts, attn_parts, heads, size, lines, n_dp):
    rows, width = own_attn.shape
    inner = heads * size
    hidden = own_mlp.shape[2]
    shapes = [(rows, hidden)] * 2 + [(rows, inner)] * 3 + [(inner, rows)]
    shapes += [(heads, size // n_dp)] * 4 + [(lines, hidden // lines // n_dp)]
    shapes += [(1, width // n_dp)] * 6
    outs = tuple(jax.ShapeDtypeStruct(s, F32) for s in shapes)
    inputs = [own_mlp, own_attn, own_packed, *mlp_parts, *attn_parts]
    return pl.pallas_call(
        finish_kernel,
        out_shape=outs,
        grid_spec=pltpu.PrefetchScalarGridSpec(
            num_scalar_prefetch=1,
            grid=(1,),
            in_specs=[whole(a) for a in inputs],
            out_specs=tuple(whole(o) for o in outs),
            scratch_shapes=[pltpu.VMEM(own_packed.shape, F32)],
        ),
        cost_estimate=cost(0, inputs),
        name="finish",
    )(place, *inputs)


def prepare_kernel(b_query, b_value, b_in, table_x, table_y, segment, box_x, box_y, *rest):
    rows, (marks, vectors, flat, row) = rest[:6], rest[6:]
    line = lambda ref: jnp.concatenate([ref[i : i + 1, :] for i in range(ref.shape[0])], axis=1)
    small = jnp.concatenate([line(v) for v in (b_query, b_value, b_in, table_x, table_y)], axis=1)
    row[...] = small
    width = flat.shape[1]
    for i in range(flat.shape[0]):
        flat[i : i + 1, :] = small[:, i * width : (i + 1) * width]
    marks[...] = jnp.zeros_like(marks)
    for p in range(marks.shape[0]):
        for i, source in enumerate((segment, box_x, box_y)):
            marks[p, i : i + 1, :] = source[p : p + 1, :]
    vectors[...] = jnp.zeros_like(vectors)
    for i, source in enumerate(rows):
        vectors[i : i + 1, :] = source[...].reshape(1, width)


def prepare(smalls, pages, rows):
    width = rows[0].shape[0]
    total = sum(v.size for v in smalls)
    outs = (
        jax.ShapeDtypeStruct((pages[0].shape[0], 8, pages[0].shape[1]), jnp.int32),
        jax.ShapeDtypeStruct((8, width), F32),
        jax.ShapeDtypeStruct((total // width, width), F32),
        jax.ShapeDtypeStruct((1, total), F32),
    )
    inputs = [*smalls, *pages, *rows]
    return pl.pallas_call(
        prepare_kernel,
        out_shape=outs,
        grid=(1,),
        in_specs=[whole(a) for a in inputs],
        out_specs=tuple(whole(o) for o in outs),
        cost_estimate=cost(0, inputs),
        name="prepare",
    )(*inputs)


def swap(array, axis, offset):
    size = lax.axis_size(axis)
    return lax.ppermute(array, axis, [(i, i ^ offset) for i in range(size)])


def add_low(left, right):
    return (left.astype(F32) + right.astype(F32)).astype(BF16)


def after(values, *first):
    flat, tree = jax.tree.flatten(values, is_leaf=lambda v: v is None)
    held = [i for i, v in enumerate(flat) if v is not None]
    tied = lax.optimization_barrier(tuple(flat[i] for i in held) + first)
    for i, v in zip(held, tied):
        flat[i] = v
    return jax.tree.unflatten(tree, flat)


def three_terms(array):
    terms, rest = [], array
    for _ in range(3):
        term = lax.reduce_precision(rest, 8, 7)
        terms.append(term.astype(BF16))
        rest = rest - term
    return terms


def with_packed(array, packed):
    return jnp.concatenate([array.reshape(-1, array.shape[-1])] + three_terms(packed), axis=0)


def take_packed(array, packed, shape):
    rows = packed.shape[0]
    for i in range(3):
        start = array.shape[0] - (3 - i) * rows
        packed = packed + array[start : start + rows].astype(F32)
    return array[: -3 * rows].reshape(shape), packed


def start_slices(own, turn):
    piece = [None] * GROUP
    piece[0] = own
    for step in turn:
        piece[step] = swap(own, "dp", step)
    return piece


def local(
    tokens,
    cotangent,
    segment,
    box_x,
    box_y,
    page_tokens,
    gain_attn,
    shift_attn,
    w_query,
    b_query,
    w_key,
    w_value,
    b_value,
    table_x,
    table_y,
    w_attn_out,
    b_attn_out,
    gain_mlp,
    shift_mlp,
    w_in,
    b_in,
    w_out,
    b_out,
):
    pages, count = segment.shape
    width = tokens.shape[1]
    heads, size = b_query.shape
    inner = heads * size
    hidden = w_in.shape[1]
    n_dp = lax.axis_size("dp")
    n_tensor = lax.axis_size("tensor")
    dp_at = lax.axis_index("dp")
    page_at = lax.axis_index("tensor")
    slice_at = dp_at % GROUP
    rows = width // GROUP
    natural = n_dp != GROUP
    place_out = 0 * slice_at if natural else slice_at
    place = jnp.stack([page_at, place_out, slice_at]).astype(jnp.int32)

    tokens3 = tokens.reshape(pages, count, width)
    cotangent3 = cotangent.reshape(pages, count, width)
    cut = lambda w, at, size: lax.dynamic_slice_in_dim(w, at * size, size, 0)
    share = 2 * inner // GROUP
    slice_mlp = [cut(w_in, slice_at, rows), cut(w_out, slice_at, rows)]
    slice_out = cut(w_attn_out, slice_at // 2, share)
    own = [w_query.T, w_key.T, w_value.T, w_attn_out]
    slice_mlp = jnp.concatenate(slice_mlp + [slice_out], axis=0)
    got = [swap(slice_mlp, "tensor", k) for k in TURNS[1:3]]

    marks, vectors, flat, small = prepare(
        (b_query, b_value, b_in, table_x, table_y),
        (segment, box_x, box_y),
        (gain_attn, shift_attn, b_attn_out, gain_mlp, shift_mlp, b_out),
    )
    order = jnp.stack([page_at ^ k for k in (1, 3, 2, 0)]).astype(jnp.int32)
    forward = lambda which: attn_forward(
        heads, which, page_tokens, tokens3, marks, vectors, own[:3], small
    )
    sent = forward(order[:2])
    slice_attn = lax.select_n(slice_at // 2, *[cut(w, slice_at % 2, inner // 2) for w in own])
    sent, turn, got, slice_attn, slice_mlp, flat = after(
        (sent, order[2:], got, slice_attn, slice_mlp, flat)
    )
    blocks = [list(range(b, b + GROUP)) for b in range(0, n_dp, GROUP)]
    groups = None if n_dp == GROUP else blocks
    panels = lax.all_gather(jnp.stack(got), "dp", axis=0, axis_index_groups=groups)
    got_last = swap(got[1], "tensor", TURNS[1])
    contexts = [swap(sent[g : g + 1], "tensor", TURNS[g + 1]) for g in (0, 1)]
    kept = forward(turn)
    contexts, kept, got_last, slice_attn, flat = after(
        (contexts, kept, got_last, slice_attn, flat)
    )

    contexts = [kept[1:2]] + contexts + [swap(kept[0:1], "tensor", TURNS[3])]
    piece = start_slices(got_last, (4, 2))
    got = [swap(slice_attn, "tensor", k) for k in TURNS[1:3]]
    contexts, piece, got, flat = after((contexts, piece, got, flat))
    piece[6] = swap(piece[4], "dp", 2)
    smalls = [flat] + [swap(flat, "tensor", k) for k in TURNS[1:3]]
    got.append(swap(got[1], "tensor", TURNS[1]))
    piece, got, smalls = after((piece, got, smalls))
    smalls.append(swap(smalls[2], "tensor", TURNS[1]))
    for j in (0, 4, 2, 6):
        piece[j + 1] = swap(piece[j], "dp", 1)
    smalls = jnp.stack(smalls).reshape(n_tensor, 1, -1)
    attn_piece = jnp.stack(got).reshape(-1, width)
    contexts, piece, smalls, panels, attn_piece = after(
        (contexts, piece, smalls, panels, attn_piece)
    )

    attn_piece = start_slices(attn_piece, (2, 4, 6))
    near_a, far_a, send_a, packed, layer_part, grad_resid = mlp(
        place, tokens3, cotangent3, contexts, w_attn_out, w_in, w_out, vectors, smalls, panels, piece
    )
    near_a, far_a, send_a, packed, layer_part, grad_resid, attn_piece = after(
        (near_a, far_a, send_a, packed, layer_part, grad_resid, attn_piece)
    )
    for j in (0, 4, 2, 6):
        attn_piece[j + 1] = swap(attn_piece[j], "dp", 1)
    layer_out = lax.all_gather(layer_part, "tensor", axis=0, tiled=True)

    def backward(last, packed_in, grad_in, extra):
        side = slice(1, 4) if last else slice(0, 1)
        return attn_backward(
            last,
            heads,
            place,
            page_tokens,
            tokens3,
            grad_in,
            contexts[side],
            marks,
            vectors,
            packed_in,
            extra,
            attn_piece if last else own,
            smalls,
        )

    if natural:
        back_part, near_c, far_c, send_c, packed = backward(False, packed, grad_resid, [])
        input_part, near_d, far_d, send_d, packed = backward(True, packed, grad_resid, [back_part])
        input_grad = lax.all_gather(input_part, "tensor", axis=0, tiled=True)
        more = n_dp // GROUP

        def scatter(near, far, given, early):
            both = jnp.stack([jnp.concatenate([near, far]), given], axis=1)
            both = both.reshape((2, 2) + both.shape[1:])
            if early:
                both = jnp.swapaxes(both, 0, 1)
            inside = both.shape[3:-2]
            both = both.reshape((GROUP,) + inside + (more, -1, both.shape[-1]))
            both = jnp.moveaxis(both, -3, 1).reshape((n_dp,) + inside + (-1, both.shape[-1]))
            total = lax.psum_scatter(both, "dp", scatter_dimension=0, tiled=False)
            return total.astype(F32)

        sum_a = scatter(near_a[:, :2], far_a[:, :2], send_a[:, :2], True)
        sum_b = scatter(near_a[:, 2:], far_a[:, 2:], send_a[:, 2:], False)
        sum_c = scatter(near_c, far_c, send_c, True)
        sum_d = scatter(near_d, far_d, send_d, False)
        packed = lax.psum(packed, ("dp", "tensor"))
    else:
        got_a = swap(send_a, "dp", 1)
        back_part, near_c, far_c, send_c, packed = backward(False, packed, grad_resid, [])
        values = (got_a, back_part, near_c, far_c, send_c, packed, grad_resid, near_a, far_a)
        values, attn_piece = after((values, attn_piece))
        got_a, back_part, near_c, far_c, send_c, packed, grad_resid, near_a, far_a = values
        near_a = [add_low(near_a[:, s], got_a[:2, s]) for s in (slice(0, 2), slice(2, 4))]
        far_a = [add_low(far_a[:, s], got_a[2:, s]) for s in (slice(0, 2), slice(2, 4))]
        near_a, far_a, back_part, packed, attn_piece = after(
            (near_a, far_a, back_part, packed, attn_piece)
        )
        got_a = swap(far_a[0], "dp", 2)
        got_b = swap(far_a[1], "dp", 4)
        got_c = swap(send_c, "dp", 1)
        input_part, near_d, far_d, send_d, packed = backward(True, packed, grad_resid, [back_part])
        input_grad = lax.all_gather(input_part, "tensor", axis=0, tiled=True)
        values = (got_a, got_b, got_c, near_a, near_c, far_c)
        values += (near_d, far_d, send_d, packed)
        values = after(values)
        got_a, got_b, got_c, near_a, near_c, far_c = values[:6]
        near_d, far_d, send_d, packed = values[6:]
        got_d, got_p = swap(send_d, "dp", 1), swap(packed, "dp", 1)
        got_d, got_p, layer_out = after((got_d, got_p, layer_out))
        packed = packed + got_p
        near_a, near_b = add_low(near_a[0], got_a), add_low(near_a[1], got_b)
        near_c, far_c = add_low(near_c, got_c[:2]), add_low(far_c, got_c[2:])
        near_d, far_d = add_low(near_d, got_d[:2]), add_low(far_d, got_d[2:])
        got_a, got_b = swap(near_a[1], "dp", 4), swap(near_b[1], "dp", 2)
        got_c, got_d = swap(far_c, "dp", 2), swap(with_packed(far_d, packed), "dp", 4)
        got_a, got_b, got_c, got_d, near_a, near_b, near_c, near_d, packed = after(
            (got_a, got_b, got_c, got_d, near_a, near_b, near_c, near_d, packed)
        )
        got_d, packed = take_packed(got_d, packed, near_d.shape)
        near_c, near_d = add_low(near_c, got_c), add_low(near_d, got_d)
        got_c, got_d = swap(near_c[1], "dp", 4), swap(with_packed(near_d[1], packed), "dp", 2)
        own_mlp = near_a[0, 0].astype(F32) + got_a[0].astype(F32)
        mlp_parts = [add_low(n[0, g], r[g]) for n, r, g in ((near_a, got_a, 1), (near_b, got_b, 0), (near_b, got_b, 1))]
        mlp_parts = [swap(p, "tensor", k) for p, k in zip(mlp_parts, TURNS[1:])]
        got_c, got_d, near_c, near_d, packed, own_mlp = after(
            (got_c, got_d, near_c, near_d, packed, own_mlp)
        )
        got_d, packed = take_packed(got_d, packed, near_d.shape[1:])
        own_attn = near_c[0, 0].astype(F32) + got_c[0].astype(F32)
        attn_parts = [add_low(n[0, g], r[g]) for n, r, g in ((near_d, got_d, 0), (near_d, got_d, 1), (near_d, got_d, 2))]
        attn_parts = [swap(with_packed(p, packed), "tensor", k) for p, k in zip(attn_parts, TURNS[1:])]
        layer_out = move(after(layer_out, own_attn))
        input_grad = move(after(input_grad, own_attn))
        mlp_parts, attn_parts, layer_out, input_grad = after(
            (mlp_parts, attn_parts, layer_out, input_grad)
        )
        done = finish(
            place,
            own_mlp,
            own_attn,
            packed,
            mlp_parts,
            attn_parts,
            heads,
            size,
            b_in.shape[0],
            n_dp,
        )
        small_vectors = [v.reshape(-1) for v in done[11:]]
        return (
            layer_out,
            input_grad,
            small_vectors[GAIN_ATTN],
            small_vectors[SHIFT_ATTN],
            done[2],
            done[6],
            done[3],
            done[4],
            done[7],
            done[8],
            done[9],
            done[5],
            small_vectors[B_ATTN],
            small_vectors[GAIN_MLP],
            small_vectors[SHIFT_MLP],
            done[0],
            done[10],
            done[1].T,
            small_vectors[B_OUT],
        )

    group = lambda mlp_sum, attn_sum: jnp.concatenate([mlp_sum, attn_sum[None]])
    sum_mlp = jnp.concatenate([sum_a, sum_b])
    sum_attn = jnp.concatenate([sum_c, sum_d])
    parts = [group(sum_mlp[g], sum_attn[g]) for g in range(n_tensor)]
    crossed = swap(jnp.stack([parts[1], parts[2]]).astype(BF16), "tensor", TURNS[1])
    total = parts[0] + crossed[0].astype(F32)
    given = (parts[3] + crossed[1].astype(F32)).astype(BF16)
    total = total + swap(given, "tensor", TURNS[3]).astype(F32)
    sum_mlp, sum_attn = total[:2], total[2]

    part = width // n_dp
    sums = lax.dynamic_slice_in_dim(packed[:GROUP_ROWS], dp_at * part, part, 1)
    mine = lax.dynamic_slice_in_dim(packed, GROUP_ROWS + 2 * page_at, 2, 0)

    def split_last(row, like):
        part = like.shape[-1] // n_dp
        return lax.dynamic_slice_in_dim(row.reshape(like.shape), dp_at * part, part, 1)

    at = 2 * inner + heads * BINS
    return (
        layer_out,
        input_grad,
        sums[GAIN_ATTN],
        sums[SHIFT_ATTN],
        sum_attn[:, :inner],
        split_last(mine[0, :inner], b_query),
        sum_attn[:, inner : 2 * inner],
        sum_attn[:, 2 * inner : 3 * inner],
        split_last(mine[0, inner : 2 * inner], b_value),
        split_last(mine[0, 2 * inner : at], table_x),
        split_last(mine[0, at:], table_y),
        sum_attn[:, 3 * inner :].T,
        sums[B_ATTN],
        sums[GAIN_MLP],
        sums[SHIFT_MLP],
        sum_mlp[0],
        split_last(mine[1], b_in),
        sum_mlp[1].T,
        sums[B_OUT],
    )


def solution(mesh):
    split = P("tensor", None)
    return jax.shard_map(
        local,
        mesh=mesh,
        in_specs=(
            P("dp", None),
            P("dp", None),
            P("dp", None),
            P("dp", None),
            P("dp", None),
            P("dp"),
            P(),
            P(),
            P(None, "tensor"),
            split,
            P(None, "tensor"),
            P(None, "tensor"),
            split,
            split,
            split,
            split,
            P(),
            P(),
            P(),
            P(None, "tensor"),
            split,
            split,
            P(),
        ),
        out_specs=(
            P("dp", None),
            P("dp", None),
            P("dp"),
            P("dp"),
            P("dp", "tensor"),
            P("tensor", "dp"),
            P("dp", "tensor"),
            P("dp", "tensor"),
            P("tensor", "dp"),
            P("tensor", "dp"),
            P("tensor", "dp"),
            P("tensor", "dp"),
            P("dp"),
            P("dp"),
            P("dp"),
            P("dp", "tensor"),
            P("tensor", "dp"),
            P("tensor", "dp"),
            P("dp"),
        ),
        check_vma=False,
    )
```

```python
import jax
import jax.numpy as jnp
from jax import lax
from jax.experimental import pallas as pl
from jax.experimental.pallas import tpu as pltpu
from jax.sharding import PartitionSpec as P

LEVELS = 128
BINS = 64
SEGS = 16
GROUP = 8
EPS = 1e-05
BARRED = -1e30
F32 = jnp.float32
BF16 = jnp.bfloat16
VMEM_BYTES = 56 * 1024 * 1024

NN = (((1,), (0,)), ((), ()))
NT = (((1,), (1,)), ((), ()))
TN = (((0,), (0,)), ((), ()))


def mm(left, right, dims=NN):
    return lax.dot_general(left, right, dims, preferred_element_type=F32)


def norm_stats(rows):
    mean = jnp.mean(rows, axis=-1, keepdims=True)
    centred = rows - mean
    inverse = lax.rsqrt(jnp.mean(centred * centred, axis=-1, keepdims=True) + EPS)
    return centred * inverse, inverse


def norm_back(grad_out, unit, inverse, gain):
    scaled = grad_out * gain
    return inverse * (
        scaled
        - jnp.mean(scaled, axis=-1, keepdims=True)
        - unit * jnp.mean(scaled * unit, axis=-1, keepdims=True)
    )


def page_columns(marks):
    return jnp.transpose(marks.astype(F32)).astype(jnp.int32)


def segment_terms(seg_col, length):
    count = seg_col.shape[0]
    lane = lax.broadcasted_iota(jnp.int32, (count, 64), 1)
    place = lax.broadcasted_iota(jnp.int32, (count, 64), 0)
    valid = place < length
    same = seg_col == lane
    query_side = jnp.where(valid, jnp.where(same, 1.0, 0.0), jnp.where(lane == SEGS, 1.0, 0.0))
    key_side = jnp.where(
        valid,
        jnp.where(same | (lane >= SEGS), 0.0, BARRED),
        jnp.where(lane <= SEGS, BARRED, 0.0),
    )
    return query_side.astype(BF16), key_side.astype(BF16)


def level_onehot(column):
    count = column.shape[0]
    lane = lax.broadcasted_iota(jnp.int32, (count, LEVELS), 1)
    return jnp.where(column == lane, 1.0, 0.0).astype(BF16)


def level_onehot_t(row):
    count = row.shape[1]
    level = lax.broadcasted_iota(jnp.int32, (LEVELS, count), 0)
    return jnp.where(row == level, 1.0, 0.0).astype(BF16)


def lookup_pair(table_row):
    lane = lax.broadcasted_iota(jnp.int32, (8, 2 * LEVELS), 1)
    first = LEVELS - BINS // 2
    wide = jnp.concatenate([table_row, jnp.zeros((1, 2 * LEVELS - BINS), F32)], axis=1)
    wide = pltpu.roll(jnp.broadcast_to(wide, (8, 2 * LEVELS)), first, 1)
    wide = jnp.where(lane < first, table_row[:, 0:1], wide)
    wide = jnp.where(lane >= first + BINS, table_row[:, BINS - 1 : BINS], wide)
    wide = jnp.broadcast_to(wide[0:1, :], (LEVELS, 2 * LEVELS))
    table = pltpu.roll(wide, 0, 1, stride=1, stride_axis=0)[:, LEVELS:]
    high = table.astype(BF16)
    rest = (table - high.astype(F32)).astype(BF16)
    return jnp.concatenate([high, rest], axis=1)


def fold_row(sums):
    lane = lax.broadcasted_iota(jnp.int32, (1, 2 * LEVELS), 1)
    start = LEVELS - 1 - BINS // 2
    low = jnp.sum(jnp.where(lane <= start, sums, 0.0), axis=1, keepdims=True)
    high = jnp.sum(jnp.where(lane >= start + BINS - 1, sums, 0.0), axis=1, keepdims=True)
    turned = pltpu.roll(jnp.broadcast_to(sums, (8, 2 * LEVELS)), 2 * LEVELS - start, 1)
    middle = turned[0:1, :BINS]
    lane = lane[:, :BINS]
    return jnp.where(lane == 0, low, jnp.where(lane == BINS - 1, high, middle))


def whole(array):
    return pl.BlockSpec(array.shape, lambda *at: (0,) * len(array.shape))


def cost(flops, arrays, exps=0):
    return pl.CostEstimate(
        flops=int(flops) // 16,
        bytes_accessed=int(sum(a.size * a.dtype.itemsize for a in arrays)) // 16,
        transcendentals=int(exps) // 16,
    )


def small_parts(heads, size, hidden):
    inner = heads * size
    b_q = slice(0, inner)
    b_v = slice(inner, 2 * inner)
    b_in = slice(2 * inner, 2 * inner + hidden)
    at = 2 * inner + hidden
    tables = [
        [slice(at + (axis * heads + h) * BINS, at + (axis * heads + h + 1) * BINS) for axis in (0, 1)]
        for h in range(heads)
    ]
    return b_q, b_v, b_in, tables


def attn_forward_kernel(
    pick, lengths, tokens, marks, vectors, w_query, w_key, w_value, small, context, *scratch
):
    looks, q_side, k_side = scratch
    step = pl.program_id(0)
    heads = looks.shape[0]
    inner = w_query.shape[0]
    size = inner // heads
    b_q, b_v, _, tables = small_parts(heads, size, small.shape[1] - 2 * inner - 2 * heads * BINS)

    @pl.when(step == 0)
    def _():
        for h in range(heads):
            for axis in range(2):
                looks[h, axis] = lookup_pair(small[0:1, tables[h][axis]])

    unit, _ = norm_stats(tokens[0].astype(F32))
    normed = (unit * vectors[0:1, :] + vectors[1:2, :]).astype(BF16)
    queries = (mm(normed, w_query[...], NT) + small[0:1, b_q]).astype(BF16)
    keys = mm(normed, w_key[...], NT).astype(BF16)
    values = (mm(normed, w_value[...], NT) + small[0:1, b_v]).astype(BF16)
    columns = page_columns(marks[0])
    seg_q, seg_k = segment_terms(columns[:, 0:1], lengths[pick[step]])
    hot_x = level_onehot(columns[:, 1:2])
    hot_y = level_onehot(columns[:, 2:3])
    k_side[:, 128:256] = hot_x
    k_side[:, 256:384] = hot_x
    k_side[:, 384:512] = hot_y
    k_side[:, 512:640] = hot_y
    factor = jnp.asarray(size ** (-0.5), BF16)
    ones = jnp.ones((queries.shape[0], size), BF16)
    results = []
    for h in range(heads):
        lanes = slice(h * size, (h + 1) * size)
        q_side[:, 0:128] = jnp.concatenate([queries[:, lanes] * factor, seg_q], axis=1)
        k_side[:, 0:128] = jnp.concatenate([keys[:, lanes], seg_k], axis=1)
        q_side[:, 128:384] = mm(hot_x, looks[h, 0]).astype(BF16)
        q_side[:, 384:640] = mm(hot_y, looks[h, 1]).astype(BF16)
        scores = mm(q_side[...], k_side[...], NT)
        peak = jnp.max(scores, axis=1, keepdims=True)
        raised = jnp.exp(scores - peak).astype(BF16)
        both = mm(raised, jnp.concatenate([values[:, lanes], ones], axis=1))
        results.append(both[:, :size] / both[:, size : size + 1])
    context[0] = jnp.concatenate(results, axis=1).astype(BF16)


def attn_forward(heads, pages, lengths, tokens, marks, vectors, weights, small):
    _, count, width = tokens.shape
    n_pages = pages.shape[0]
    inner = weights[0].shape[0]
    flops = n_pages * (2 * count * width * 3 * inner + heads * 2 * count * count * 1400)
    return pl.pallas_call(
        attn_forward_kernel,
        out_shape=jax.ShapeDtypeStruct((n_pages, count, inner), BF16),
        grid_spec=pltpu.PrefetchScalarGridSpec(
            num_scalar_prefetch=2,
            grid=(n_pages,),
            in_specs=[
                pl.BlockSpec((1, count, width), lambda i, p, n: (p[i], 0, 0)),
                pl.BlockSpec((1,) + marks.shape[1:], lambda i, p, n: (p[i], 0, 0)),
                whole(vectors),
            ]
            + [whole(w) for w in weights]
            + [whole(small)],
            out_specs=pl.BlockSpec((1, count, inner), lambda i, p, n: (i, 0, 0)),
            scratch_shapes=[
                pltpu.VMEM((heads, 2, LEVELS, 2 * LEVELS), BF16),
                pltpu.VMEM((count, 640), BF16),
                pltpu.VMEM((count, 640), BF16),
            ],
        ),
        compiler_params=pltpu.CompilerParams(vmem_limit_bytes=VMEM_BYTES),
        cost_estimate=cost(flops, [tokens], n_pages * heads * count * count),
        name="attn_forward",
    )(pages, lengths, tokens, marks, vectors, *weights, small)


EARLY = (0, 4, 2, 6)
LATE = (0, 2, 4, 6)
TURNS = (0, 1, 3, 2)
GAIN_ATTN, SHIFT_ATTN, GAIN_MLP, SHIFT_MLP, B_ATTN, B_OUT, GROUP_ROWS = range(7)


def slot_order(turned, ordered, place, orders):
    rows = turned.shape[0] // GROUP
    for v, order in enumerate(orders):
        for slot in range(4):
            spot = place[1] ^ order[slot]
            at = slot * rows
            ordered[v, at : at + rows, :] = turned[pl.ds(pl.multiple_of(spot * rows, rows), rows), :]
            other = spot ^ 1
            at = (4 + slot) * rows
            ordered[v, at : at + rows, :] = turned[pl.ds(pl.multiple_of(other * rows, rows), rows), :]


def hand_out(values, near, far, send):
    rows = values.shape[0] // GROUP
    low = values.astype(BF16)
    for slot in range(4):
        held = (near, far)[slot // 2][slot % 2]
        held[...] = low[slot * rows : (slot + 1) * rows, :]
        send[slot][...] = low[(4 + slot) * rows : (5 + slot) * rows, :]


def mlp_chunk(state, w_up, w_down, b_up, variant, near, far, send):
    low, low_t, cotangent, cot_t, out_sum, back_sum = state
    before = mm(low[...], w_up) + b_up
    half = 0.5 * (1.0 + lax.erf(before * (0.5**0.5)))
    active = (before * half).astype(BF16)
    slope = half + before * (jnp.exp(-0.5 * before * before) * 0.3989422804014327)
    out_sum[...] += mm(active, w_down)
    grad_before = (mm(cotangent, w_down, NT) * slope).astype(BF16)
    back_sum[...] += mm(grad_before, w_up, NT)
    for side, values in ((0, mm(low_t[variant], grad_before)), (1, mm(cot_t[variant], active))):
        hand_out(
            values,
            [near.at[s, side] for s in range(2)],
            [far.at[s, side] for s in range(2)],
            [send.at[s, side] for s in range(4)],
        )
    return jnp.sum(grad_before.astype(F32), axis=0, keepdims=True)


def mlp_kernel(place, tokens, cotangent, *rest):
    contexts = rest[:4]
    w_attn, w_in, w_out, vectors, small, panels, panels_all = rest[4:11]
    pieces = rest[11 : 11 + GROUP]
    near, far, send, packed, layer_out, grad_resid = rest[11 + GROUP : 17 + GROUP]
    resid, low, low_t, cot_t, out_sum, back_sum, turned, others, extra, sems, late_sems = rest[
        17 + GROUP :
    ]
    step = pl.program_id(0)
    width, hidden = w_in.shape
    inner = w_attn.shape[0]
    rows = width // GROUP
    share = 2 * inner // GROUP
    top = cotangent[0]
    state = (low, low_t, top, cot_t, out_sum, back_sum)

    def chunk(w_up, w_down, variant):
        row = mlp_chunk(
            state,
            w_up,
            w_down,
            small[0, 0:1, 2 * inner : 2 * inner + hidden],
            variant,
            near.at[:, 0],
            far.at[:, 0],
            send.at[:, 0],
        )
        turn = jnp.where(step < 2, step, 5 - step)
        packed[pl.ds(GROUP_ROWS + 1 + 2 * (place[0] ^ turn), 1), :] = row

    late_copies = []
    for j in range(GROUP):
        spot = (place[2] ^ j) * rows
        for side in range(2):
            target = pl.multiple_of(side * width + spot, rows)
            late_copies.append(
                pltpu.make_async_copy(
                    pieces[j].at[pl.ds(side * rows, rows), :],
                    extra.at[pl.ds(target, rows), :],
                    late_sems.at[len(late_copies)],
                )
            )

    @pl.when(step == 0)
    def _():
        copies = []
        for g in range(3):
            for j in range(0, GROUP, 2):
                source = panels_all.at[j, g] if g < 2 else pieces[j]
                spot = j // 2 if g < 2 else (place[2] ^ j) // 2
                target = pl.multiple_of(g * inner + spot * share, share)
                copies.append(
                    pltpu.make_async_copy(
                        source.at[pl.ds(2 * rows, share), :],
                        others.at[pl.ds(target, share), :],
                        sems.at[len(copies)],
                    )
                )
        for copy in copies + late_copies:
            copy.start()
        packed[...] = jnp.zeros_like(packed)
        turned[...] = jnp.transpose(top)
        slot_order(turned, cot_t, place, (EARLY, LATE))
        total = tokens[0].astype(F32) + vectors[2:3, :]
        total = total + mm(contexts[0][0], w_attn[...])
        for copy in copies:
            copy.wait()
        total = total + mm(jnp.concatenate([c[0] for c in contexts[1:]], axis=1), others[...])
        resid[...] = total
        unit, _ = norm_stats(total)
        normed = (unit * vectors[3:4, :] + vectors[4:5, :]).astype(BF16)
        low[...] = normed
        turned[...] = jnp.transpose(normed)
        slot_order(turned, low_t, place, (EARLY, LATE))
        out_sum[...] = jnp.zeros_like(out_sum)
        back_sum[...] = jnp.zeros_like(back_sum)
        chunk(w_in[...], w_out[...], 0)

    @pl.when((step == 1) | (step == 2))
    def _():
        late = step >= 2
        chunk(
            panels[:, 0, :rows, :].reshape(width, hidden),
            panels[:, 0, rows : 2 * rows, :].reshape(hidden, width),
            jnp.where(late, 1, 0),
        )

    @pl.when(step == 3)
    def _():
        for copy in late_copies:
            copy.wait()
        chunk(extra[:width, :], extra[width:, :], 1)

    @pl.when(step == pl.num_programs(0) - 1)
    def _():
        wide = top.astype(F32)
        layer_out[...] = (resid[...] + (out_sum[...] + vectors[5:6, :])).astype(BF16)
        unit, inverse = norm_stats(resid[...])
        back = back_sum[...]
        grad = wide + norm_back(back, unit, inverse, vectors[3:4, :])
        grad_resid[...] = grad
        column_sum = lambda v: jnp.sum(v, axis=0, keepdims=True)
        packed[GAIN_MLP : GAIN_MLP + 1, :] = column_sum(back * unit)
        packed[SHIFT_MLP : SHIFT_MLP + 1, :] = column_sum(back)
        packed[B_ATTN : B_ATTN + 1, :] = column_sum(grad.astype(BF16).astype(F32))
        packed[B_OUT : B_OUT + 1, :] = column_sum(wide)


def mlp(place, tokens, cotangent, contexts, w_attn, w_in, w_out, vectors, small, panels, pieces):
    _, count, width = tokens.shape
    hidden = w_in.shape[1]
    inner = w_attn.shape[0]
    groups = len(contexts)
    rows = width // GROUP
    page = pl.BlockSpec((1, count, width), lambda g, p: (p[0], 0, 0))
    outs = (
        jax.ShapeDtypeStruct((2, groups, 2, rows, hidden), BF16),
        jax.ShapeDtypeStruct((2, groups, 2, rows, hidden), BF16),
        jax.ShapeDtypeStruct((4, groups, 2, rows, hidden), BF16),
        jax.ShapeDtypeStruct((16, width), F32),
        jax.ShapeDtypeStruct((count, width), BF16),
        jax.ShapeDtypeStruct((count, width), F32),
    )
    held = lambda n: pl.BlockSpec((n, 1, 2, rows, hidden), lambda g, p: (0, g, 0, 0, 0))
    return pl.pallas_call(
        mlp_kernel,
        out_shape=outs,
        grid_spec=pltpu.PrefetchScalarGridSpec(
            num_scalar_prefetch=1,
            grid=(groups,),
            in_specs=[page, page]
            + [whole(c) for c in contexts]
            + [whole(w_attn), whole(w_in), whole(w_out), whole(vectors)]
            + [
                pl.BlockSpec((1,) + small.shape[1:], lambda g, p: (g, 0, 0)),
                pl.BlockSpec(
                    (GROUP, 1, 2 * rows, width),
                    lambda g, p: (0, jnp.minimum(jnp.maximum(g - 1, 0), 1), 0, 0),
                ),
                pl.BlockSpec(memory_space=pl.ANY),
            ]
            + [pl.BlockSpec(memory_space=pl.ANY)] * GROUP,
            out_specs=(held(2), held(2), held(4), whole(outs[3]), whole(outs[4]), whole(outs[5])),
            scratch_shapes=[
                pltpu.VMEM((count, width), F32),
                pltpu.VMEM((count, width), BF16),
                pltpu.VMEM((2, width, count), BF16),
                pltpu.VMEM((2, width, count), BF16),
                pltpu.VMEM((count, width), F32),
                pltpu.VMEM((count, width), F32),
                pltpu.VMEM((width, count), BF16),
                pltpu.VMEM((3 * inner, width), BF16),
                pltpu.VMEM((2 * width, hidden), BF16),
                pltpu.SemaphoreType.DMA((12,)),
                pltpu.SemaphoreType.DMA((2 * GROUP,)),
            ],
        ),
        compiler_params=pltpu.CompilerParams(vmem_limit_bytes=VMEM_BYTES),
        cost_estimate=cost(2 * count * width * (width + 24 * hidden), outs, 4 * count * hidden),
        name="mlp",
    )(
        place,
        tokens,
        cotangent,
        *contexts,
        w_attn,
        w_in,
        w_out,
        vectors,
        small,
        panels,
        panels,
        *pieces,
    )


def attn_backward_kernel(last, groups, place, lengths, tokens, grad_resid, *rest):
    context_refs = rest[:groups]
    marks, vectors, packed_start = rest[groups : groups + 3]
    at = groups + 3
    if last:
        back_start = rest[at]
        at += 1
    n_sources = GROUP if last else 4
    sources = rest[at : at + n_sources]
    at += n_sources
    small, result, near, far, send, packed = rest[at : at + 6]
    at += 6
    low, low_t, branch, branch_t, back_sum = rest[at : at + 5]
    hot, hot_t, q_side, k_side, both_weights, context, turned, sems = rest[at + 5 :]
    step = pl.program_id(0)
    count, width = low.shape
    inner = context.shape[1]
    heads = (small.shape[2] - width - 2 * inner) // (2 * BINS)
    size = inner // heads
    b_q, b_v, _, tables = small_parts(heads, size, width)
    rows = width // GROUP
    copies = [[] for _ in range(groups)]

    def fetch(slot, source, target, size):
        copies[slot].append(
            pltpu.make_async_copy(
                source, both_weights.at[slot, pl.ds(target, size), :], sems.at[slot, len(copies[slot])]
            )
        )

    if last:
        for j in range(GROUP):
            spot = pl.multiple_of((place[2] ^ j) * rows, rows)
            for slot in range(groups):
                fetch(slot, sources[j].at[pl.ds(slot * rows, rows), :], spot, rows)
    else:
        for i in range(4):
            fetch(0, sources[i], i * inner, inner)

    @pl.when(step == 0)
    def _():
        for slot in range(groups):
            for copy in copies[slot]:
                copy.start()
        packed[...] = packed_start[...]
        unit, _ = norm_stats(tokens[0].astype(F32))
        normed = (unit * vectors[0:1, :] + vectors[1:2, :]).astype(BF16)
        order = (EARLY, LATE) if last else (EARLY,)
        low[...] = normed
        turned[...] = jnp.transpose(normed)
        slot_order(turned, low_t, place, order)
        rounded = grad_resid[...].astype(BF16)
        branch[...] = rounded
        turned[...] = jnp.transpose(rounded)
        slot_order(turned, branch_t, place, order)
        back_sum[...] = back_start[...] if last else jnp.zeros_like(back_sum)
        columns = page_columns(marks[0])
        seg_q, seg_k = segment_terms(columns[:, 0:1], lengths[place[0]])
        hot_x = level_onehot(columns[:, 1:2])
        hot_y = level_onehot(columns[:, 2:3])
        hot[:, 0:128] = level_onehot(LEVELS - 1 - columns[:, 1:2])
        hot[:, 128:256] = level_onehot(LEVELS - 1 - columns[:, 2:3])
        hot_t[0:128, :] = level_onehot_t(marks[0, 1:2, :])
        hot_t[128:256, :] = level_onehot_t(marks[0, 2:3, :])
        q_side[:, 0:128] = jnp.concatenate([seg_q, seg_q], axis=1)
        k_side[:, 0:128] = jnp.concatenate([seg_k, seg_k], axis=1)
        k_side[:, 128:256] = hot_x
        k_side[:, 256:384] = hot_x
        k_side[:, 384:512] = hot_y
        k_side[:, 512:640] = hot_y

    for g in range(groups):

        @pl.when(step == g)
        def _(g=g):
            context[...] = context_refs[g][0]
            for copy in copies[g]:
                copy.wait()

    weights = both_weights.at[step]
    w_qkv = weights[: 3 * inner, :]
    qkv = mm(low[...], w_qkv, NT)
    queries = (qkv[:, :inner] + small[0, 0:1, b_q]).astype(BF16)
    keys = qkv[:, inner : 2 * inner].astype(BF16)
    values = (qkv[:, 2 * inner :] + small[0, 0:1, b_v]).astype(BF16)
    grad_ctx = mm(branch[...], weights[3 * inner :, :], NT).astype(BF16)
    factor = jnp.asarray(size ** (-0.5), BF16)
    grad_q, grad_k, grad_v = [], [], []
    tables_out = [[], []]
    for h in range(heads):
        lanes = slice(h * size, (h + 1) * size)
        query = queries[:, lanes] * factor
        key = keys[:, lanes]
        grad_here = grad_ctx[:, lanes]
        q_side[:, 0:size] = query
        k_side[:, 0:size] = key
        q_side[:, 128:384] = mm(
            k_side[:, 128:256], lookup_pair(small[0, 0:1, tables[h][0]])
        ).astype(BF16)
        q_side[:, 384:640] = mm(
            k_side[:, 384:512], lookup_pair(small[0, 0:1, tables[h][1]])
        ).astype(BF16)
        scores = mm(k_side[...], q_side[...], NT)
        raised = jnp.exp(scores - jnp.max(scores, axis=0, keepdims=True))
        probs = raised * (1.0 / jnp.sum(raised, axis=0, keepdims=True))
        grad_v.append(mm(probs.astype(BF16), grad_here))
        weighted = probs * mm(values[:, lanes], grad_here, NT)
        grad_scores = weighted - probs * jnp.sum(weighted, axis=0, keepdims=True)
        low_scores = grad_scores.astype(BF16)
        grad_k.append(mm(low_scores, query))
        grad_q.append(jnp.transpose(mm(key, low_scores, TN)) * (size ** (-0.5)))
        spread = mm(low_scores, hot[...]).astype(BF16)
        for axis in range(2):
            cut = slice(axis * LEVELS, (axis + 1) * LEVELS)
            square = mm(hot_t[cut, :], spread[:, cut])
            wide = jnp.concatenate([square, jnp.zeros_like(square)], axis=1)
            turned = pltpu.roll(wide, 0, 1, stride=1, stride_axis=0)
            tables_out[axis].append(fold_row(jnp.sum(turned, axis=0, keepdims=True)))
    grad_q = jnp.concatenate(grad_q, axis=1).astype(BF16)
    grad_k = jnp.concatenate(grad_k, axis=1).astype(BF16)
    grad_v = jnp.concatenate(grad_v, axis=1).astype(BF16)
    group = step + 1 if last else step
    turn = jnp.where(group < 2, group, 5 - group)
    packed[pl.ds(GROUP_ROWS + 2 * (place[0] ^ turn), 1), :] = jnp.concatenate(
        [
            jnp.sum(grad_q.astype(F32), axis=0, keepdims=True),
            jnp.sum(grad_v.astype(F32), axis=0, keepdims=True),
        ]
        + tables_out[0]
        + tables_out[1],
        axis=1,
    )
    grad_qkv = jnp.concatenate([grad_q, grad_k, grad_v], axis=1)
    back_sum[...] += mm(grad_qkv, w_qkv)
    variant = jnp.where(step > 0, 1, 0) if last else 0
    hand_out(
        jnp.concatenate([mm(low_t[variant], grad_qkv), mm(branch_t[variant], context[...])], axis=1),
        [near.at[s, 0] for s in range(2)],
        [far.at[s, 0] for s in range(2)],
        [send.at[s, 0] for s in range(4)],
    )

    @pl.when(step == groups - 1)
    def _():
        back = back_sum[...]
        if last:
            unit, inverse = norm_stats(tokens[0].astype(F32))
            result[...] = (
                grad_resid[...] + norm_back(back, unit, inverse, vectors[0:1, :])
            ).astype(BF16)
            packed[GAIN_ATTN : GAIN_ATTN + 1, :] = jnp.sum(back * unit, axis=0, keepdims=True)
            packed[SHIFT_ATTN : SHIFT_ATTN + 1, :] = jnp.sum(back, axis=0, keepdims=True)
        else:
            result[...] = back


def attn_backward(
    last,
    heads,
    place,
    lengths,
    tokens,
    grad_resid,
    contexts,
    marks,
    vectors,
    packed,
    extra,
    sources,
    small,
):
    _, count, width = tokens.shape
    groups = len(contexts)
    inner = contexts[0].shape[2]
    rows = width // GROUP
    first = 1 if last else 0
    outs = (
        jax.ShapeDtypeStruct((count, width), BF16 if last else F32),
        jax.ShapeDtypeStruct((2, groups, rows, 4 * inner), BF16),
        jax.ShapeDtypeStruct((2, groups, rows, 4 * inner), BF16),
        jax.ShapeDtypeStruct((4, groups, rows, 4 * inner), BF16),
        jax.ShapeDtypeStruct(packed.shape, F32),
    )
    held = lambda n: pl.BlockSpec((n, 1, rows, 4 * inner), lambda g, p, q: (0, g, 0, 0))
    flops = groups * (6 * count * width * 4 * inner + heads * 2 * count * count * 2900)
    body = lambda *refs: attn_backward_kernel(last, groups, *refs)
    return pl.pallas_call(
        body,
        out_shape=outs,
        grid_spec=pltpu.PrefetchScalarGridSpec(
            num_scalar_prefetch=2,
            grid=(groups,),
            in_specs=[
                pl.BlockSpec((1, count, width), lambda g, p, n: (p[0], 0, 0)),
                whole(grad_resid),
            ]
            + [whole(c) for c in contexts]
            + [
                pl.BlockSpec((1,) + marks.shape[1:], lambda g, p, n: (p[0], 0, 0)),
                whole(vectors),
                whole(packed),
            ]
            + [whole(e) for e in extra]
            + [pl.BlockSpec(memory_space=pl.ANY)] * len(sources)
            + [pl.BlockSpec((1,) + small.shape[1:], lambda g, p, n: (g + first, 0, 0))],
            out_specs=(whole(outs[0]), held(2), held(2), held(4), whole(outs[4])),
            scratch_shapes=[
                pltpu.VMEM((count, width), BF16),
                pltpu.VMEM((2 if last else 1, width, count), BF16),
                pltpu.VMEM((count, width), BF16),
                pltpu.VMEM((2 if last else 1, width, count), BF16),
                pltpu.VMEM((count, width), F32),
                pltpu.VMEM((count, 256), BF16),
                pltpu.VMEM((256, count), BF16),
                pltpu.VMEM((count, 640), BF16),
                pltpu.VMEM((count, 640), BF16),
                pltpu.VMEM((groups, 4 * inner, width), BF16),
                pltpu.VMEM((count, inner), BF16),
                pltpu.VMEM((width, count), BF16),
                pltpu.SemaphoreType.DMA((groups, GROUP)),
            ],
        ),
        compiler_params=pltpu.CompilerParams(vmem_limit_bytes=VMEM_BYTES),
        cost_estimate=cost(flops, outs, groups * heads * count * count),
        name="attn_backward",
    )(
        place,
        lengths,
        tokens,
        grad_resid,
        *contexts,
        marks,
        vectors,
        packed,
        *extra,
        *sources,
        small,
    )


def move_kernel(source, target):
    target[...] = source[...]


def move(array):
    rows, width = array.shape
    spec = pl.BlockSpec((rows // 4, width), lambda i: (i, 0))
    return pl.pallas_call(
        move_kernel,
        out_shape=jax.ShapeDtypeStruct(array.shape, array.dtype),
        grid=(4,),
        in_specs=[spec],
        out_specs=spec,
        cost_estimate=cost(0, [array, array]),
        name="move",
    )(array)


def finish_kernel(place, own_mlp, own_attn, own_packed, *rest):
    parts, grad_in, grad_out = rest[:3], rest[3], rest[4]
    grad_qkv, grad_attn_out = rest[5:8], rest[8]
    small_heads, small_hidden, vectors = rest[9:13], rest[13], rest[14:20]
    summed = rest[20]
    rows = own_attn.shape[0]
    inner = grad_qkv[0].shape[1]
    for side, target in ((0, grad_in), (1, grad_out)):
        total = own_mlp[side]
        for part in parts:
            total = total + part[side * rows : (side + 1) * rows, :].astype(F32)
        target[...] = total
    total = own_attn[...]
    packed = own_packed[...]
    for part in parts:
        total = total + part[2 * rows : 3 * rows, :].astype(F32)
        for i in range(3):
            start = 3 * rows + 16 * i
            packed = packed + part[start : start + 16, :].astype(F32)
    for i in range(3):
        grad_qkv[i][...] = total[:, i * inner : (i + 1) * inner]
    grad_attn_out[...] = jnp.transpose(total[:, 3 * inner :])
    summed[...] = packed
    width = packed.shape[1]

    def lanes(row, start, size):
        wide = jnp.broadcast_to(row, (8, width))
        return pltpu.roll(wide, width - start, 1)[0:1, :size]

    share = vectors[0].shape[1]
    for i, target in enumerate(vectors):
        target[...] = lanes(packed[i : i + 1, :], place[1] * share, share)
    heads, part = small_heads[0].shape
    head_size = part * (width // share)
    mine = summed[pl.ds(GROUP_ROWS + 2 * place[0], 1), :]
    for i, target in enumerate(small_heads):
        for h in range(heads):
            start = (i * heads + h) * head_size + place[1] * part
            target[h : h + 1, :] = lanes(mine, start, part)
    mine = summed[pl.ds(GROUP_ROWS + 1 + 2 * place[0], 1), :]
    lines, part = small_hidden.shape
    for r in range(lines):
        start = r * (width // lines) + place[1] * part
        small_hidden[r : r + 1, :] = lanes(mine, start, part)


def finish(place, own_mlp, own_attn, own_packed, parts, heads, size, lines, n_dp):
    rows, width = own_attn.shape
    inner = heads * size
    hidden = own_mlp.shape[2]
    shapes = [(rows, hidden)] * 2 + [(rows, inner)] * 3 + [(inner, rows)]
    shapes += [(heads, size // n_dp)] * 4 + [(lines, hidden // lines // n_dp)]
    shapes += [(1, width // n_dp)] * 6
    outs = tuple(jax.ShapeDtypeStruct(s, F32) for s in shapes)
    inputs = [own_mlp, own_attn, own_packed, *parts]
    return pl.pallas_call(
        finish_kernel,
        out_shape=outs,
        grid_spec=pltpu.PrefetchScalarGridSpec(
            num_scalar_prefetch=1,
            grid=(1,),
            in_specs=[whole(a) for a in inputs],
            out_specs=tuple(whole(o) for o in outs),
            scratch_shapes=[pltpu.VMEM(own_packed.shape, F32)],
        ),
        cost_estimate=cost(0, inputs),
        name="finish",
    )(place, *inputs)


def prepare_kernel(b_query, b_value, b_in, table_x, table_y, segment, box_x, box_y, *rest):
    rows, (marks, vectors, flat, row) = rest[:6], rest[6:]
    line = lambda ref: jnp.concatenate([ref[i : i + 1, :] for i in range(ref.shape[0])], axis=1)
    small = jnp.concatenate([line(v) for v in (b_query, b_value, b_in, table_x, table_y)], axis=1)
    row[...] = small
    width = flat.shape[1]
    for i in range(flat.shape[0]):
        flat[i : i + 1, :] = small[:, i * width : (i + 1) * width]
    marks[...] = jnp.zeros_like(marks)
    for p in range(marks.shape[0]):
        for i, source in enumerate((segment, box_x, box_y)):
            marks[p, i : i + 1, :] = source[p : p + 1, :]
    vectors[...] = jnp.zeros_like(vectors)
    for i, source in enumerate(rows):
        vectors[i : i + 1, :] = source[...].reshape(1, width)


def prepare(smalls, pages, rows):
    width = rows[0].shape[0]
    total = sum(v.size for v in smalls)
    outs = (
        jax.ShapeDtypeStruct((pages[0].shape[0], 8, pages[0].shape[1]), jnp.int32),
        jax.ShapeDtypeStruct((8, width), F32),
        jax.ShapeDtypeStruct((total // width, width), F32),
        jax.ShapeDtypeStruct((1, total), F32),
    )
    inputs = [*smalls, *pages, *rows]
    return pl.pallas_call(
        prepare_kernel,
        out_shape=outs,
        grid=(1,),
        in_specs=[whole(a) for a in inputs],
        out_specs=tuple(whole(o) for o in outs),
        cost_estimate=cost(0, inputs),
        name="prepare",
    )(*inputs)


def assemble_kernel(place, *refs):
    step = pl.program_id(0)
    for g in range(4):

        @pl.when(step == g)
        def _(g=g):
            refs[4][...] = refs[g][...]


def assemble(place, parts):
    rows, width = parts[0].shape
    turn = lambda g, p: (p[0] ^ jnp.where(g < 2, g, 5 - g), 0)
    return pl.pallas_call(
        assemble_kernel,
        out_shape=jax.ShapeDtypeStruct((4 * rows, width), parts[0].dtype),
        grid_spec=pltpu.PrefetchScalarGridSpec(
            num_scalar_prefetch=1,
            grid=(4,),
            in_specs=[whole(a) for a in parts],
            out_specs=pl.BlockSpec((rows, width), turn),
        ),
        cost_estimate=cost(0, parts),
        name="assemble",
    )(place, *parts)


def swap(array, axis, offset):
    size = lax.axis_size(axis)
    return lax.ppermute(array, axis, [(i, i ^ offset) for i in range(size)])


def add_low(left, right):
    return (left.astype(F32) + right.astype(F32)).astype(BF16)


def after(values, *first):
    flat, tree = jax.tree.flatten(values, is_leaf=lambda v: v is None)
    held = [i for i, v in enumerate(flat) if v is not None]
    tied = lax.optimization_barrier(tuple(flat[i] for i in held) + first)
    for i, v in zip(held, tied):
        flat[i] = v
    return jax.tree.unflatten(tree, flat)


def three_terms(array):
    terms, rest = [], array
    for _ in range(3):
        term = lax.reduce_precision(rest, 8, 7)
        terms.append(term.astype(BF16))
        rest = rest - term
    return terms


def with_packed(array, packed):
    return jnp.concatenate([array.reshape(-1, array.shape[-1])] + three_terms(packed), axis=0)


def take_packed(array, packed, shape):
    rows = packed.shape[0]
    for i in range(3):
        start = array.shape[0] - (3 - i) * rows
        packed = packed + array[start : start + rows].astype(F32)
    return array[: -3 * rows].reshape(shape), packed


def start_slices(own, turn):
    piece = [None] * GROUP
    piece[0] = own
    for step in turn:
        piece[step] = swap(own, "dp", step)
    return piece


def local(
    tokens,
    cotangent,
    segment,
    box_x,
    box_y,
    page_tokens,
    gain_attn,
    shift_attn,
    w_query,
    b_query,
    w_key,
    w_value,
    b_value,
    table_x,
    table_y,
    w_attn_out,
    b_attn_out,
    gain_mlp,
    shift_mlp,
    w_in,
    b_in,
    w_out,
    b_out,
):
    pages, count = segment.shape
    width = tokens.shape[1]
    heads, size = b_query.shape
    inner = heads * size
    hidden = w_in.shape[1]
    n_dp = lax.axis_size("dp")
    n_tensor = lax.axis_size("tensor")
    dp_at = lax.axis_index("dp")
    page_at = lax.axis_index("tensor")
    slice_at = dp_at % GROUP
    rows = width // GROUP
    natural = n_dp != GROUP
    place_out = 0 * slice_at if natural else slice_at
    place = jnp.stack([page_at, place_out, slice_at]).astype(jnp.int32)

    tokens3 = tokens.reshape(pages, count, width)
    cotangent3 = cotangent.reshape(pages, count, width)
    cut = lambda w, at, size: lax.dynamic_slice_in_dim(w, at * size, size, 0)
    share = 2 * inner // GROUP
    slice_mlp = [cut(w_in, slice_at, rows), cut(w_out, slice_at, rows)]
    slice_out = cut(w_attn_out, slice_at // 2, share)
    own = [w_query.T, w_key.T, w_value.T, w_attn_out]
    slice_mlp = jnp.concatenate(slice_mlp + [slice_out], axis=0)
    got = [swap(slice_mlp, "tensor", k) for k in TURNS[1:3]]

    marks, vectors, flat, small = prepare(
        (b_query, b_value, b_in, table_x, table_y),
        (segment, box_x, box_y),
        (gain_attn, shift_attn, b_attn_out, gain_mlp, shift_mlp, b_out),
    )
    order = jnp.stack([page_at ^ k for k in (1, 3, 2, 0)]).astype(jnp.int32)
    forward = lambda which: attn_forward(
        heads, which, page_tokens, tokens3, marks, vectors, own[:3], small
    )
    sent = forward(order[:2])
    slice_attn = lax.select_n(slice_at // 2, *[cut(w, slice_at % 2, inner // 2) for w in own])
    sent, turn, got, slice_attn, slice_mlp, flat = after(
        (sent, order[2:], got, slice_attn, slice_mlp, flat)
    )
    blocks = [list(range(b, b + GROUP)) for b in range(0, n_dp, GROUP)]
    groups = None if n_dp == GROUP else blocks
    panels = lax.all_gather(jnp.stack(got), "dp", axis=0, axis_index_groups=groups)
    got_last = swap(got[1], "tensor", TURNS[1])
    contexts = [swap(sent[g : g + 1], "tensor", TURNS[g + 1]) for g in (0, 1)]
    kept = forward(turn)
    contexts, kept, got_last, slice_attn, flat = after(
        (contexts, kept, got_last, slice_attn, flat)
    )

    contexts = [kept[1:2]] + contexts + [swap(kept[0:1], "tensor", TURNS[3])]
    piece = start_slices(got_last, (4, 2))
    got = [swap(slice_attn, "tensor", k) for k in TURNS[1:3]]
    contexts, piece, got, flat = after((contexts, piece, got, flat))
    piece[6] = swap(piece[4], "dp", 2)
    smalls = [flat] + [swap(flat, "tensor", k) for k in TURNS[1:3]]
    got.append(swap(got[1], "tensor", TURNS[1]))
    piece, got, smalls = after((piece, got, smalls))
    smalls.append(swap(smalls[2], "tensor", TURNS[1]))
    for j in (0, 4, 2, 6):
        piece[j + 1] = swap(piece[j], "dp", 1)
    smalls = jnp.stack(smalls).reshape(n_tensor, 1, -1)
    attn_piece = jnp.stack(got).reshape(-1, width)
    contexts, piece, smalls, panels = after((contexts, piece, smalls, panels))

    attn_piece = start_slices(attn_piece, (2, 4, 6))
    near_a, far_a, send_a, packed, layer_part, grad_resid = mlp(
        place, tokens3, cotangent3, contexts, w_attn_out, w_in, w_out, vectors, smalls, panels, piece
    )
    near_a, far_a, send_a, packed, layer_part, grad_resid, attn_piece = after(
        (near_a, far_a, send_a, packed, layer_part, grad_resid, attn_piece)
    )
    for j in (0, 4, 2, 6):
        attn_piece[j + 1] = swap(attn_piece[j], "dp", 1)
    layer_out = lax.all_gather(layer_part, "tensor", axis=0, tiled=True)

    def backward(last, packed_in, grad_in, extra):
        side = slice(1, 4) if last else slice(0, 1)
        return attn_backward(
            last,
            heads,
            place,
            page_tokens,
            tokens3,
            grad_in,
            contexts[side],
            marks,
            vectors,
            packed_in,
            extra,
            attn_piece if last else own,
            smalls,
        )

    if natural:
        back_part, near_c, far_c, send_c, packed = backward(False, packed, grad_resid, [])
        input_part, near_d, far_d, send_d, packed = backward(True, packed, grad_resid, [back_part])
        input_grad = lax.all_gather(input_part, "tensor", axis=0, tiled=True)
        more = n_dp // GROUP

        def scatter(near, far, given, early):
            both = jnp.stack([jnp.concatenate([near, far]), given], axis=1)
            both = both.reshape((2, 2) + both.shape[1:])
            if early:
                both = jnp.swapaxes(both, 0, 1)
            inside = both.shape[3:-2]
            both = both.reshape((GROUP,) + inside + (more, -1, both.shape[-1]))
            both = jnp.moveaxis(both, -3, 1).reshape((n_dp,) + inside + (-1, both.shape[-1]))
            total = lax.psum_scatter(both, "dp", scatter_dimension=0, tiled=False)
            return total.astype(F32)

        sum_a = scatter(near_a[:, :2], far_a[:, :2], send_a[:, :2], True)
        sum_b = scatter(near_a[:, 2:], far_a[:, 2:], send_a[:, 2:], False)
        sum_c = scatter(near_c, far_c, send_c, True)
        sum_d = [scatter(a[0], a[1], a[2], i == 0) for i, a in enumerate(
            [[v[:, cut] for v in (near_d, far_d, send_d)] for cut in (slice(0, 1), slice(1, 3))]
        )]
        sum_d = jnp.concatenate(sum_d)
        packed = lax.psum(packed, ("dp", "tensor"))
    else:
        got_a = swap(send_a, "dp", 1)
        back_part, near_c, far_c, send_c, packed = backward(False, packed, grad_resid, [])
        values = (got_a, back_part, near_c, far_c, send_c, packed, grad_resid, near_a, far_a)
        values, attn_piece = after((values, attn_piece))
        got_a, back_part, near_c, far_c, send_c, packed, grad_resid, near_a, far_a = values
        near_a = [add_low(near_a[:, s], got_a[:2, s]) for s in (slice(0, 2), slice(2, 4))]
        far_a = [add_low(far_a[:, s], got_a[2:, s]) for s in (slice(0, 2), slice(2, 4))]
        near_a, far_a, back_part, packed, attn_piece = after(
            (near_a, far_a, back_part, packed, attn_piece)
        )
        got_a = swap(far_a[0], "dp", 2)
        got_b = swap(far_a[1], "dp", 4)
        got_c = swap(send_c, "dp", 1)
        input_part, near_d, far_d, send_d, packed = backward(True, packed, grad_resid, [back_part])
        values = (got_a, got_b, got_c, near_a, near_c, far_c)
        values += (input_part, near_d, far_d, send_d, packed)
        values = after(values)
        got_a, got_b, got_c, near_a, near_c, far_c = values[:6]
        input_part, near_d, far_d, send_d, packed = values[6:]
        input_parts = [input_part] + [swap(input_part, "tensor", k) for k in TURNS[1:3]]
        got_d, got_p = swap(send_d, "dp", 1), swap(packed, "dp", 1)
        got_d, got_p, layer_out = after((got_d, got_p, layer_out))
        packed = packed + got_p
        first, others = slice(0, 1), slice(1, 3)
        flat2 = lambda a: a.reshape(-1, width)
        near_a, near_b = add_low(near_a[0], got_a), add_low(near_a[1], got_b)
        near_c = jnp.concatenate(
            [add_low(near_c, got_c[:2]), add_low(near_d[:, first], got_d[:2, first])], axis=1
        )
        far_c = [add_low(far_c, got_c[2:]), add_low(far_d[:, first], got_d[2:, first])]
        near_d = add_low(near_d[:, others], got_d[:2, others])
        far_d = add_low(far_d[:, others], got_d[2:, others])
        along_x = jnp.concatenate([flat2(near_b[1])] + [flat2(f) for f in far_c])
        along_y = with_packed(jnp.concatenate([flat2(near_a[1]), flat2(far_d)]), packed)
        along_x, along_y = swap(along_x, "dp", 2), swap(along_y, "dp", 4)
        along_x, along_y, near_a, near_b, near_c, near_d, packed = after(
            (along_x, along_y, near_a, near_b, near_c, near_d, packed)
        )
        size_b = near_b[1].size // width
        size_c = 2 * rows
        got_b = along_x[:size_b].reshape(near_b[1].shape)
        got_c = jnp.stack(
            [
                along_x[size_b : size_b + size_c].reshape(2, rows, width),
                along_x[size_b + size_c :].reshape(2, rows, width),
            ],
            axis=1,
        )
        got_a = along_y[:size_b].reshape(near_a[1].shape)
        got_d, packed = take_packed(along_y[size_b:], packed, near_d.shape)
        near_c, near_d = add_low(near_c, got_c), add_low(near_d, got_d)
        got_c, got_d = swap(near_c[1], "dp", 4), swap(with_packed(near_d[1], packed), "dp", 2)
        mlp_parts = [
            add_low(n[0, g], r[g])
            for n, r, g in ((near_a, got_a, 1), (near_b, got_b, 0), (near_b, got_b, 1))
        ]
        own_mlp = near_a[0, 0].astype(F32) + got_a[0].astype(F32)
        got_c, got_d, near_c, near_d, packed, own_mlp, mlp_parts, input_parts = after(
            (got_c, got_d, near_c, near_d, packed, own_mlp, mlp_parts, input_parts)
        )
        input_parts.append(swap(input_parts[2], "tensor", TURNS[1]))
        got_d, packed = take_packed(got_d, packed, near_d.shape[1:])
        own_attn = near_c[0, 0].astype(F32) + got_c[0].astype(F32)
        attn_parts = [
            add_low(n[0, g], r[g])
            for n, r, g in ((near_c, got_c, 1), (near_d, got_d, 0), (near_d, got_d, 1))
        ]
        parts = [
            swap(with_packed(jnp.concatenate([flat2(m), p]), packed), "tensor", k)
            for m, p, k in zip(mlp_parts, attn_parts, TURNS[1:])
        ]
        layer_out = move(after(layer_out, own_attn))
        input_grad = assemble(place, input_parts)
        parts, layer_out, input_grad = after((parts, layer_out, input_grad))
        done = finish(
            place,
            own_mlp,
            own_attn,
            packed,
            parts,
            heads,
            size,
            b_in.shape[0],
            n_dp,
        )
        small_vectors = [v.reshape(-1) for v in done[11:]]
        return (
            layer_out,
            input_grad,
            small_vectors[GAIN_ATTN],
            small_vectors[SHIFT_ATTN],
            done[2],
            done[6],
            done[3],
            done[4],
            done[7],
            done[8],
            done[9],
            done[5],
            small_vectors[B_ATTN],
            small_vectors[GAIN_MLP],
            small_vectors[SHIFT_MLP],
            done[0],
            done[10],
            done[1].T,
            small_vectors[B_OUT],
        )

    group = lambda mlp_sum, attn_sum: jnp.concatenate([mlp_sum, attn_sum[None]])
    sum_mlp = jnp.concatenate([sum_a, sum_b])
    sum_attn = jnp.concatenate([sum_c, sum_d])
    parts = [group(sum_mlp[g], sum_attn[g]) for g in range(n_tensor)]
    crossed = swap(jnp.stack([parts[1], parts[2]]).astype(BF16), "tensor", TURNS[1])
    total = parts[0] + crossed[0].astype(F32)
    given = (parts[3] + crossed[1].astype(F32)).astype(BF16)
    total = total + swap(given, "tensor", TURNS[3]).astype(F32)
    sum_mlp, sum_attn = total[:2], total[2]

    part = width // n_dp
    sums = lax.dynamic_slice_in_dim(packed[:GROUP_ROWS], dp_at * part, part, 1)
    mine = lax.dynamic_slice_in_dim(packed, GROUP_ROWS + 2 * page_at, 2, 0)

    def split_last(row, like):
        part = like.shape[-1] // n_dp
        return lax.dynamic_slice_in_dim(row.reshape(like.shape), dp_at * part, part, 1)

    at = 2 * inner + heads * BINS
    return (
        layer_out,
        input_grad,
        sums[GAIN_ATTN],
        sums[SHIFT_ATTN],
        sum_attn[:, :inner],
        split_last(mine[0, :inner], b_query),
        sum_attn[:, inner : 2 * inner],
        sum_attn[:, 2 * inner : 3 * inner],
        split_last(mine[0, inner : 2 * inner], b_value),
        split_last(mine[0, 2 * inner : at], table_x),
        split_last(mine[0, at:], table_y),
        sum_attn[:, 3 * inner :].T,
        sums[B_ATTN],
        sums[GAIN_MLP],
        sums[SHIFT_MLP],
        sum_mlp[0],
        split_last(mine[1], b_in),
        sum_mlp[1].T,
        sums[B_OUT],
    )


def solution(mesh):
    split = P("tensor", None)
    return jax.shard_map(
        local,
        mesh=mesh,
        in_specs=(
            P("dp", None),
            P("dp", None),
            P("dp", None),
            P("dp", None),
            P("dp", None),
            P("dp"),
            P(),
            P(),
            P(None, "tensor"),
            split,
            P(None, "tensor"),
            P(None, "tensor"),
            split,
            split,
            split,
            split,
            P(),
            P(),
            P(),
            P(None, "tensor"),
            split,
            split,
            P(),
        ),
        out_specs=(
            P("dp", None),
            P("dp", None),
            P("dp"),
            P("dp"),
            P("dp", "tensor"),
            P("tensor", "dp"),
            P("dp", "tensor"),
            P("dp", "tensor"),
            P("tensor", "dp"),
            P("tensor", "dp"),
            P("tensor", "dp"),
            P("tensor", "dp"),
            P("dp"),
            P("dp"),
            P("dp"),
            P("dp", "tensor"),
            P("tensor", "dp"),
            P("tensor", "dp"),
            P("dp"),
        ),
        check_vma=False,
    )
```

```python
import jax
import jax.numpy as jnp
from jax import lax
from jax.experimental import pallas as pl
from jax.experimental.pallas import tpu as pltpu
from jax.sharding import PartitionSpec as P

LEVELS = 128
BINS = 64
SEGS = 16
GROUP = 8
EPS = 1e-05
BARRED = -1e30
F32 = jnp.float32
BF16 = jnp.bfloat16
VMEM_BYTES = 56 * 1024 * 1024

NN = (((1,), (0,)), ((), ()))
NT = (((1,), (1,)), ((), ()))
TN = (((0,), (0,)), ((), ()))


def mm(left, right, dims=NN):
    return lax.dot_general(left, right, dims, preferred_element_type=F32)


def norm_stats(rows):
    mean = jnp.mean(rows, axis=-1, keepdims=True)
    centred = rows - mean
    inverse = lax.rsqrt(jnp.mean(centred * centred, axis=-1, keepdims=True) + EPS)
    return centred * inverse, inverse


def norm_back(grad_out, unit, inverse, gain):
    scaled = grad_out * gain
    return inverse * (
        scaled
        - jnp.mean(scaled, axis=-1, keepdims=True)
        - unit * jnp.mean(scaled * unit, axis=-1, keepdims=True)
    )


def page_columns(marks):
    return jnp.transpose(marks.astype(F32)).astype(jnp.int32)


def segment_terms(seg_col, length):
    count = seg_col.shape[0]
    lane = lax.broadcasted_iota(jnp.int32, (count, 64), 1)
    place = lax.broadcasted_iota(jnp.int32, (count, 64), 0)
    valid = place < length
    same = seg_col == lane
    query_side = jnp.where(valid, jnp.where(same, 1.0, 0.0), jnp.where(lane == SEGS, 1.0, 0.0))
    key_side = jnp.where(
        valid,
        jnp.where(same | (lane >= SEGS), 0.0, BARRED),
        jnp.where(lane <= SEGS, BARRED, 0.0),
    )
    return query_side.astype(BF16), key_side.astype(BF16)


def level_onehot(column):
    count = column.shape[0]
    lane = lax.broadcasted_iota(jnp.int32, (count, LEVELS), 1)
    return jnp.where(column == lane, 1.0, 0.0).astype(BF16)


def level_onehot_t(row):
    count = row.shape[1]
    level = lax.broadcasted_iota(jnp.int32, (LEVELS, count), 0)
    return jnp.where(row == level, 1.0, 0.0).astype(BF16)


def lookup_pair(table_row):
    lane = lax.broadcasted_iota(jnp.int32, (8, 2 * LEVELS), 1)
    first = LEVELS - BINS // 2
    wide = jnp.concatenate([table_row, jnp.zeros((1, 2 * LEVELS - BINS), F32)], axis=1)
    wide = pltpu.roll(jnp.broadcast_to(wide, (8, 2 * LEVELS)), first, 1)
    wide = jnp.where(lane < first, table_row[:, 0:1], wide)
    wide = jnp.where(lane >= first + BINS, table_row[:, BINS - 1 : BINS], wide)
    wide = jnp.broadcast_to(wide[0:1, :], (LEVELS, 2 * LEVELS))
    table = pltpu.roll(wide, 0, 1, stride=1, stride_axis=0)[:, LEVELS:]
    high = table.astype(BF16)
    rest = (table - high.astype(F32)).astype(BF16)
    return jnp.concatenate([high, rest], axis=1)


def fold_row(sums):
    lane = lax.broadcasted_iota(jnp.int32, (1, 2 * LEVELS), 1)
    start = LEVELS - 1 - BINS // 2
    low = jnp.sum(jnp.where(lane <= start, sums, 0.0), axis=1, keepdims=True)
    high = jnp.sum(jnp.where(lane >= start + BINS - 1, sums, 0.0), axis=1, keepdims=True)
    turned = pltpu.roll(jnp.broadcast_to(sums, (8, 2 * LEVELS)), 2 * LEVELS - start, 1)
    middle = turned[0:1, :BINS]
    lane = lane[:, :BINS]
    return jnp.where(lane == 0, low, jnp.where(lane == BINS - 1, high, middle))


def whole(array):
    return pl.BlockSpec(array.shape, lambda *at: (0,) * len(array.shape))


def cost(flops, arrays, exps=0):
    return pl.CostEstimate(
        flops=int(flops) // 16,
        bytes_accessed=int(sum(a.size * a.dtype.itemsize for a in arrays)) // 16,
        transcendentals=int(exps) // 16,
    )


def small_parts(heads, size, hidden):
    inner = heads * size
    b_q = slice(0, inner)
    b_v = slice(inner, 2 * inner)
    b_in = slice(2 * inner, 2 * inner + hidden)
    at = 2 * inner + hidden
    tables = [
        [slice(at + (axis * heads + h) * BINS, at + (axis * heads + h + 1) * BINS) for axis in (0, 1)]
        for h in range(heads)
    ]
    return b_q, b_v, b_in, tables


def attn_forward_kernel(
    pick, lengths, tokens, marks, vectors, w_query, w_key, w_value, small, context, *scratch
):
    looks, q_side, k_side = scratch
    step = pl.program_id(0)
    heads = looks.shape[0]
    inner = w_query.shape[0]
    size = inner // heads
    b_q, b_v, _, tables = small_parts(heads, size, small.shape[1] - 2 * inner - 2 * heads * BINS)

    @pl.when(step == 0)
    def _():
        for h in range(heads):
            for axis in range(2):
                looks[h, axis] = lookup_pair(small[0:1, tables[h][axis]])

    unit, _ = norm_stats(tokens[0].astype(F32))
    normed = (unit * vectors[0:1, :] + vectors[1:2, :]).astype(BF16)
    queries = (mm(normed, w_query[...], NT) + small[0:1, b_q]).astype(BF16)
    keys = mm(normed, w_key[...], NT).astype(BF16)
    values = (mm(normed, w_value[...], NT) + small[0:1, b_v]).astype(BF16)
    columns = page_columns(marks[0])
    seg_q, seg_k = segment_terms(columns[:, 0:1], lengths[pick[step]])
    hot_x = level_onehot(columns[:, 1:2])
    hot_y = level_onehot(columns[:, 2:3])
    k_side[:, 128:256] = hot_x
    k_side[:, 256:384] = hot_x
    k_side[:, 384:512] = hot_y
    k_side[:, 512:640] = hot_y
    factor = jnp.asarray(size ** (-0.5), BF16)
    ones = jnp.ones((queries.shape[0], size), BF16)
    results = []
    for h in range(heads):
        lanes = slice(h * size, (h + 1) * size)
        q_side[:, 0:128] = jnp.concatenate([queries[:, lanes] * factor, seg_q], axis=1)
        k_side[:, 0:128] = jnp.concatenate([keys[:, lanes], seg_k], axis=1)
        q_side[:, 128:384] = mm(hot_x, looks[h, 0]).astype(BF16)
        q_side[:, 384:640] = mm(hot_y, looks[h, 1]).astype(BF16)
        scores = mm(q_side[...], k_side[...], NT)
        peak = jnp.max(scores, axis=1, keepdims=True)
        raised = jnp.exp(scores - peak).astype(BF16)
        both = mm(raised, jnp.concatenate([values[:, lanes], ones], axis=1))
        results.append(both[:, :size] / both[:, size : size + 1])
    context[0] = jnp.concatenate(results, axis=1).astype(BF16)


def attn_forward(heads, pages, lengths, tokens, marks, vectors, weights, small):
    _, count, width = tokens.shape
    n_pages = pages.shape[0]
    inner = weights[0].shape[0]
    flops = n_pages * (2 * count * width * 3 * inner + heads * 2 * count * count * 1400)
    return pl.pallas_call(
        attn_forward_kernel,
        out_shape=jax.ShapeDtypeStruct((n_pages, count, inner), BF16),
        grid_spec=pltpu.PrefetchScalarGridSpec(
            num_scalar_prefetch=2,
            grid=(n_pages,),
            in_specs=[
                pl.BlockSpec((1, count, width), lambda i, p, n: (p[i], 0, 0)),
                pl.BlockSpec((1,) + marks.shape[1:], lambda i, p, n: (p[i], 0, 0)),
                whole(vectors),
            ]
            + [whole(w) for w in weights]
            + [whole(small)],
            out_specs=pl.BlockSpec((1, count, inner), lambda i, p, n: (i, 0, 0)),
            scratch_shapes=[
                pltpu.VMEM((heads, 2, LEVELS, 2 * LEVELS), BF16),
                pltpu.VMEM((count, 640), BF16),
                pltpu.VMEM((count, 640), BF16),
            ],
        ),
        compiler_params=pltpu.CompilerParams(vmem_limit_bytes=VMEM_BYTES),
        cost_estimate=cost(flops, [tokens], n_pages * heads * count * count),
        name="attn_forward",
    )(pages, lengths, tokens, marks, vectors, *weights, small)


EARLY = (0, 4, 2, 6)
LATE = (0, 2, 4, 6)
TURNS = (0, 1, 3, 2)
GAIN_ATTN, SHIFT_ATTN, GAIN_MLP, SHIFT_MLP, B_ATTN, B_OUT, GROUP_ROWS = range(7)


def slot_order(turned, ordered, place, orders):
    rows = turned.shape[0] // GROUP
    for v, order in enumerate(orders):
        for slot in range(4):
            spot = place[1] ^ order[slot]
            at = slot * rows
            ordered[v, at : at + rows, :] = turned[pl.ds(pl.multiple_of(spot * rows, rows), rows), :]
            other = spot ^ 1
            at = (4 + slot) * rows
            ordered[v, at : at + rows, :] = turned[pl.ds(pl.multiple_of(other * rows, rows), rows), :]


def hand_out(values, near, far, send):
    rows = values.shape[0] // GROUP
    low = values.astype(BF16)
    for slot in range(4):
        held = (near, far)[slot // 2][slot % 2]
        held[...] = low[slot * rows : (slot + 1) * rows, :]
        send[slot][...] = low[(4 + slot) * rows : (5 + slot) * rows, :]


def mlp_chunk(state, w_up, w_down, b_up, variant, near, far, send):
    low, low_t, cotangent, cot_t, out_sum, back_sum = state
    before = mm(low[...], w_up) + b_up
    half = 0.5 * (1.0 + lax.erf(before * (0.5**0.5)))
    active = (before * half).astype(BF16)
    slope = half + before * (jnp.exp(-0.5 * before * before) * 0.3989422804014327)
    out_sum[...] += mm(active, w_down)
    grad_before = (mm(cotangent, w_down, NT) * slope).astype(BF16)
    back_sum[...] += mm(grad_before, w_up, NT)
    for side, values in ((0, mm(low_t[variant], grad_before)), (1, mm(cot_t[variant], active))):
        hand_out(
            values,
            [near.at[s, side] for s in range(2)],
            [far.at[s, side] for s in range(2)],
            [send.at[s, side] for s in range(4)],
        )
    return jnp.sum(grad_before.astype(F32), axis=0, keepdims=True)


def mlp_kernel(place, tokens, cotangent, *rest):
    contexts = rest[:4]
    w_attn, w_in, w_out, vectors, small, panels, panels_all = rest[4:11]
    pieces = rest[11 : 11 + GROUP]
    near, far, send, packed, layer_out, grad_resid = rest[11 + GROUP : 17 + GROUP]
    resid, low, low_t, cot_t, out_sum, back_sum, turned, others, extra, sems, late_sems = rest[
        17 + GROUP :
    ]
    step = pl.program_id(0)
    width, hidden = w_in.shape
    inner = w_attn.shape[0]
    rows = width // GROUP
    share = 2 * inner // GROUP
    top = cotangent[0]
    state = (low, low_t, top, cot_t, out_sum, back_sum)

    def chunk(w_up, w_down, variant):
        row = mlp_chunk(
            state,
            w_up,
            w_down,
            small[0, 0:1, 2 * inner : 2 * inner + hidden],
            variant,
            near.at[:, 0],
            far.at[:, 0],
            send.at[:, 0],
        )
        turn = jnp.where(step < 2, step, 5 - step)
        packed[pl.ds(GROUP_ROWS + 1 + 2 * (place[0] ^ turn), 1), :] = row

    late_copies = []
    for j in range(GROUP):
        spot = (place[2] ^ j) * rows
        for side in range(2):
            target = pl.multiple_of(side * width + spot, rows)
            late_copies.append(
                pltpu.make_async_copy(
                    pieces[j].at[pl.ds(side * rows, rows), :],
                    extra.at[pl.ds(target, rows), :],
                    late_sems.at[len(late_copies)],
                )
            )

    @pl.when(step == 0)
    def _():
        copies = []
        for g in range(3):
            for j in range(0, GROUP, 2):
                source = panels_all.at[j, g] if g < 2 else pieces[j]
                spot = j // 2 if g < 2 else (place[2] ^ j) // 2
                target = pl.multiple_of(g * inner + spot * share, share)
                copies.append(
                    pltpu.make_async_copy(
                        source.at[pl.ds(2 * rows, share), :],
                        others.at[pl.ds(target, share), :],
                        sems.at[len(copies)],
                    )
                )
        for copy in copies + late_copies:
            copy.start()
        packed[...] = jnp.zeros_like(packed)
        turned[...] = jnp.transpose(top)
        slot_order(turned, cot_t, place, (EARLY, LATE))
        total = tokens[0].astype(F32) + vectors[2:3, :]
        total = total + mm(contexts[0][0], w_attn[...])
        for copy in copies:
            copy.wait()
        total = total + mm(jnp.concatenate([c[0] for c in contexts[1:]], axis=1), others[...])
        resid[...] = total
        unit, _ = norm_stats(total)
        normed = (unit * vectors[3:4, :] + vectors[4:5, :]).astype(BF16)
        low[...] = normed
        turned[...] = jnp.transpose(normed)
        slot_order(turned, low_t, place, (EARLY, LATE))
        out_sum[...] = jnp.zeros_like(out_sum)
        back_sum[...] = jnp.zeros_like(back_sum)
        chunk(w_in[...], w_out[...], 0)

    @pl.when((step == 1) | (step == 2))
    def _():
        late = step >= 2
        chunk(
            panels[:, 0, :rows, :].reshape(width, hidden),
            panels[:, 0, rows : 2 * rows, :].reshape(hidden, width),
            jnp.where(late, 1, 0),
        )

    @pl.when(step == 3)
    def _():
        for copy in late_copies:
            copy.wait()
        chunk(extra[:width, :], extra[width:, :], 1)

    @pl.when(step == pl.num_programs(0) - 1)
    def _():
        wide = top.astype(F32)
        layer_out[...] = (resid[...] + (out_sum[...] + vectors[5:6, :])).astype(BF16)
        unit, inverse = norm_stats(resid[...])
        back = back_sum[...]
        grad = wide + norm_back(back, unit, inverse, vectors[3:4, :])
        grad_resid[...] = grad
        column_sum = lambda v: jnp.sum(v, axis=0, keepdims=True)
        packed[GAIN_MLP : GAIN_MLP + 1, :] = column_sum(back * unit)
        packed[SHIFT_MLP : SHIFT_MLP + 1, :] = column_sum(back)
        packed[B_ATTN : B_ATTN + 1, :] = column_sum(grad.astype(BF16).astype(F32))
        packed[B_OUT : B_OUT + 1, :] = column_sum(wide)


def mlp(place, tokens, cotangent, contexts, w_attn, w_in, w_out, vectors, small, panels, pieces):
    _, count, width = tokens.shape
    hidden = w_in.shape[1]
    inner = w_attn.shape[0]
    groups = len(contexts)
    rows = width // GROUP
    page = pl.BlockSpec((1, count, width), lambda g, p: (p[0], 0, 0))
    outs = (
        jax.ShapeDtypeStruct((2, groups, 2, rows, hidden), BF16),
        jax.ShapeDtypeStruct((2, groups, 2, rows, hidden), BF16),
        jax.ShapeDtypeStruct((4, groups, 2, rows, hidden), BF16),
        jax.ShapeDtypeStruct((16, width), F32),
        jax.ShapeDtypeStruct((count, width), BF16),
        jax.ShapeDtypeStruct((count, width), F32),
    )
    held = lambda n: pl.BlockSpec((n, 1, 2, rows, hidden), lambda g, p: (0, g, 0, 0, 0))
    return pl.pallas_call(
        mlp_kernel,
        out_shape=outs,
        grid_spec=pltpu.PrefetchScalarGridSpec(
            num_scalar_prefetch=1,
            grid=(groups,),
            in_specs=[page, page]
            + [whole(c) for c in contexts]
            + [whole(w_attn), whole(w_in), whole(w_out), whole(vectors)]
            + [
                pl.BlockSpec((1,) + small.shape[1:], lambda g, p: (g, 0, 0)),
                pl.BlockSpec(
                    (GROUP, 1, 2 * rows, width),
                    lambda g, p: (0, jnp.minimum(jnp.maximum(g - 1, 0), 1), 0, 0),
                ),
                pl.BlockSpec(memory_space=pl.ANY),
            ]
            + [pl.BlockSpec(memory_space=pl.ANY)] * GROUP,
            out_specs=(held(2), held(2), held(4), whole(outs[3]), whole(outs[4]), whole(outs[5])),
            scratch_shapes=[
                pltpu.VMEM((count, width), F32),
                pltpu.VMEM((count, width), BF16),
                pltpu.VMEM((2, width, count), BF16),
                pltpu.VMEM((2, width, count), BF16),
                pltpu.VMEM((count, width), F32),
                pltpu.VMEM((count, width), F32),
                pltpu.VMEM((width, count), BF16),
                pltpu.VMEM((3 * inner, width), BF16),
                pltpu.VMEM((2 * width, hidden), BF16),
                pltpu.SemaphoreType.DMA((12,)),
                pltpu.SemaphoreType.DMA((2 * GROUP,)),
            ],
        ),
        compiler_params=pltpu.CompilerParams(vmem_limit_bytes=VMEM_BYTES),
        cost_estimate=cost(2 * count * width * (width + 24 * hidden), outs, 4 * count * hidden),
        name="mlp",
    )(
        place,
        tokens,
        cotangent,
        *contexts,
        w_attn,
        w_in,
        w_out,
        vectors,
        small,
        panels,
        panels,
        *pieces,
    )


def attn_backward_kernel(last, groups, place, lengths, tokens, grad_resid, *rest):
    context_refs = rest[:groups]
    marks, vectors, packed_start = rest[groups : groups + 3]
    at = groups + 3
    if last:
        back_start = rest[at]
        at += 1
    n_sources = GROUP if last else 4
    sources = rest[at : at + n_sources]
    at += n_sources
    small, result, near, far, send, packed = rest[at : at + 6]
    at += 6
    low, low_t, branch, branch_t, back_sum = rest[at : at + 5]
    hot, hot_t, q_side, k_side, both_weights, context, turned, sems = rest[at + 5 :]
    step = pl.program_id(0)
    count, width = low.shape
    inner = context.shape[1]
    heads = (small.shape[2] - width - 2 * inner) // (2 * BINS)
    size = inner // heads
    b_q, b_v, _, tables = small_parts(heads, size, width)
    rows = width // GROUP
    copies = [[] for _ in range(groups)]

    def fetch(slot, source, target, size):
        copies[slot].append(
            pltpu.make_async_copy(
                source, both_weights.at[slot, pl.ds(target, size), :], sems.at[slot, len(copies[slot])]
            )
        )

    if last:
        for j in range(GROUP):
            spot = pl.multiple_of((place[2] ^ j) * rows, rows)
            for slot in range(groups):
                fetch(slot, sources[j].at[pl.ds(slot * rows, rows), :], spot, rows)
    else:
        for i in range(4):
            fetch(0, sources[i], i * inner, inner)

    @pl.when(step == 0)
    def _():
        for slot in range(groups):
            for copy in copies[slot]:
                copy.start()
        packed[...] = packed_start[...]
        unit, _ = norm_stats(tokens[0].astype(F32))
        normed = (unit * vectors[0:1, :] + vectors[1:2, :]).astype(BF16)
        order = (EARLY, LATE) if last else (EARLY,)
        low[...] = normed
        turned[...] = jnp.transpose(normed)
        slot_order(turned, low_t, place, order)
        rounded = grad_resid[...].astype(BF16)
        branch[...] = rounded
        turned[...] = jnp.transpose(rounded)
        slot_order(turned, branch_t, place, order)
        back_sum[...] = back_start[...] if last else jnp.zeros_like(back_sum)
        columns = page_columns(marks[0])
        seg_q, seg_k = segment_terms(columns[:, 0:1], lengths[place[0]])
        hot_x = level_onehot(columns[:, 1:2])
        hot_y = level_onehot(columns[:, 2:3])
        hot[:, 0:128] = level_onehot(LEVELS - 1 - columns[:, 1:2])
        hot[:, 128:256] = level_onehot(LEVELS - 1 - columns[:, 2:3])
        hot_t[0:128, :] = level_onehot_t(marks[0, 1:2, :])
        hot_t[128:256, :] = level_onehot_t(marks[0, 2:3, :])
        q_side[:, 0:128] = jnp.concatenate([seg_q, seg_q], axis=1)
        k_side[:, 0:128] = jnp.concatenate([seg_k, seg_k], axis=1)
        k_side[:, 128:256] = hot_x
        k_side[:, 256:384] = hot_x
        k_side[:, 384:512] = hot_y
        k_side[:, 512:640] = hot_y

    for g in range(groups):

        @pl.when(step == g)
        def _(g=g):
            context[...] = context_refs[g][0]
            for copy in copies[g]:
                copy.wait()

    weights = both_weights.at[step]
    w_qkv = weights[: 3 * inner, :]
    qkv = mm(low[...], w_qkv, NT)
    queries = (qkv[:, :inner] + small[0, 0:1, b_q]).astype(BF16)
    keys = qkv[:, inner : 2 * inner].astype(BF16)
    values = (qkv[:, 2 * inner :] + small[0, 0:1, b_v]).astype(BF16)
    grad_ctx = mm(branch[...], weights[3 * inner :, :], NT).astype(BF16)
    factor = jnp.asarray(size ** (-0.5), BF16)
    grad_q, grad_k, grad_v = [], [], []
    tables_out = [[], []]
    for h in range(heads):
        lanes = slice(h * size, (h + 1) * size)
        query = queries[:, lanes] * factor
        key = keys[:, lanes]
        grad_here = grad_ctx[:, lanes]
        q_side[:, 0:size] = query
        k_side[:, 0:size] = key
        q_side[:, 128:384] = mm(
            k_side[:, 128:256], lookup_pair(small[0, 0:1, tables[h][0]])
        ).astype(BF16)
        q_side[:, 384:640] = mm(
            k_side[:, 384:512], lookup_pair(small[0, 0:1, tables[h][1]])
        ).astype(BF16)
        scores = mm(k_side[...], q_side[...], NT)
        raised = jnp.exp(scores - jnp.max(scores, axis=0, keepdims=True))
        probs = raised * (1.0 / jnp.sum(raised, axis=0, keepdims=True))
        grad_v.append(mm(probs.astype(BF16), grad_here))
        weighted = probs * mm(values[:, lanes], grad_here, NT)
        grad_scores = weighted - probs * jnp.sum(weighted, axis=0, keepdims=True)
        low_scores = grad_scores.astype(BF16)
        grad_k.append(mm(low_scores, query))
        grad_q.append(jnp.transpose(mm(key, low_scores, TN)) * (size ** (-0.5)))
        spread = mm(low_scores, hot[...]).astype(BF16)
        for axis in range(2):
            cut = slice(axis * LEVELS, (axis + 1) * LEVELS)
            square = mm(hot_t[cut, :], spread[:, cut])
            wide = jnp.concatenate([square, jnp.zeros_like(square)], axis=1)
            turned = pltpu.roll(wide, 0, 1, stride=1, stride_axis=0)
            tables_out[axis].append(fold_row(jnp.sum(turned, axis=0, keepdims=True)))
    grad_q = jnp.concatenate(grad_q, axis=1).astype(BF16)
    grad_k = jnp.concatenate(grad_k, axis=1).astype(BF16)
    grad_v = jnp.concatenate(grad_v, axis=1).astype(BF16)
    group = step + 1 if last else step
    turn = jnp.where(group < 2, group, 5 - group)
    packed[pl.ds(GROUP_ROWS + 2 * (place[0] ^ turn), 1), :] = jnp.concatenate(
        [
            jnp.sum(grad_q.astype(F32), axis=0, keepdims=True),
            jnp.sum(grad_v.astype(F32), axis=0, keepdims=True),
        ]
        + tables_out[0]
        + tables_out[1],
        axis=1,
    )
    grad_qkv = jnp.concatenate([grad_q, grad_k, grad_v], axis=1)
    back_sum[...] += mm(grad_qkv, w_qkv)
    variant = jnp.where(step > 0, 1, 0) if last else 0
    hand_out(
        jnp.concatenate([mm(low_t[variant], grad_qkv), mm(branch_t[variant], context[...])], axis=1),
        [near.at[s, 0] for s in range(2)],
        [far.at[s, 0] for s in range(2)],
        [send.at[s, 0] for s in range(4)],
    )

    @pl.when(step == groups - 1)
    def _():
        back = back_sum[...]
        if last:
            unit, inverse = norm_stats(tokens[0].astype(F32))
            result[...] = (
                grad_resid[...] + norm_back(back, unit, inverse, vectors[0:1, :])
            ).astype(BF16)
            packed[GAIN_ATTN : GAIN_ATTN + 1, :] = jnp.sum(back * unit, axis=0, keepdims=True)
            packed[SHIFT_ATTN : SHIFT_ATTN + 1, :] = jnp.sum(back, axis=0, keepdims=True)
        else:
            result[...] = back


def attn_backward(
    last,
    heads,
    place,
    lengths,
    tokens,
    grad_resid,
    contexts,
    marks,
    vectors,
    packed,
    extra,
    sources,
    small,
):
    _, count, width = tokens.shape
    groups = len(contexts)
    inner = contexts[0].shape[2]
    rows = width // GROUP
    first = 1 if last else 0
    outs = (
        jax.ShapeDtypeStruct((count, width), BF16 if last else F32),
        jax.ShapeDtypeStruct((2, groups, rows, 4 * inner), BF16),
        jax.ShapeDtypeStruct((2, groups, rows, 4 * inner), BF16),
        jax.ShapeDtypeStruct((4, groups, rows, 4 * inner), BF16),
        jax.ShapeDtypeStruct(packed.shape, F32),
    )
    held = lambda n: pl.BlockSpec((n, 1, rows, 4 * inner), lambda g, p, q: (0, g, 0, 0))
    flops = groups * (6 * count * width * 4 * inner + heads * 2 * count * count * 2900)
    body = lambda *refs: attn_backward_kernel(last, groups, *refs)
    return pl.pallas_call(
        body,
        out_shape=outs,
        grid_spec=pltpu.PrefetchScalarGridSpec(
            num_scalar_prefetch=2,
            grid=(groups,),
            in_specs=[
                pl.BlockSpec((1, count, width), lambda g, p, n: (p[0], 0, 0)),
                whole(grad_resid),
            ]
            + [whole(c) for c in contexts]
            + [
                pl.BlockSpec((1,) + marks.shape[1:], lambda g, p, n: (p[0], 0, 0)),
                whole(vectors),
                whole(packed),
            ]
            + [whole(e) for e in extra]
            + [pl.BlockSpec(memory_space=pl.ANY)] * len(sources)
            + [pl.BlockSpec((1,) + small.shape[1:], lambda g, p, n: (g + first, 0, 0))],
            out_specs=(whole(outs[0]), held(2), held(2), held(4), whole(outs[4])),
            scratch_shapes=[
                pltpu.VMEM((count, width), BF16),
                pltpu.VMEM((2 if last else 1, width, count), BF16),
                pltpu.VMEM((count, width), BF16),
                pltpu.VMEM((2 if last else 1, width, count), BF16),
                pltpu.VMEM((count, width), F32),
                pltpu.VMEM((count, 256), BF16),
                pltpu.VMEM((256, count), BF16),
                pltpu.VMEM((count, 640), BF16),
                pltpu.VMEM((count, 640), BF16),
                pltpu.VMEM((groups, 4 * inner, width), BF16),
                pltpu.VMEM((count, inner), BF16),
                pltpu.VMEM((width, count), BF16),
                pltpu.SemaphoreType.DMA((groups, GROUP)),
            ],
        ),
        compiler_params=pltpu.CompilerParams(vmem_limit_bytes=VMEM_BYTES),
        cost_estimate=cost(flops, outs, groups * heads * count * count),
        name="attn_backward",
    )(
        place,
        lengths,
        tokens,
        grad_resid,
        *contexts,
        marks,
        vectors,
        packed,
        *extra,
        *sources,
        small,
    )


def move_kernel(source, target):
    target[...] = source[...]


def move(array):
    rows, width = array.shape
    spec = pl.BlockSpec((rows // 4, width), lambda i: (i, 0))
    return pl.pallas_call(
        move_kernel,
        out_shape=jax.ShapeDtypeStruct(array.shape, array.dtype),
        grid=(4,),
        in_specs=[spec],
        out_specs=spec,
        cost_estimate=cost(0, [array, array]),
        name="move",
    )(array)


def finish_kernel(place, own_mlp, own_attn, own_packed, *rest):
    parts, grad_in, grad_out = rest[:3], rest[3], rest[4]
    grad_qkv, grad_attn_out = rest[5:8], rest[8]
    small_heads, small_hidden, vectors = rest[9:13], rest[13], rest[14:20]
    summed = rest[20]
    rows = own_attn.shape[0]
    inner = grad_qkv[0].shape[1]
    for side, target in ((0, grad_in), (1, grad_out)):
        total = own_mlp[side]
        for part in parts:
            total = total + part[side * rows : (side + 1) * rows, :].astype(F32)
        target[...] = total
    total = own_attn[...]
    packed = own_packed[...]
    for part in parts:
        total = total + part[2 * rows : 3 * rows, :].astype(F32)
        for i in range(3):
            start = 3 * rows + 16 * i
            packed = packed + part[start : start + 16, :].astype(F32)
    for i in range(3):
        grad_qkv[i][...] = total[:, i * inner : (i + 1) * inner]
    grad_attn_out[...] = jnp.transpose(total[:, 3 * inner :])
    summed[...] = packed
    width = packed.shape[1]

    def lanes(row, start, size):
        wide = jnp.broadcast_to(row, (8, width))
        return pltpu.roll(wide, width - start, 1)[0:1, :size]

    share = vectors[0].shape[1]
    for i, target in enumerate(vectors):
        target[...] = lanes(packed[i : i + 1, :], place[1] * share, share)
    heads, part = small_heads[0].shape
    head_size = part * (width // share)
    mine = summed[pl.ds(GROUP_ROWS + 2 * place[0], 1), :]
    for i, target in enumerate(small_heads):
        for h in range(heads):
            start = (i * heads + h) * head_size + place[1] * part
            target[h : h + 1, :] = lanes(mine, start, part)
    mine = summed[pl.ds(GROUP_ROWS + 1 + 2 * place[0], 1), :]
    lines, part = small_hidden.shape
    for r in range(lines):
        start = r * (width // lines) + place[1] * part
        small_hidden[r : r + 1, :] = lanes(mine, start, part)


def finish(place, own_mlp, own_attn, own_packed, parts, heads, size, lines, n_dp):
    rows, width = own_attn.shape
    inner = heads * size
    hidden = own_mlp.shape[2]
    shapes = [(rows, hidden)] * 2 + [(rows, inner)] * 3 + [(inner, rows)]
    shapes += [(heads, size // n_dp)] * 4 + [(lines, hidden // lines // n_dp)]
    shapes += [(1, width // n_dp)] * 6
    outs = tuple(jax.ShapeDtypeStruct(s, F32) for s in shapes)
    inputs = [own_mlp, own_attn, own_packed, *parts]
    return pl.pallas_call(
        finish_kernel,
        out_shape=outs,
        grid_spec=pltpu.PrefetchScalarGridSpec(
            num_scalar_prefetch=1,
            grid=(1,),
            in_specs=[whole(a) for a in inputs],
            out_specs=tuple(whole(o) for o in outs),
            scratch_shapes=[pltpu.VMEM(own_packed.shape, F32)],
        ),
        cost_estimate=cost(0, inputs),
        name="finish",
    )(place, *inputs)


def prepare_kernel(b_query, b_value, b_in, table_x, table_y, segment, box_x, box_y, *rest):
    rows, (marks, vectors, flat, row) = rest[:6], rest[6:]
    line = lambda ref: jnp.concatenate([ref[i : i + 1, :] for i in range(ref.shape[0])], axis=1)
    small = jnp.concatenate([line(v) for v in (b_query, b_value, b_in, table_x, table_y)], axis=1)
    row[...] = small
    width = flat.shape[1]
    for i in range(flat.shape[0]):
        flat[i : i + 1, :] = small[:, i * width : (i + 1) * width]
    marks[...] = jnp.zeros_like(marks)
    for p in range(marks.shape[0]):
        for i, source in enumerate((segment, box_x, box_y)):
            marks[p, i : i + 1, :] = source[p : p + 1, :]
    vectors[...] = jnp.zeros_like(vectors)
    for i, source in enumerate(rows):
        vectors[i : i + 1, :] = source[...].reshape(1, width)


def prepare(smalls, pages, rows):
    width = rows[0].shape[0]
    total = sum(v.size for v in smalls)
    outs = (
        jax.ShapeDtypeStruct((pages[0].shape[0], 8, pages[0].shape[1]), jnp.int32),
        jax.ShapeDtypeStruct((8, width), F32),
        jax.ShapeDtypeStruct((total // width, width), F32),
        jax.ShapeDtypeStruct((1, total), F32),
    )
    inputs = [*smalls, *pages, *rows]
    return pl.pallas_call(
        prepare_kernel,
        out_shape=outs,
        grid=(1,),
        in_specs=[whole(a) for a in inputs],
        out_specs=tuple(whole(o) for o in outs),
        cost_estimate=cost(0, inputs),
        name="prepare",
    )(*inputs)


def assemble_kernel(place, *refs):
    step = pl.program_id(0)
    for g in range(4):

        @pl.when(step == g)
        def _(g=g):
            refs[4][...] = refs[g][...]


def assemble(place, parts):
    rows, width = parts[0].shape
    turn = lambda g, p: (p[0] ^ jnp.where(g < 2, g, 5 - g), 0)
    return pl.pallas_call(
        assemble_kernel,
        out_shape=jax.ShapeDtypeStruct((4 * rows, width), parts[0].dtype),
        grid_spec=pltpu.PrefetchScalarGridSpec(
            num_scalar_prefetch=1,
            grid=(4,),
            in_specs=[whole(a) for a in parts],
            out_specs=pl.BlockSpec((rows, width), turn),
        ),
        cost_estimate=cost(0, parts),
        name="assemble",
    )(place, *parts)


def swap(array, axis, offset):
    size = lax.axis_size(axis)
    return lax.ppermute(array, axis, [(i, i ^ offset) for i in range(size)])


def add_low(left, right):
    return (left.astype(F32) + right.astype(F32)).astype(BF16)


def after(values, *first):
    flat, tree = jax.tree.flatten(values, is_leaf=lambda v: v is None)
    held = [i for i, v in enumerate(flat) if v is not None]
    tied = lax.optimization_barrier(tuple(flat[i] for i in held) + first)
    for i, v in zip(held, tied):
        flat[i] = v
    return jax.tree.unflatten(tree, flat)


def three_terms(array):
    terms, rest = [], array
    for _ in range(3):
        term = lax.reduce_precision(rest, 8, 7)
        terms.append(term.astype(BF16))
        rest = rest - term
    return terms


def with_packed(array, packed):
    return jnp.concatenate([array.reshape(-1, array.shape[-1])] + three_terms(packed), axis=0)


def take_packed(array, packed, shape):
    rows = packed.shape[0]
    for i in range(3):
        start = array.shape[0] - (3 - i) * rows
        packed = packed + array[start : start + rows].astype(F32)
    return array[: -3 * rows].reshape(shape), packed


def start_slices(own, turn):
    piece = [None] * GROUP
    piece[0] = own
    for step in turn:
        piece[step] = swap(own, "dp", step)
    return piece


def local(
    tokens,
    cotangent,
    segment,
    box_x,
    box_y,
    page_tokens,
    gain_attn,
    shift_attn,
    w_query,
    b_query,
    w_key,
    w_value,
    b_value,
    table_x,
    table_y,
    w_attn_out,
    b_attn_out,
    gain_mlp,
    shift_mlp,
    w_in,
    b_in,
    w_out,
    b_out,
):
    pages, count = segment.shape
    width = tokens.shape[1]
    heads, size = b_query.shape
    inner = heads * size
    hidden = w_in.shape[1]
    n_dp = lax.axis_size("dp")
    n_tensor = lax.axis_size("tensor")
    dp_at = lax.axis_index("dp")
    page_at = lax.axis_index("tensor")
    slice_at = dp_at % GROUP
    rows = width // GROUP
    natural = n_dp != GROUP
    place_out = 0 * slice_at if natural else slice_at
    place = jnp.stack([page_at, place_out, slice_at]).astype(jnp.int32)

    tokens3 = tokens.reshape(pages, count, width)
    cotangent3 = cotangent.reshape(pages, count, width)
    cut = lambda w, at, size: lax.dynamic_slice_in_dim(w, at * size, size, 0)
    share = 2 * inner // GROUP
    slice_mlp = [cut(w_in, slice_at, rows), cut(w_out, slice_at, rows)]
    slice_out = cut(w_attn_out, slice_at // 2, share)
    own = [w_query.T, w_key.T, w_value.T, w_attn_out]
    slice_mlp = jnp.concatenate(slice_mlp + [slice_out], axis=0)
    got = [swap(slice_mlp, "tensor", k) for k in TURNS[1:3]]

    marks, vectors, flat, small = prepare(
        (b_query, b_value, b_in, table_x, table_y),
        (segment, box_x, box_y),
        (gain_attn, shift_attn, b_attn_out, gain_mlp, shift_mlp, b_out),
    )
    order = jnp.stack([page_at ^ k for k in (1, 3, 2, 0)]).astype(jnp.int32)
    forward = lambda which: attn_forward(
        heads, which, page_tokens, tokens3, marks, vectors, own[:3], small
    )
    sent = forward(order[:2])
    slice_attn = lax.select_n(slice_at // 2, *[cut(w, slice_at % 2, inner // 2) for w in own])
    sent, turn, got, slice_attn, slice_mlp, flat = after(
        (sent, order[2:], got, slice_attn, slice_mlp, flat)
    )
    blocks = [list(range(b, b + GROUP)) for b in range(0, n_dp, GROUP)]
    groups = None if n_dp == GROUP else blocks
    panels = lax.all_gather(jnp.stack(got), "dp", axis=0, axis_index_groups=groups)
    got_last = swap(got[1], "tensor", TURNS[1])
    contexts = [swap(sent[g : g + 1], "tensor", TURNS[g + 1]) for g in (0, 1)]
    kept = forward(turn)
    contexts, kept, got_last, slice_attn, flat = after(
        (contexts, kept, got_last, slice_attn, flat)
    )

    contexts = [kept[1:2]] + contexts + [swap(kept[0:1], "tensor", TURNS[3])]
    piece = start_slices(got_last, (4, 2))
    got = [swap(slice_attn, "tensor", k) for k in TURNS[1:3]]
    contexts, piece, got, flat, place = after((contexts, piece, got, flat, place))
    piece[6] = swap(piece[4], "dp", 2)
    smalls = [flat] + [swap(flat, "tensor", k) for k in TURNS[1:]]
    got.append(swap(got[1], "tensor", TURNS[1]))
    piece, got, smalls = after((piece, got, smalls))
    for j in (0, 4, 2, 6):
        piece[j + 1] = swap(piece[j], "dp", 1)
    attn_piece = start_slices(jnp.stack(got).reshape(-1, width), (2, 4, 6))
    smalls = jnp.stack(smalls).reshape(n_tensor, 1, -1)
    contexts, piece, smalls, panels = after((contexts, piece, smalls, panels))

    near_a, far_a, send_a, packed, layer_part, grad_resid = mlp(
        place, tokens3, cotangent3, contexts, w_attn_out, w_in, w_out, vectors, smalls, panels, piece
    )
    near_a, far_a, send_a, packed, layer_part, grad_resid, attn_piece = after(
        (near_a, far_a, send_a, packed, layer_part, grad_resid, attn_piece)
    )
    for j in (0, 4, 2, 6):
        attn_piece[j + 1] = swap(attn_piece[j], "dp", 1)
    layer_out = lax.all_gather(layer_part, "tensor", axis=0, tiled=True)

    def backward(last, packed_in, grad_in, extra):
        side = slice(1, 4) if last else slice(0, 1)
        return attn_backward(
            last,
            heads,
            place,
            page_tokens,
            tokens3,
            grad_in,
            contexts[side],
            marks,
            vectors,
            packed_in,
            extra,
            attn_piece if last else own,
            smalls,
        )

    if natural:
        back_part, near_c, far_c, send_c, packed = backward(False, packed, grad_resid, [])
        input_part, near_d, far_d, send_d, packed = backward(True, packed, grad_resid, [back_part])
        input_grad = lax.all_gather(input_part, "tensor", axis=0, tiled=True)
        more = n_dp // GROUP

        def scatter(near, far, given, early):
            both = jnp.stack([jnp.concatenate([near, far]), given], axis=1)
            both = both.reshape((2, 2) + both.shape[1:])
            if early:
                both = jnp.swapaxes(both, 0, 1)
            inside = both.shape[3:-2]
            both = both.reshape((GROUP,) + inside + (more, -1, both.shape[-1]))
            both = jnp.moveaxis(both, -3, 1).reshape((n_dp,) + inside + (-1, both.shape[-1]))
            total = lax.psum_scatter(both, "dp", scatter_dimension=0, tiled=False)
            return total.astype(F32)

        sum_a = scatter(near_a[:, :2], far_a[:, :2], send_a[:, :2], True)
        sum_b = scatter(near_a[:, 2:], far_a[:, 2:], send_a[:, 2:], False)
        sum_c = scatter(near_c, far_c, send_c, True)
        sum_d = [scatter(a[0], a[1], a[2], i == 0) for i, a in enumerate(
            [[v[:, cut] for v in (near_d, far_d, send_d)] for cut in (slice(0, 1), slice(1, 3))]
        )]
        sum_d = jnp.concatenate(sum_d)
        packed = lax.psum(packed, ("dp", "tensor"))
    else:
        got_a = swap(send_a, "dp", 1)
        back_part, near_c, far_c, send_c, packed = backward(False, packed, grad_resid, [])
        values = (got_a, back_part, near_c, far_c, send_c, packed, grad_resid, near_a, far_a)
        values, attn_piece = after((values, attn_piece))
        got_a, back_part, near_c, far_c, send_c, packed, grad_resid, near_a, far_a = values
        near_a = [add_low(near_a[:, s], got_a[:2, s]) for s in (slice(0, 2), slice(2, 4))]
        far_a = [add_low(far_a[:, s], got_a[2:, s]) for s in (slice(0, 2), slice(2, 4))]
        near_a, far_a, back_part, packed, attn_piece = after(
            (near_a, far_a, back_part, packed, attn_piece)
        )
        got_a = swap(far_a[0], "dp", 2)
        got_b = swap(far_a[1], "dp", 4)
        got_c = swap(send_c, "dp", 1)
        input_part, near_d, far_d, send_d, packed = backward(True, packed, grad_resid, [back_part])
        values = (got_a, got_b, got_c, near_a, near_c, far_c)
        values += (input_part, near_d, far_d, send_d, packed)
        values = after(values)
        got_a, got_b, got_c, near_a, near_c, far_c = values[:6]
        input_part, near_d, far_d, send_d, packed = values[6:]
        input_parts = [input_part] + [swap(input_part, "tensor", k) for k in TURNS[1:3]]
        got_d, got_p = swap(send_d, "dp", 1), swap(packed, "dp", 1)
        got_d, got_p, layer_out = after((got_d, got_p, layer_out))
        packed = packed + got_p
        first, others = slice(0, 1), slice(1, 3)
        flat2 = lambda a: a.reshape(-1, width)
        near_a, near_b = add_low(near_a[0], got_a), add_low(near_a[1], got_b)
        near_c = jnp.concatenate(
            [add_low(near_c, got_c[:2]), add_low(near_d[:, first], got_d[:2, first])], axis=1
        )
        far_c = [add_low(far_c, got_c[2:]), add_low(far_d[:, first], got_d[2:, first])]
        near_d = add_low(near_d[:, others], got_d[:2, others])
        far_d = add_low(far_d[:, others], got_d[2:, others])
        along_x = jnp.concatenate([flat2(near_b[1])] + [flat2(f) for f in far_c])
        along_y = with_packed(jnp.concatenate([flat2(near_a[1]), flat2(far_d)]), packed)
        along_x, along_y = swap(along_x, "dp", 2), swap(along_y, "dp", 4)
        along_x, along_y, near_a, near_b, near_c, near_d, packed = after(
            (along_x, along_y, near_a, near_b, near_c, near_d, packed)
        )
        size_b = near_b[1].size // width
        size_c = 2 * rows
        got_b = along_x[:size_b].reshape(near_b[1].shape)
        got_c = jnp.stack(
            [
                along_x[size_b : size_b + size_c].reshape(2, rows, width),
                along_x[size_b + size_c :].reshape(2, rows, width),
            ],
            axis=1,
        )
        got_a = along_y[:size_b].reshape(near_a[1].shape)
        got_d, packed = take_packed(along_y[size_b:], packed, near_d.shape)
        near_c, near_d = add_low(near_c, got_c), add_low(near_d, got_d)
        got_c, got_d = swap(near_c[1], "dp", 4), swap(with_packed(near_d[1], packed), "dp", 2)
        mlp_parts = [
            add_low(n[0, g], r[g])
            for n, r, g in ((near_a, got_a, 1), (near_b, got_b, 0), (near_b, got_b, 1))
        ]
        own_mlp = near_a[0, 0].astype(F32) + got_a[0].astype(F32)
        got_c, got_d, near_c, near_d, packed, own_mlp, mlp_parts, input_parts = after(
            (got_c, got_d, near_c, near_d, packed, own_mlp, mlp_parts, input_parts)
        )
        input_parts.append(swap(input_parts[2], "tensor", TURNS[1]))
        got_d, packed = take_packed(got_d, packed, near_d.shape[1:])
        own_attn = near_c[0, 0].astype(F32) + got_c[0].astype(F32)
        attn_parts = [
            add_low(n[0, g], r[g])
            for n, r, g in ((near_c, got_c, 1), (near_d, got_d, 0), (near_d, got_d, 1))
        ]
        parts = [
            swap(with_packed(jnp.concatenate([flat2(m), p]), packed), "tensor", k)
            for m, p, k in zip(mlp_parts, attn_parts, TURNS[1:])
        ]
        layer_out = move(after(layer_out, own_attn))
        input_grad = assemble(place, input_parts)
        parts, layer_out, input_grad = after((parts, layer_out, input_grad))
        done = finish(
            place,
            own_mlp,
            own_attn,
            packed,
            parts,
            heads,
            size,
            b_in.shape[0],
            n_dp,
        )
        small_vectors = [v.reshape(-1) for v in done[11:]]
        return (
            layer_out,
            input_grad,
            small_vectors[GAIN_ATTN],
            small_vectors[SHIFT_ATTN],
            done[2],
            done[6],
            done[3],
            done[4],
            done[7],
            done[8],
            done[9],
            done[5],
            small_vectors[B_ATTN],
            small_vectors[GAIN_MLP],
            small_vectors[SHIFT_MLP],
            done[0],
            done[10],
            done[1].T,
            small_vectors[B_OUT],
        )

    group = lambda mlp_sum, attn_sum: jnp.concatenate([mlp_sum, attn_sum[None]])
    sum_mlp = jnp.concatenate([sum_a, sum_b])
    sum_attn = jnp.concatenate([sum_c, sum_d])
    parts = [group(sum_mlp[g], sum_attn[g]) for g in range(n_tensor)]
    crossed = swap(jnp.stack([parts[1], parts[2]]).astype(BF16), "tensor", TURNS[1])
    total = parts[0] + crossed[0].astype(F32)
    given = (parts[3] + crossed[1].astype(F32)).astype(BF16)
    total = total + swap(given, "tensor", TURNS[3]).astype(F32)
    sum_mlp, sum_attn = total[:2], total[2]

    part = width // n_dp
    sums = lax.dynamic_slice_in_dim(packed[:GROUP_ROWS], dp_at * part, part, 1)
    mine = lax.dynamic_slice_in_dim(packed, GROUP_ROWS + 2 * page_at, 2, 0)

    def split_last(row, like):
        part = like.shape[-1] // n_dp
        return lax.dynamic_slice_in_dim(row.reshape(like.shape), dp_at * part, part, 1)

    at = 2 * inner + heads * BINS
    return (
        layer_out,
        input_grad,
        sums[GAIN_ATTN],
        sums[SHIFT_ATTN],
        sum_attn[:, :inner],
        split_last(mine[0, :inner], b_query),
        sum_attn[:, inner : 2 * inner],
        sum_attn[:, 2 * inner : 3 * inner],
        split_last(mine[0, inner : 2 * inner], b_value),
        split_last(mine[0, 2 * inner : at], table_x),
        split_last(mine[0, at:], table_y),
        sum_attn[:, 3 * inner :].T,
        sums[B_ATTN],
        sums[GAIN_MLP],
        sums[SHIFT_MLP],
        sum_mlp[0],
        split_last(mine[1], b_in),
        sum_mlp[1].T,
        sums[B_OUT],
    )


def solution(mesh):
    split = P("tensor", None)
    return jax.shard_map(
        local,
        mesh=mesh,
        in_specs=(
            P("dp", None),
            P("dp", None),
            P("dp", None),
            P("dp", None),
            P("dp", None),
            P("dp"),
            P(),
            P(),
            P(None, "tensor"),
            split,
            P(None, "tensor"),
            P(None, "tensor"),
            split,
            split,
            split,
            split,
            P(),
            P(),
            P(),
            P(None, "tensor"),
            split,
            split,
            P(),
        ),
        out_specs=(
            P("dp", None),
            P("dp", None),
            P("dp"),
            P("dp"),
            P("dp", "tensor"),
            P("tensor", "dp"),
            P("dp", "tensor"),
            P("dp", "tensor"),
            P("tensor", "dp"),
            P("tensor", "dp"),
            P("tensor", "dp"),
            P("tensor", "dp"),
            P("dp"),
            P("dp"),
            P("dp"),
            P("dp", "tensor"),
            P("tensor", "dp"),
            P("tensor", "dp"),
            P("dp"),
        ),
        check_vma=False,
    )
```

```python
import jax
import jax.numpy as jnp
from jax import lax
from jax.experimental import pallas as pl
from jax.experimental.pallas import tpu as pltpu
from jax.sharding import PartitionSpec as P

LEVELS = 128
BINS = 64
SEGS = 16
GROUP = 8
EPS = 1e-05
BARRED = -1e30
F32 = jnp.float32
BF16 = jnp.bfloat16
VMEM_BYTES = 56 * 1024 * 1024

NN = (((1,), (0,)), ((), ()))
NT = (((1,), (1,)), ((), ()))
TN = (((0,), (0,)), ((), ()))


def mm(left, right, dims=NN):
    return lax.dot_general(left, right, dims, preferred_element_type=F32)


def norm_stats(rows):
    mean = jnp.mean(rows, axis=-1, keepdims=True)
    centred = rows - mean
    inverse = lax.rsqrt(jnp.mean(centred * centred, axis=-1, keepdims=True) + EPS)
    return centred * inverse, inverse


def norm_back(grad_out, unit, inverse, gain):
    scaled = grad_out * gain
    return inverse * (
        scaled
        - jnp.mean(scaled, axis=-1, keepdims=True)
        - unit * jnp.mean(scaled * unit, axis=-1, keepdims=True)
    )


def page_columns(marks):
    return jnp.transpose(marks.astype(F32)).astype(jnp.int32)


def segment_terms(seg_col, length):
    count = seg_col.shape[0]
    lane = lax.broadcasted_iota(jnp.int32, (count, 64), 1)
    place = lax.broadcasted_iota(jnp.int32, (count, 64), 0)
    valid = place < length
    same = seg_col == lane
    query_side = jnp.where(valid, jnp.where(same, 1.0, 0.0), jnp.where(lane == SEGS, 1.0, 0.0))
    key_side = jnp.where(
        valid,
        jnp.where(same | (lane >= SEGS), 0.0, BARRED),
        jnp.where(lane <= SEGS, BARRED, 0.0),
    )
    return query_side.astype(BF16), key_side.astype(BF16)


def level_onehot(column):
    count = column.shape[0]
    lane = lax.broadcasted_iota(jnp.int32, (count, LEVELS), 1)
    return jnp.where(column == lane, 1.0, 0.0).astype(BF16)


def level_onehot_t(row):
    count = row.shape[1]
    level = lax.broadcasted_iota(jnp.int32, (LEVELS, count), 0)
    return jnp.where(row == level, 1.0, 0.0).astype(BF16)


def lookup_pair(table_row):
    lane = lax.broadcasted_iota(jnp.int32, (8, 2 * LEVELS), 1)
    first = LEVELS - BINS // 2
    wide = jnp.concatenate([table_row, jnp.zeros((1, 2 * LEVELS - BINS), F32)], axis=1)
    wide = pltpu.roll(jnp.broadcast_to(wide, (8, 2 * LEVELS)), first, 1)
    wide = jnp.where(lane < first, table_row[:, 0:1], wide)
    wide = jnp.where(lane >= first + BINS, table_row[:, BINS - 1 : BINS], wide)
    wide = jnp.broadcast_to(wide[0:1, :], (LEVELS, 2 * LEVELS))
    table = pltpu.roll(wide, 0, 1, stride=1, stride_axis=0)[:, LEVELS:]
    high = table.astype(BF16)
    rest = (table - high.astype(F32)).astype(BF16)
    return jnp.concatenate([high, rest], axis=1)


def fold_row(sums):
    lane = lax.broadcasted_iota(jnp.int32, (1, 2 * LEVELS), 1)
    start = LEVELS - 1 - BINS // 2
    low = jnp.sum(jnp.where(lane <= start, sums, 0.0), axis=1, keepdims=True)
    high = jnp.sum(jnp.where(lane >= start + BINS - 1, sums, 0.0), axis=1, keepdims=True)
    turned = pltpu.roll(jnp.broadcast_to(sums, (8, 2 * LEVELS)), 2 * LEVELS - start, 1)
    middle = turned[0:1, :BINS]
    lane = lane[:, :BINS]
    return jnp.where(lane == 0, low, jnp.where(lane == BINS - 1, high, middle))


def whole(array):
    return pl.BlockSpec(array.shape, lambda *at: (0,) * len(array.shape))


def cost(flops, arrays, exps=0):
    return pl.CostEstimate(
        flops=int(flops) // 16,
        bytes_accessed=int(sum(a.size * a.dtype.itemsize for a in arrays)) // 16,
        transcendentals=int(exps) // 16,
    )


def small_parts(heads, size, hidden):
    inner = heads * size
    b_q = slice(0, inner)
    b_v = slice(inner, 2 * inner)
    b_in = slice(2 * inner, 2 * inner + hidden)
    at = 2 * inner + hidden
    tables = [
        [slice(at + (axis * heads + h) * BINS, at + (axis * heads + h + 1) * BINS) for axis in (0, 1)]
        for h in range(heads)
    ]
    return b_q, b_v, b_in, tables


def attn_forward_kernel(
    pick, lengths, tokens, marks, vectors, w_query, w_key, w_value, small, context, *scratch
):
    looks, q_side, k_side = scratch
    step = pl.program_id(0)
    heads = looks.shape[0]
    inner = w_query.shape[0]
    size = inner // heads
    b_q, b_v, _, tables = small_parts(heads, size, small.shape[1] - 2 * inner - 2 * heads * BINS)

    @pl.when(step == 0)
    def _():
        for h in range(heads):
            for axis in range(2):
                looks[h, axis] = lookup_pair(small[0:1, tables[h][axis]])

    unit, _ = norm_stats(tokens[0].astype(F32))
    normed = (unit * vectors[0:1, :] + vectors[1:2, :]).astype(BF16)
    queries = (mm(normed, w_query[...], NT) + small[0:1, b_q]).astype(BF16)
    keys = mm(normed, w_key[...], NT).astype(BF16)
    values = (mm(normed, w_value[...], NT) + small[0:1, b_v]).astype(BF16)
    columns = page_columns(marks[0])
    seg_q, seg_k = segment_terms(columns[:, 0:1], lengths[pick[step]])
    hot_x = level_onehot(columns[:, 1:2])
    hot_y = level_onehot(columns[:, 2:3])
    k_side[:, 128:256] = hot_x
    k_side[:, 256:384] = hot_x
    k_side[:, 384:512] = hot_y
    k_side[:, 512:640] = hot_y
    factor = jnp.asarray(size ** (-0.5), BF16)
    ones = jnp.ones((queries.shape[0], size), BF16)
    results = []
    for h in range(heads):
        lanes = slice(h * size, (h + 1) * size)
        q_side[:, 0:128] = jnp.concatenate([queries[:, lanes] * factor, seg_q], axis=1)
        k_side[:, 0:128] = jnp.concatenate([keys[:, lanes], seg_k], axis=1)
        q_side[:, 128:384] = mm(hot_x, looks[h, 0]).astype(BF16)
        q_side[:, 384:640] = mm(hot_y, looks[h, 1]).astype(BF16)
        scores = mm(q_side[...], k_side[...], NT)
        peak = jnp.max(scores, axis=1, keepdims=True)
        raised = jnp.exp(scores - peak).astype(BF16)
        both = mm(raised, jnp.concatenate([values[:, lanes], ones], axis=1))
        results.append(both[:, :size] / both[:, size : size + 1])
    context[0] = jnp.concatenate(results, axis=1).astype(BF16)


def attn_forward(heads, pages, lengths, tokens, marks, vectors, weights, small):
    _, count, width = tokens.shape
    n_pages = pages.shape[0]
    inner = weights[0].shape[0]
    flops = n_pages * (2 * count * width * 3 * inner + heads * 2 * count * count * 1400)
    return pl.pallas_call(
        attn_forward_kernel,
        out_shape=jax.ShapeDtypeStruct((n_pages, count, inner), BF16),
        grid_spec=pltpu.PrefetchScalarGridSpec(
            num_scalar_prefetch=2,
            grid=(n_pages,),
            in_specs=[
                pl.BlockSpec((1, count, width), lambda i, p, n: (p[i], 0, 0)),
                pl.BlockSpec((1,) + marks.shape[1:], lambda i, p, n: (p[i], 0, 0)),
                whole(vectors),
            ]
            + [whole(w) for w in weights]
            + [whole(small)],
            out_specs=pl.BlockSpec((1, count, inner), lambda i, p, n: (i, 0, 0)),
            scratch_shapes=[
                pltpu.VMEM((heads, 2, LEVELS, 2 * LEVELS), BF16),
                pltpu.VMEM((count, 640), BF16),
                pltpu.VMEM((count, 640), BF16),
            ],
        ),
        compiler_params=pltpu.CompilerParams(vmem_limit_bytes=VMEM_BYTES),
        cost_estimate=cost(flops, [tokens], n_pages * heads * count * count),
        name="attn_forward",
    )(pages, lengths, tokens, marks, vectors, *weights, small)


EARLY = (0, 4, 2, 6)
LATE = (0, 2, 4, 6)
TURNS = (0, 1, 3, 2)
GAIN_ATTN, SHIFT_ATTN, GAIN_MLP, SHIFT_MLP, B_ATTN, B_OUT, GROUP_ROWS = range(7)


def slot_order(turned, ordered, place, orders):
    rows = turned.shape[0] // GROUP
    for v, order in enumerate(orders):
        for slot in range(4):
            spot = place[1] ^ order[slot]
            at = slot * rows
            ordered[v, at : at + rows, :] = turned[pl.ds(pl.multiple_of(spot * rows, rows), rows), :]
            other = spot ^ 1
            at = (4 + slot) * rows
            ordered[v, at : at + rows, :] = turned[pl.ds(pl.multiple_of(other * rows, rows), rows), :]


def hand_out(values, near, far, send):
    rows = values.shape[0] // GROUP
    low = values.astype(BF16)
    for slot in range(4):
        held = (near, far)[slot // 2][slot % 2]
        held[...] = low[slot * rows : (slot + 1) * rows, :]
        send[slot][...] = low[(4 + slot) * rows : (5 + slot) * rows, :]


def mlp_chunk(state, w_up, w_down, b_up, variant, near, far, send):
    low, low_t, cotangent, cot_t, out_sum, back_sum = state
    before = mm(low[...], w_up) + b_up
    half = 0.5 * (1.0 + lax.erf(before * (0.5**0.5)))
    active = (before * half).astype(BF16)
    slope = half + before * (jnp.exp(-0.5 * before * before) * 0.3989422804014327)
    out_sum[...] += mm(active, w_down)
    grad_before = (mm(cotangent, w_down, NT) * slope).astype(BF16)
    back_sum[...] += mm(grad_before, w_up, NT)
    for side, values in ((0, mm(low_t[variant], grad_before)), (1, mm(cot_t[variant], active))):
        hand_out(
            values,
            [near.at[s, side] for s in range(2)],
            [far.at[s, side] for s in range(2)],
            [send.at[s, side] for s in range(4)],
        )
    return jnp.sum(grad_before.astype(F32), axis=0, keepdims=True)


def mlp_kernel(place, tokens, cotangent, *rest):
    contexts = rest[:4]
    w_attn, w_in, w_out, vectors, small, panels, panels_all = rest[4:11]
    pieces = rest[11 : 11 + GROUP]
    near, far, send, packed, layer_out, grad_resid = rest[11 + GROUP : 17 + GROUP]
    resid, low, low_t, cot_t, out_sum, back_sum, turned, others, extra, sems, late_sems = rest[
        17 + GROUP :
    ]
    step = pl.program_id(0)
    width, hidden = w_in.shape
    inner = w_attn.shape[0]
    rows = width // GROUP
    share = 2 * inner // GROUP
    top = cotangent[0]
    state = (low, low_t, top, cot_t, out_sum, back_sum)

    def chunk(w_up, w_down, variant):
        row = mlp_chunk(
            state,
            w_up,
            w_down,
            small[0, 0:1, 2 * inner : 2 * inner + hidden],
            variant,
            near.at[:, 0],
            far.at[:, 0],
            send.at[:, 0],
        )
        turn = jnp.where(step < 2, step, 5 - step)
        packed[pl.ds(GROUP_ROWS + 1 + 2 * (place[0] ^ turn), 1), :] = row

    late_copies = []
    for j in range(GROUP):
        spot = (place[2] ^ j) * rows
        for side in range(2):
            target = pl.multiple_of(side * width + spot, rows)
            late_copies.append(
                pltpu.make_async_copy(
                    pieces[j].at[pl.ds(side * rows, rows), :],
                    extra.at[pl.ds(target, rows), :],
                    late_sems.at[len(late_copies)],
                )
            )

    @pl.when(step == 0)
    def _():
        copies = []
        for g in range(3):
            for j in range(0, GROUP, 2):
                source = panels_all.at[j, g] if g < 2 else pieces[j]
                spot = j // 2 if g < 2 else (place[2] ^ j) // 2
                target = pl.multiple_of(g * inner + spot * share, share)
                copies.append(
                    pltpu.make_async_copy(
                        source.at[pl.ds(2 * rows, share), :],
                        others.at[pl.ds(target, share), :],
                        sems.at[len(copies)],
                    )
                )
        for copy in copies + late_copies:
            copy.start()
        packed[...] = jnp.zeros_like(packed)
        turned[...] = jnp.transpose(top)
        slot_order(turned, cot_t, place, (EARLY, LATE))
        total = tokens[0].astype(F32) + vectors[2:3, :]
        total = total + mm(contexts[0][0], w_attn[...])
        for copy in copies:
            copy.wait()
        total = total + mm(jnp.concatenate([c[0] for c in contexts[1:]], axis=1), others[...])
        resid[...] = total
        unit, _ = norm_stats(total)
        normed = (unit * vectors[3:4, :] + vectors[4:5, :]).astype(BF16)
        low[...] = normed
        turned[...] = jnp.transpose(normed)
        slot_order(turned, low_t, place, (EARLY, LATE))
        out_sum[...] = jnp.zeros_like(out_sum)
        back_sum[...] = jnp.zeros_like(back_sum)
        chunk(w_in[...], w_out[...], 0)

    @pl.when((step == 1) | (step == 2))
    def _():
        late = step >= 2
        chunk(
            panels[:, 0, :rows, :].reshape(width, hidden),
            panels[:, 0, rows : 2 * rows, :].reshape(hidden, width),
            jnp.where(late, 1, 0),
        )

    @pl.when(step == 3)
    def _():
        for copy in late_copies:
            copy.wait()
        chunk(extra[:width, :], extra[width:, :], 1)

    @pl.when(step == pl.num_programs(0) - 1)
    def _():
        wide = top.astype(F32)
        layer_out[...] = (resid[...] + (out_sum[...] + vectors[5:6, :])).astype(BF16)
        unit, inverse = norm_stats(resid[...])
        back = back_sum[...]
        grad = wide + norm_back(back, unit, inverse, vectors[3:4, :])
        grad_resid[...] = grad
        column_sum = lambda v: jnp.sum(v, axis=0, keepdims=True)
        packed[GAIN_MLP : GAIN_MLP + 1, :] = column_sum(back * unit)
        packed[SHIFT_MLP : SHIFT_MLP + 1, :] = column_sum(back)
        packed[B_ATTN : B_ATTN + 1, :] = column_sum(grad.astype(BF16).astype(F32))
        packed[B_OUT : B_OUT + 1, :] = column_sum(wide)


def mlp(place, tokens, cotangent, contexts, w_attn, w_in, w_out, vectors, small, panels, pieces):
    _, count, width = tokens.shape
    hidden = w_in.shape[1]
    inner = w_attn.shape[0]
    groups = len(contexts)
    rows = width // GROUP
    page = pl.BlockSpec((1, count, width), lambda g, p: (p[0], 0, 0))
    outs = (
        jax.ShapeDtypeStruct((2, groups, 2, rows, hidden), BF16),
        jax.ShapeDtypeStruct((2, groups, 2, rows, hidden), BF16),
        jax.ShapeDtypeStruct((4, groups, 2, rows, hidden), BF16),
        jax.ShapeDtypeStruct((16, width), F32),
        jax.ShapeDtypeStruct((count, width), BF16),
        jax.ShapeDtypeStruct((count, width), F32),
    )
    held = lambda n: pl.BlockSpec((n, 1, 2, rows, hidden), lambda g, p: (0, g, 0, 0, 0))
    return pl.pallas_call(
        mlp_kernel,
        out_shape=outs,
        grid_spec=pltpu.PrefetchScalarGridSpec(
            num_scalar_prefetch=1,
            grid=(groups,),
            in_specs=[page, page]
            + [whole(c) for c in contexts]
            + [whole(w_attn), whole(w_in), whole(w_out), whole(vectors)]
            + [
                pl.BlockSpec((1,) + small.shape[1:], lambda g, p: (g, 0, 0)),
                pl.BlockSpec(
                    (GROUP, 1, 2 * rows, width),
                    lambda g, p: (0, jnp.minimum(jnp.maximum(g - 1, 0), 1), 0, 0),
                ),
                pl.BlockSpec(memory_space=pl.ANY),
            ]
            + [pl.BlockSpec(memory_space=pl.ANY)] * GROUP,
            out_specs=(held(2), held(2), held(4), whole(outs[3]), whole(outs[4]), whole(outs[5])),
            scratch_shapes=[
                pltpu.VMEM((count, width), F32),
                pltpu.VMEM((count, width), BF16),
                pltpu.VMEM((2, width, count), BF16),
                pltpu.VMEM((2, width, count), BF16),
                pltpu.VMEM((count, width), F32),
                pltpu.VMEM((count, width), F32),
                pltpu.VMEM((width, count), BF16),
                pltpu.VMEM((3 * inner, width), BF16),
                pltpu.VMEM((2 * width, hidden), BF16),
                pltpu.SemaphoreType.DMA((12,)),
                pltpu.SemaphoreType.DMA((2 * GROUP,)),
            ],
        ),
        compiler_params=pltpu.CompilerParams(vmem_limit_bytes=VMEM_BYTES),
        cost_estimate=cost(2 * count * width * (width + 24 * hidden), outs, 4 * count * hidden),
        name="mlp",
    )(
        place,
        tokens,
        cotangent,
        *contexts,
        w_attn,
        w_in,
        w_out,
        vectors,
        small,
        panels,
        panels,
        *pieces,
    )


def attn_backward_kernel(last, groups, place, lengths, tokens, grad_resid, *rest):
    context_refs = rest[:groups]
    marks, vectors, packed_start = rest[groups : groups + 3]
    at = groups + 3
    if last:
        back_start = rest[at]
        at += 1
    n_sources = GROUP if last else 4
    sources = rest[at : at + n_sources]
    at += n_sources
    small, result, near, far, send, packed = rest[at : at + 6]
    at += 6
    low, low_t, branch, branch_t, back_sum = rest[at : at + 5]
    hot, hot_t, q_side, k_side, both_weights, context, turned, sems = rest[at + 5 :]
    step = pl.program_id(0)
    count, width = low.shape
    inner = context.shape[1]
    heads = (small.shape[2] - width - 2 * inner) // (2 * BINS)
    size = inner // heads
    b_q, b_v, _, tables = small_parts(heads, size, width)
    rows = width // GROUP
    copies = [[] for _ in range(groups)]

    def fetch(slot, source, target, size):
        copies[slot].append(
            pltpu.make_async_copy(
                source, both_weights.at[slot, pl.ds(target, size), :], sems.at[slot, len(copies[slot])]
            )
        )

    if last:
        for j in range(GROUP):
            spot = pl.multiple_of((place[2] ^ j) * rows, rows)
            for slot in range(groups):
                fetch(slot, sources[j].at[pl.ds(slot * rows, rows), :], spot, rows)
    else:
        for i in range(4):
            fetch(0, sources[i], i * inner, inner)

    @pl.when(step == 0)
    def _():
        for slot in range(groups):
            for copy in copies[slot]:
                copy.start()
        packed[...] = packed_start[...]
        unit, _ = norm_stats(tokens[0].astype(F32))
        normed = (unit * vectors[0:1, :] + vectors[1:2, :]).astype(BF16)
        order = (EARLY, LATE) if last else (EARLY,)
        low[...] = normed
        turned[...] = jnp.transpose(normed)
        slot_order(turned, low_t, place, order)
        rounded = grad_resid[...].astype(BF16)
        branch[...] = rounded
        turned[...] = jnp.transpose(rounded)
        slot_order(turned, branch_t, place, order)
        back_sum[...] = back_start[...] if last else jnp.zeros_like(back_sum)
        columns = page_columns(marks[0])
        seg_q, seg_k = segment_terms(columns[:, 0:1], lengths[place[0]])
        hot_x = level_onehot(columns[:, 1:2])
        hot_y = level_onehot(columns[:, 2:3])
        hot[:, 0:128] = level_onehot(LEVELS - 1 - columns[:, 1:2])
        hot[:, 128:256] = level_onehot(LEVELS - 1 - columns[:, 2:3])
        hot_t[0:128, :] = level_onehot_t(marks[0, 1:2, :])
        hot_t[128:256, :] = level_onehot_t(marks[0, 2:3, :])
        q_side[:, 0:128] = jnp.concatenate([seg_q, seg_q], axis=1)
        k_side[:, 0:128] = jnp.concatenate([seg_k, seg_k], axis=1)
        k_side[:, 128:256] = hot_x
        k_side[:, 256:384] = hot_x
        k_side[:, 384:512] = hot_y
        k_side[:, 512:640] = hot_y

    for g in range(groups):

        @pl.when(step == g)
        def _(g=g):
            context[...] = context_refs[g][0]
            for copy in copies[g]:
                copy.wait()

    weights = both_weights.at[step]
    w_qkv = weights[: 3 * inner, :]
    qkv = mm(low[...], w_qkv, NT)
    queries = (qkv[:, :inner] + small[0, 0:1, b_q]).astype(BF16)
    keys = qkv[:, inner : 2 * inner].astype(BF16)
    values = (qkv[:, 2 * inner :] + small[0, 0:1, b_v]).astype(BF16)
    grad_ctx = mm(branch[...], weights[3 * inner :, :], NT).astype(BF16)
    factor = jnp.asarray(size ** (-0.5), BF16)
    grad_q, grad_k, grad_v = [], [], []
    tables_out = [[], []]
    for h in range(heads):
        lanes = slice(h * size, (h + 1) * size)
        query = queries[:, lanes] * factor
        key = keys[:, lanes]
        grad_here = grad_ctx[:, lanes]
        q_side[:, 0:size] = query
        k_side[:, 0:size] = key
        q_side[:, 128:384] = mm(
            k_side[:, 128:256], lookup_pair(small[0, 0:1, tables[h][0]])
        ).astype(BF16)
        q_side[:, 384:640] = mm(
            k_side[:, 384:512], lookup_pair(small[0, 0:1, tables[h][1]])
        ).astype(BF16)
        scores = mm(k_side[...], q_side[...], NT)
        raised = jnp.exp(scores - jnp.max(scores, axis=0, keepdims=True))
        probs = raised * (1.0 / jnp.sum(raised, axis=0, keepdims=True))
        grad_v.append(mm(probs.astype(BF16), grad_here))
        weighted = probs * mm(values[:, lanes], grad_here, NT)
        grad_scores = weighted - probs * jnp.sum(weighted, axis=0, keepdims=True)
        low_scores = grad_scores.astype(BF16)
        grad_k.append(mm(low_scores, query))
        grad_q.append(jnp.transpose(mm(key, low_scores, TN)) * (size ** (-0.5)))
        spread = mm(low_scores, hot[...]).astype(BF16)
        for axis in range(2):
            cut = slice(axis * LEVELS, (axis + 1) * LEVELS)
            square = mm(hot_t[cut, :], spread[:, cut])
            wide = jnp.concatenate([square, jnp.zeros_like(square)], axis=1)
            turned = pltpu.roll(wide, 0, 1, stride=1, stride_axis=0)
            tables_out[axis].append(fold_row(jnp.sum(turned, axis=0, keepdims=True)))
    grad_q = jnp.concatenate(grad_q, axis=1).astype(BF16)
    grad_k = jnp.concatenate(grad_k, axis=1).astype(BF16)
    grad_v = jnp.concatenate(grad_v, axis=1).astype(BF16)
    group = step + 1 if last else step
    turn = jnp.where(group < 2, group, 5 - group)
    packed[pl.ds(GROUP_ROWS + 2 * (place[0] ^ turn), 1), :] = jnp.concatenate(
        [
            jnp.sum(grad_q.astype(F32), axis=0, keepdims=True),
            jnp.sum(grad_v.astype(F32), axis=0, keepdims=True),
        ]
        + tables_out[0]
        + tables_out[1],
        axis=1,
    )
    grad_qkv = jnp.concatenate([grad_q, grad_k, grad_v], axis=1)
    back_sum[...] += mm(grad_qkv, w_qkv)
    variant = jnp.where(step > 0, 1, 0) if last else 0
    hand_out(
        jnp.concatenate([mm(low_t[variant], grad_qkv), mm(branch_t[variant], context[...])], axis=1),
        [near.at[s, 0] for s in range(2)],
        [far.at[s, 0] for s in range(2)],
        [send.at[s, 0] for s in range(4)],
    )

    @pl.when(step == groups - 1)
    def _():
        back = back_sum[...]
        if last:
            unit, inverse = norm_stats(tokens[0].astype(F32))
            result[...] = (
                grad_resid[...] + norm_back(back, unit, inverse, vectors[0:1, :])
            ).astype(BF16)
            packed[GAIN_ATTN : GAIN_ATTN + 1, :] = jnp.sum(back * unit, axis=0, keepdims=True)
            packed[SHIFT_ATTN : SHIFT_ATTN + 1, :] = jnp.sum(back, axis=0, keepdims=True)
        else:
            result[...] = back


def attn_backward(
    last,
    heads,
    place,
    lengths,
    tokens,
    grad_resid,
    contexts,
    marks,
    vectors,
    packed,
    extra,
    sources,
    small,
):
    _, count, width = tokens.shape
    groups = len(contexts)
    inner = contexts[0].shape[2]
    rows = width // GROUP
    first = 1 if last else 0
    outs = (
        jax.ShapeDtypeStruct((count, width), BF16 if last else F32),
        jax.ShapeDtypeStruct((2, groups, rows, 4 * inner), BF16),
        jax.ShapeDtypeStruct((2, groups, rows, 4 * inner), BF16),
        jax.ShapeDtypeStruct((4, groups, rows, 4 * inner), BF16),
        jax.ShapeDtypeStruct(packed.shape, F32),
    )
    held = lambda n: pl.BlockSpec((n, 1, rows, 4 * inner), lambda g, p, q: (0, g, 0, 0))
    flops = groups * (6 * count * width * 4 * inner + heads * 2 * count * count * 2900)
    body = lambda *refs: attn_backward_kernel(last, groups, *refs)
    return pl.pallas_call(
        body,
        out_shape=outs,
        grid_spec=pltpu.PrefetchScalarGridSpec(
            num_scalar_prefetch=2,
            grid=(groups,),
            in_specs=[
                pl.BlockSpec((1, count, width), lambda g, p, n: (p[0], 0, 0)),
                whole(grad_resid),
            ]
            + [whole(c) for c in contexts]
            + [
                pl.BlockSpec((1,) + marks.shape[1:], lambda g, p, n: (p[0], 0, 0)),
                whole(vectors),
                whole(packed),
            ]
            + [whole(e) for e in extra]
            + [pl.BlockSpec(memory_space=pl.ANY)] * len(sources)
            + [pl.BlockSpec((1,) + small.shape[1:], lambda g, p, n: (g + first, 0, 0))],
            out_specs=(whole(outs[0]), held(2), held(2), held(4), whole(outs[4])),
            scratch_shapes=[
                pltpu.VMEM((count, width), BF16),
                pltpu.VMEM((2 if last else 1, width, count), BF16),
                pltpu.VMEM((count, width), BF16),
                pltpu.VMEM((2 if last else 1, width, count), BF16),
                pltpu.VMEM((count, width), F32),
                pltpu.VMEM((count, 256), BF16),
                pltpu.VMEM((256, count), BF16),
                pltpu.VMEM((count, 640), BF16),
                pltpu.VMEM((count, 640), BF16),
                pltpu.VMEM((groups, 4 * inner, width), BF16),
                pltpu.VMEM((count, inner), BF16),
                pltpu.VMEM((width, count), BF16),
                pltpu.SemaphoreType.DMA((groups, GROUP)),
            ],
        ),
        compiler_params=pltpu.CompilerParams(vmem_limit_bytes=VMEM_BYTES),
        cost_estimate=cost(flops, outs, groups * heads * count * count),
        name="attn_backward",
    )(
        place,
        lengths,
        tokens,
        grad_resid,
        *contexts,
        marks,
        vectors,
        packed,
        *extra,
        *sources,
        small,
    )


def move_kernel(source, target):
    target[...] = source[...]


def move(array):
    rows, width = array.shape
    spec = pl.BlockSpec((rows // 4, width), lambda i: (i, 0))
    return pl.pallas_call(
        move_kernel,
        out_shape=jax.ShapeDtypeStruct(array.shape, array.dtype),
        grid=(4,),
        in_specs=[spec],
        out_specs=spec,
        cost_estimate=cost(0, [array, array]),
        name="move",
    )(array)


def finish_kernel(place, own_mlp, own_attn, own_packed, *rest):
    parts, grad_in, grad_out = rest[:3], rest[3], rest[4]
    grad_qkv, grad_attn_out = rest[5:8], rest[8]
    small_heads, small_hidden, vectors = rest[9:13], rest[13], rest[14:20]
    summed = rest[20]
    rows = own_attn.shape[0]
    inner = grad_qkv[0].shape[1]
    for side, target in ((0, grad_in), (1, grad_out)):
        total = own_mlp[side]
        for part in parts:
            total = total + part[side * rows : (side + 1) * rows, :].astype(F32)
        target[...] = total
    total = own_attn[...]
    packed = own_packed[...]
    for part in parts:
        total = total + part[2 * rows : 3 * rows, :].astype(F32)
        for i in range(3):
            start = 3 * rows + 16 * i
            packed = packed + part[start : start + 16, :].astype(F32)
    for i in range(3):
        grad_qkv[i][...] = total[:, i * inner : (i + 1) * inner]
    grad_attn_out[...] = jnp.transpose(total[:, 3 * inner :])
    summed[...] = packed
    width = packed.shape[1]

    def lanes(row, start, size):
        wide = jnp.broadcast_to(row, (8, width))
        return pltpu.roll(wide, width - start, 1)[0:1, :size]

    share = vectors[0].shape[1]
    for i, target in enumerate(vectors):
        target[...] = lanes(packed[i : i + 1, :], place[1] * share, share)
    heads, part = small_heads[0].shape
    head_size = part * (width // share)
    mine = summed[pl.ds(GROUP_ROWS + 2 * place[0], 1), :]
    for i, target in enumerate(small_heads):
        for h in range(heads):
            start = (i * heads + h) * head_size + place[1] * part
            target[h : h + 1, :] = lanes(mine, start, part)
    mine = summed[pl.ds(GROUP_ROWS + 1 + 2 * place[0], 1), :]
    lines, part = small_hidden.shape
    for r in range(lines):
        start = r * (width // lines) + place[1] * part
        small_hidden[r : r + 1, :] = lanes(mine, start, part)


def finish(place, own_mlp, own_attn, own_packed, parts, heads, size, lines, n_dp):
    rows, width = own_attn.shape
    inner = heads * size
    hidden = own_mlp.shape[2]
    shapes = [(rows, hidden)] * 2 + [(rows, inner)] * 3 + [(inner, rows)]
    shapes += [(heads, size // n_dp)] * 4 + [(lines, hidden // lines // n_dp)]
    shapes += [(1, width // n_dp)] * 6
    outs = tuple(jax.ShapeDtypeStruct(s, F32) for s in shapes)
    inputs = [own_mlp, own_attn, own_packed, *parts]
    return pl.pallas_call(
        finish_kernel,
        out_shape=outs,
        grid_spec=pltpu.PrefetchScalarGridSpec(
            num_scalar_prefetch=1,
            grid=(1,),
            in_specs=[whole(a) for a in inputs],
            out_specs=tuple(whole(o) for o in outs),
            scratch_shapes=[pltpu.VMEM(own_packed.shape, F32)],
        ),
        cost_estimate=cost(0, inputs),
        name="finish",
    )(place, *inputs)


def prepare_kernel(b_query, b_value, b_in, table_x, table_y, segment, box_x, box_y, *rest):
    rows, (marks, vectors, flat, row) = rest[:6], rest[6:]
    line = lambda ref: jnp.concatenate([ref[i : i + 1, :] for i in range(ref.shape[0])], axis=1)
    small = jnp.concatenate([line(v) for v in (b_query, b_value, b_in, table_x, table_y)], axis=1)
    row[...] = small
    width = flat.shape[1]
    for i in range(flat.shape[0]):
        flat[i : i + 1, :] = small[:, i * width : (i + 1) * width]
    marks[...] = jnp.zeros_like(marks)
    for p in range(marks.shape[0]):
        for i, source in enumerate((segment, box_x, box_y)):
            marks[p, i : i + 1, :] = source[p : p + 1, :]
    vectors[...] = jnp.zeros_like(vectors)
    for i, source in enumerate(rows):
        vectors[i : i + 1, :] = source[...].reshape(1, width)


def prepare(smalls, pages, rows):
    width = rows[0].shape[0]
    total = sum(v.size for v in smalls)
    outs = (
        jax.ShapeDtypeStruct((pages[0].shape[0], 8, pages[0].shape[1]), jnp.int32),
        jax.ShapeDtypeStruct((8, width), F32),
        jax.ShapeDtypeStruct((total // width, width), F32),
        jax.ShapeDtypeStruct((1, total), F32),
    )
    inputs = [*smalls, *pages, *rows]
    return pl.pallas_call(
        prepare_kernel,
        out_shape=outs,
        grid=(1,),
        in_specs=[whole(a) for a in inputs],
        out_specs=tuple(whole(o) for o in outs),
        cost_estimate=cost(0, inputs),
        name="prepare",
    )(*inputs)


def assemble_kernel(place, *refs):
    step = pl.program_id(0)
    for g in range(4):

        @pl.when(step == g)
        def _(g=g):
            refs[4][...] = refs[g][...]


def assemble(place, parts):
    rows, width = parts[0].shape
    turn = lambda g, p: (p[0] ^ jnp.where(g < 2, g, 5 - g), 0)
    return pl.pallas_call(
        assemble_kernel,
        out_shape=jax.ShapeDtypeStruct((4 * rows, width), parts[0].dtype),
        grid_spec=pltpu.PrefetchScalarGridSpec(
            num_scalar_prefetch=1,
            grid=(4,),
            in_specs=[whole(a) for a in parts],
            out_specs=pl.BlockSpec((rows, width), turn),
        ),
        cost_estimate=cost(0, parts),
        name="assemble",
    )(place, *parts)


def swap(array, axis, offset):
    size = lax.axis_size(axis)
    return lax.ppermute(array, axis, [(i, i ^ offset) for i in range(size)])


def add_low(left, right):
    return (left.astype(F32) + right.astype(F32)).astype(BF16)


def after(values, *first):
    flat, tree = jax.tree.flatten(values, is_leaf=lambda v: v is None)
    held = [i for i, v in enumerate(flat) if v is not None]
    tied = lax.optimization_barrier(tuple(flat[i] for i in held) + first)
    for i, v in zip(held, tied):
        flat[i] = v
    return jax.tree.unflatten(tree, flat)


def three_terms(array):
    terms, rest = [], array
    for _ in range(3):
        term = lax.reduce_precision(rest, 8, 7)
        terms.append(term.astype(BF16))
        rest = rest - term
    return terms


def with_packed(array, packed):
    return jnp.concatenate([array.reshape(-1, array.shape[-1])] + three_terms(packed), axis=0)


def take_packed(array, packed, shape):
    rows = packed.shape[0]
    for i in range(3):
        start = array.shape[0] - (3 - i) * rows
        packed = packed + array[start : start + rows].astype(F32)
    return array[: -3 * rows].reshape(shape), packed


def start_slices(own, turn):
    piece = [None] * GROUP
    piece[0] = own
    for step in turn:
        piece[step] = swap(own, "dp", step)
    return piece


def local(
    tokens,
    cotangent,
    segment,
    box_x,
    box_y,
    page_tokens,
    gain_attn,
    shift_attn,
    w_query,
    b_query,
    w_key,
    w_value,
    b_value,
    table_x,
    table_y,
    w_attn_out,
    b_attn_out,
    gain_mlp,
    shift_mlp,
    w_in,
    b_in,
    w_out,
    b_out,
):
    pages, count = segment.shape
    width = tokens.shape[1]
    heads, size = b_query.shape
    inner = heads * size
    hidden = w_in.shape[1]
    n_dp = lax.axis_size("dp")
    n_tensor = lax.axis_size("tensor")
    dp_at = lax.axis_index("dp")
    page_at = lax.axis_index("tensor")
    slice_at = dp_at % GROUP
    rows = width // GROUP
    natural = n_dp != GROUP
    place_out = 0 * slice_at if natural else slice_at
    place = jnp.stack([page_at, place_out, slice_at]).astype(jnp.int32)

    tokens3 = tokens.reshape(pages, count, width)
    cotangent3 = cotangent.reshape(pages, count, width)
    cut = lambda w, at, size: lax.dynamic_slice_in_dim(w, at * size, size, 0)
    share = 2 * inner // GROUP
    slice_mlp = [cut(w_in, slice_at, rows), cut(w_out, slice_at, rows)]
    slice_out = cut(w_attn_out, slice_at // 2, share)
    own = [w_query.T, w_key.T, w_value.T, w_attn_out]
    slice_mlp = jnp.concatenate(slice_mlp + [slice_out], axis=0)
    got = [swap(slice_mlp, "tensor", k) for k in TURNS[1:3]]

    marks, vectors, flat, small = prepare(
        (b_query, b_value, b_in, table_x, table_y),
        (segment, box_x, box_y),
        (gain_attn, shift_attn, b_attn_out, gain_mlp, shift_mlp, b_out),
    )
    order = jnp.stack([page_at ^ k for k in (1, 3, 2, 0)]).astype(jnp.int32)
    forward = lambda which: attn_forward(
        heads, which, page_tokens, tokens3, marks, vectors, own[:3], small
    )
    sent = forward(order[:2])
    slice_attn = lax.select_n(slice_at // 2, *[cut(w, slice_at % 2, inner // 2) for w in own])
    sent, turn, got, slice_attn, slice_mlp, flat = after(
        (sent, order[2:], got, slice_attn, slice_mlp, flat)
    )
    blocks = [list(range(b, b + GROUP)) for b in range(0, n_dp, GROUP)]
    groups = None if n_dp == GROUP else blocks
    panels = lax.all_gather(jnp.stack(got), "dp", axis=0, axis_index_groups=groups)
    got_last = swap(got[1], "tensor", TURNS[1])
    contexts = [swap(sent[g : g + 1], "tensor", TURNS[g + 1]) for g in (0, 1)]
    kept = forward(turn)
    kept, got_last = after((kept, got_last))
    piece = start_slices(got_last, (4, 2))
    contexts, kept, slice_attn, flat = after((contexts, kept, slice_attn, flat))

    contexts = [kept[1:2]] + contexts + [swap(kept[0:1], "tensor", TURNS[3])]
    got = [swap(slice_attn, "tensor", k) for k in TURNS[1:3]]
    contexts, piece, got, flat, place = after((contexts, piece, got, flat, place))
    piece[6] = swap(piece[4], "dp", 2)
    smalls = [flat] + [swap(flat, "tensor", k) for k in TURNS[1:]]
    got.append(swap(got[1], "tensor", TURNS[1]))
    piece, got, smalls = after((piece, got, smalls))
    for j in (0, 4, 2, 6):
        piece[j + 1] = swap(piece[j], "dp", 1)
    attn_piece = start_slices(jnp.stack(got).reshape(-1, width), (2, 4, 6))
    smalls = jnp.stack(smalls).reshape(n_tensor, 1, -1)
    contexts, piece, smalls, panels = after((contexts, piece, smalls, panels))

    near_a, far_a, send_a, packed, layer_part, grad_resid = mlp(
        place, tokens3, cotangent3, contexts, w_attn_out, w_in, w_out, vectors, smalls, panels, piece
    )
    near_a, far_a, send_a, packed, layer_part, grad_resid, attn_piece = after(
        (near_a, far_a, send_a, packed, layer_part, grad_resid, attn_piece)
    )
    for j in (0, 4, 2, 6):
        attn_piece[j + 1] = swap(attn_piece[j], "dp", 1)
    layer_out = lax.all_gather(layer_part, "tensor", axis=0, tiled=True)

    def backward(last, packed_in, grad_in, extra):
        side = slice(1, 4) if last else slice(0, 1)
        return attn_backward(
            last,
            heads,
            place,
            page_tokens,
            tokens3,
            grad_in,
            contexts[side],
            marks,
            vectors,
            packed_in,
            extra,
            attn_piece if last else own,
            smalls,
        )

    if natural:
        back_part, near_c, far_c, send_c, packed = backward(False, packed, grad_resid, [])
        input_part, near_d, far_d, send_d, packed = backward(True, packed, grad_resid, [back_part])
        input_grad = lax.all_gather(input_part, "tensor", axis=0, tiled=True)
        more = n_dp // GROUP

        def scatter(near, far, given, early):
            both = jnp.stack([jnp.concatenate([near, far]), given], axis=1)
            both = both.reshape((2, 2) + both.shape[1:])
            if early:
                both = jnp.swapaxes(both, 0, 1)
            inside = both.shape[3:-2]
            both = both.reshape((GROUP,) + inside + (more, -1, both.shape[-1]))
            both = jnp.moveaxis(both, -3, 1).reshape((n_dp,) + inside + (-1, both.shape[-1]))
            total = lax.psum_scatter(both, "dp", scatter_dimension=0, tiled=False)
            return total.astype(F32)

        sum_a = scatter(near_a[:, :2], far_a[:, :2], send_a[:, :2], True)
        sum_b = scatter(near_a[:, 2:], far_a[:, 2:], send_a[:, 2:], False)
        sum_c = scatter(near_c, far_c, send_c, True)
        sum_d = [scatter(a[0], a[1], a[2], i == 0) for i, a in enumerate(
            [[v[:, cut] for v in (near_d, far_d, send_d)] for cut in (slice(0, 1), slice(1, 3))]
        )]
        sum_d = jnp.concatenate(sum_d)
        packed = lax.psum(packed, ("dp", "tensor"))
    else:
        got_a = swap(send_a, "dp", 1)
        back_part, near_c, far_c, send_c, packed = backward(False, packed, grad_resid, [])
        values = (got_a, back_part, near_c, far_c, send_c, packed, grad_resid, near_a, far_a)
        values, attn_piece = after((values, attn_piece))
        got_a, back_part, near_c, far_c, send_c, packed, grad_resid, near_a, far_a = values
        near_a = [add_low(near_a[:, s], got_a[:2, s]) for s in (slice(0, 2), slice(2, 4))]
        far_a = [add_low(far_a[:, s], got_a[2:, s]) for s in (slice(0, 2), slice(2, 4))]
        near_a, far_a, back_part, packed, attn_piece = after(
            (near_a, far_a, back_part, packed, attn_piece)
        )
        got_a = swap(far_a[0], "dp", 2)
        got_b = swap(far_a[1], "dp", 4)
        got_c = swap(send_c, "dp", 1)
        input_part, near_d, far_d, send_d, packed = backward(True, packed, grad_resid, [back_part])
        values = (got_a, got_b, got_c, near_a, near_c, far_c)
        values += (input_part, near_d, far_d, send_d, packed)
        values = after(values)
        got_a, got_b, got_c, near_a, near_c, far_c = values[:6]
        input_part, near_d, far_d, send_d, packed = values[6:]
        input_parts = [input_part] + [swap(input_part, "tensor", k) for k in TURNS[1:3]]
        got_d, got_p = swap(send_d, "dp", 1), swap(packed, "dp", 1)
        got_d, got_p, layer_out = after((got_d, got_p, layer_out))
        packed = packed + got_p
        first, others = slice(0, 1), slice(1, 3)
        flat2 = lambda a: a.reshape(-1, width)
        near_a, near_b = add_low(near_a[0], got_a), add_low(near_a[1], got_b)
        near_c = jnp.concatenate(
            [add_low(near_c, got_c[:2]), add_low(near_d[:, first], got_d[:2, first])], axis=1
        )
        far_c = [add_low(far_c, got_c[2:]), add_low(far_d[:, first], got_d[2:, first])]
        near_d = add_low(near_d[:, others], got_d[:2, others])
        far_d = add_low(far_d[:, others], got_d[2:, others])
        along_x = jnp.concatenate([flat2(near_b[1])] + [flat2(f) for f in far_c])
        along_y = with_packed(jnp.concatenate([flat2(near_a[1]), flat2(far_d)]), packed)
        along_x, along_y = swap(along_x, "dp", 2), swap(along_y, "dp", 4)
        along_x, along_y, near_a, near_b, near_c, near_d, packed = after(
            (along_x, along_y, near_a, near_b, near_c, near_d, packed)
        )
        size_b = near_b[1].size // width
        size_c = 2 * rows
        got_b = along_x[:size_b].reshape(near_b[1].shape)
        got_c = jnp.stack(
            [
                along_x[size_b : size_b + size_c].reshape(2, rows, width),
                along_x[size_b + size_c :].reshape(2, rows, width),
            ],
            axis=1,
        )
        got_a = along_y[:size_b].reshape(near_a[1].shape)
        got_d, packed = take_packed(along_y[size_b:], packed, near_d.shape)
        near_c, near_d = add_low(near_c, got_c), add_low(near_d, got_d)
        got_c, got_d = swap(near_c[1], "dp", 4), swap(with_packed(near_d[1], packed), "dp", 2)
        mlp_parts = [
            add_low(n[0, g], r[g])
            for n, r, g in ((near_a, got_a, 1), (near_b, got_b, 0), (near_b, got_b, 1))
        ]
        own_mlp = near_a[0, 0].astype(F32) + got_a[0].astype(F32)
        got_c, got_d, near_c, near_d, packed, own_mlp, mlp_parts, input_parts = after(
            (got_c, got_d, near_c, near_d, packed, own_mlp, mlp_parts, input_parts)
        )
        input_parts.append(swap(input_parts[2], "tensor", TURNS[1]))
        got_d, packed = take_packed(got_d, packed, near_d.shape[1:])
        own_attn = near_c[0, 0].astype(F32) + got_c[0].astype(F32)
        attn_parts = [
            add_low(n[0, g], r[g])
            for n, r, g in ((near_c, got_c, 1), (near_d, got_d, 0), (near_d, got_d, 1))
        ]
        parts = [
            swap(with_packed(jnp.concatenate([flat2(m), p]), packed), "tensor", k)
            for m, p, k in zip(mlp_parts, attn_parts, TURNS[1:])
        ]
        layer_out = move(after(layer_out, own_attn))
        input_grad = assemble(place, input_parts)
        parts, layer_out, input_grad = after((parts, layer_out, input_grad))
        done = finish(
            place,
            own_mlp,
            own_attn,
            packed,
            parts,
            heads,
            size,
            b_in.shape[0],
            n_dp,
        )
        small_vectors = [v.reshape(-1) for v in done[11:]]
        return (
            layer_out,
            input_grad,
            small_vectors[GAIN_ATTN],
            small_vectors[SHIFT_ATTN],
            done[2],
            done[6],
            done[3],
            done[4],
            done[7],
            done[8],
            done[9],
            done[5],
            small_vectors[B_ATTN],
            small_vectors[GAIN_MLP],
            small_vectors[SHIFT_MLP],
            done[0],
            done[10],
            done[1].T,
            small_vectors[B_OUT],
        )

    group = lambda mlp_sum, attn_sum: jnp.concatenate([mlp_sum, attn_sum[None]])
    sum_mlp = jnp.concatenate([sum_a, sum_b])
    sum_attn = jnp.concatenate([sum_c, sum_d])
    parts = [group(sum_mlp[g], sum_attn[g]) for g in range(n_tensor)]
    crossed = swap(jnp.stack([parts[1], parts[2]]).astype(BF16), "tensor", TURNS[1])
    total = parts[0] + crossed[0].astype(F32)
    given = (parts[3] + crossed[1].astype(F32)).astype(BF16)
    total = total + swap(given, "tensor", TURNS[3]).astype(F32)
    sum_mlp, sum_attn = total[:2], total[2]

    part = width // n_dp
    sums = lax.dynamic_slice_in_dim(packed[:GROUP_ROWS], dp_at * part, part, 1)
    mine = lax.dynamic_slice_in_dim(packed, GROUP_ROWS + 2 * page_at, 2, 0)

    def split_last(row, like):
        part = like.shape[-1] // n_dp
        return lax.dynamic_slice_in_dim(row.reshape(like.shape), dp_at * part, part, 1)

    at = 2 * inner + heads * BINS
    return (
        layer_out,
        input_grad,
        sums[GAIN_ATTN],
        sums[SHIFT_ATTN],
        sum_attn[:, :inner],
        split_last(mine[0, :inner], b_query),
        sum_attn[:, inner : 2 * inner],
        sum_attn[:, 2 * inner : 3 * inner],
        split_last(mine[0, inner : 2 * inner], b_value),
        split_last(mine[0, 2 * inner : at], table_x),
        split_last(mine[0, at:], table_y),
        sum_attn[:, 3 * inner :].T,
        sums[B_ATTN],
        sums[GAIN_MLP],
        sums[SHIFT_MLP],
        sum_mlp[0],
        split_last(mine[1], b_in),
        sum_mlp[1].T,
        sums[B_OUT],
    )


def solution(mesh):
    split = P("tensor", None)
    return jax.shard_map(
        local,
        mesh=mesh,
        in_specs=(
            P("dp", None),
            P("dp", None),
            P("dp", None),
            P("dp", None),
            P("dp", None),
            P("dp"),
            P(),
            P(),
            P(None, "tensor"),
            split,
            P(None, "tensor"),
            P(None, "tensor"),
            split,
            split,
            split,
            split,
            P(),
            P(),
            P(),
            P(None, "tensor"),
            split,
            split,
            P(),
        ),
        out_specs=(
            P("dp", None),
            P("dp", None),
            P("dp"),
            P("dp"),
            P("dp", "tensor"),
            P("tensor", "dp"),
            P("dp", "tensor"),
            P("dp", "tensor"),
            P("tensor", "dp"),
            P("tensor", "dp"),
            P("tensor", "dp"),
            P("tensor", "dp"),
            P("dp"),
            P("dp"),
            P("dp"),
            P("dp", "tensor"),
            P("tensor", "dp"),
            P("tensor", "dp"),
            P("dp"),
        ),
        check_vma=False,
    )
```
